1024 devices in a mesh: dom: 256 (over z, x, core), sub: 4 (over y).
Axes of the slice: x: 4, y: 4, z: 32, core: 2. Of those that a mesh axis runs over, the one named last changes fastest.
Arguments:
- rhs_local: float32 [2048, 128, 128], P('dom', 'sub'), may hold values from -8 to 8
- coefficient: float32 [2048, 128, 128], P('dom', 'sub'), may hold values from 0.3 to 3
Outputs:
- preconditioned: float32 [2048, 128, 128], P('dom', 'sub')
- coarse_solution: float32 [512, 32, 32], P('dom', 'sub')
The draws below stay inside these ranges and needn't reach their ends.
All inputs are finite; a program needn't handle non-finite values.
Results may differ from the reference program's by a relative error of at most 0.0003.
Values sent between devices are 32-bit elements; how exact they have to be, the bound alone decides.
A program may use at most 64 MiB of HBM per device.

```python
import math
import jax
import jax.numpy as jnp
import numpy as np
from jax import lax

EZ = 16
NX = 2048
NY = 128
NZ = 128
MX = 512
MY = 32
MZ = 32
N_DOM = 256


def shard_levels(key, dims, shards, least, largest):
    loudness = 1.0
    for dim, blocks in shards:
        heights = jax.random.uniform(jax.random.fold_in(jax.random.fold_in(key, 6), dim), (blocks,), jnp.float32, least / len(shards), largest / len(shards))
        loudness = loudness * jnp.repeat(jnp.exp(heights), dims[dim] // blocks).reshape((-1,) + (1,) * (len(dims) - 1 - dim))
    return loudness


def gaussian(rng, shape, spread, reach, shards=(), kind=jnp.bfloat16):
    entries = jax.random.normal(rng, shape, jnp.float32) * spread
    if len(shards) > 0:
        entries = shard_levels(rng, shape, shards, -0.22, 0.18) * entries
    return jnp.clip(entries, min=-reach, max=reach).astype(kind)


def setup_inputs(seed: int = 0) -> dict:
    splits = jax.random.split(jax.random.key(seed), 3)
    rhs_local = gaussian(splits[0], (NX, NY, NZ), 1.0, 8.0, ((0, 256), (1, 4)), jnp.float32)
    coefficient = jnp.clip(jnp.exp(math.log(3.0) - 2.3025851 * jax.random.uniform(splits[1], (NX, NY, NZ), jnp.float32) ** shard_levels(splits[1], (NX, NY, NZ), ((0, 256), (1, 4)), -0.2, 0.2)), 0.3, 3.0)
    return dict(rhs_local=rhs_local, coefficient=coefficient)


def legendre_value(points, degree):
    previous = np.ones(points.shape)
    current = points.copy()
    for level in range(1, degree):
        following = ((2 * level + 1) * points * current - level * previous) / (level + 1)
        previous = current
        current = following
    return current


def tables():
    degree = 7
    points = np.array([-1.0, -0.8717401485096066, -0.5917001814331423, -0.2092992179024789,
                       0.2092992179024789, 0.5917001814331423, 0.8717401485096066, 1.0])
    values = legendre_value(points, degree)
    weights = 2.0 / (degree * (degree + 1) * values ** 2)
    derivative = np.zeros((8, 8))
    for row_at in range(8):
        for col_at in range(8):
            if row_at != col_at:
                derivative[row_at, col_at] = values[row_at] / (values[col_at] * (points[row_at] - points[col_at]))
    derivative[0, 0] = -degree * (degree + 1) / 4.0
    derivative[7, 7] = degree * (degree + 1) / 4.0
    interp = np.stack([(1.0 - points) / 2.0, (1.0 + points) / 2.0], axis=1)
    slopes = np.array([-0.5, 0.5])
    return derivative, weights, interp, slopes


def fold_local(field, axis_at, per_elem):
    dims_of = field.shape
    elements = dims_of[axis_at] // per_elem
    split = field.reshape(dims_of[:axis_at] + (elements, per_elem) + dims_of[axis_at + 1:])
    first_face = lax.index_in_dim(split, 0, axis_at + 1, keepdims=False)
    last_face = lax.index_in_dim(split, per_elem - 1, axis_at + 1, keepdims=False)
    empty_face = jnp.zeros_like(lax.slice_in_dim(first_face, 0, 1, axis=axis_at))
    from_left = jnp.concatenate([empty_face, lax.slice_in_dim(last_face, 0, elements - 1, axis=axis_at)], axis_at)
    from_right = jnp.concatenate([lax.slice_in_dim(first_face, 1, elements, axis=axis_at), empty_face], axis_at)
    middle = lax.slice_in_dim(split, 1, per_elem - 1, axis=axis_at + 1)
    joined = jnp.concatenate([jnp.expand_dims(first_face + from_left, axis_at + 1), middle,
                              jnp.expand_dims(last_face + from_right, axis_at + 1)], axis_at + 1)
    return joined.reshape(dims_of)


def assemble_all(stacked, per_elem):
    return fold_local(fold_local(fold_local(stacked, 1, per_elem), 2, per_elem), 3, per_elem)


def edge_mask(total):
    spots = jnp.arange(total)
    return ((spots > 0) & (spots < total - 1)).astype(jnp.float32)


def box_mask(size_x, size_y, size_z):
    return edge_mask(size_x)[:, None, None] * edge_mask(size_y)[None, :, None] * edge_mask(size_z)[None, None, :]


def weight_field(size_x, size_y, size_z, weights):
    wvec = jnp.asarray(weights, jnp.float32)
    along_x = jnp.tile(wvec, size_x // 8)
    along_y = jnp.tile(wvec, size_y // 8)
    along_z = jnp.tile(wvec, size_z // 8)
    return along_x[:, None, None] * along_y[None, :, None] * along_z[None, None, :]


def local_operator(field, weighted, derivative, z_matrix):
    size_x, size_y, size_z = field.shape
    precise = lax.Precision.HIGHEST
    z_block = z_matrix.shape[0]
    grad_x = jnp.einsum("ab,ebyz->eayz", derivative, field.reshape(size_x // 8, 8, size_y, size_z), precision=precise).reshape(field.shape)
    grad_y = jnp.einsum("ab,xebz->xeaz", derivative, field.reshape(size_x, size_y // 8, 8, size_z), precision=precise).reshape(field.shape)
    grad_z = jnp.dot(field.reshape(-1, z_block), z_matrix.T, precision=precise, preferred_element_type=jnp.float32).reshape(field.shape)
    flux_x = (weighted * grad_x).reshape(size_x // 8, 8, size_y, size_z)
    flux_y = (weighted * grad_y).reshape(size_x, size_y // 8, 8, size_z)
    flux_z = (weighted * grad_z).reshape(-1, z_block)
    back_x = jnp.einsum("ab,eayz->ebyz", derivative, flux_x, precision=precise).reshape(field.shape)
    back_y = jnp.einsum("ab,xeaz->xebz", derivative, flux_y, precision=precise).reshape(field.shape)
    back_z = jnp.dot(flux_z, z_matrix, precision=precise, preferred_element_type=jnp.float32).reshape(field.shape)
    return back_x + back_y + back_z


def diagonal_local(weighted, derivative, z_matrix):
    size_x, size_y, size_z = weighted.shape
    precise = lax.Precision.HIGHEST
    squared = derivative * derivative
    z_block = z_matrix.shape[0]
    part_x = jnp.einsum("ka,ekyz->eayz", squared, weighted.reshape(size_x // 8, 8, size_y, size_z), precision=precise).reshape(weighted.shape)
    part_y = jnp.einsum("ka,xekz->xeaz", squared, weighted.reshape(size_x, size_y // 8, 8, size_z), precision=precise).reshape(weighted.shape)
    part_z = jnp.dot(weighted.reshape(-1, z_block), z_matrix * z_matrix, precision=precise, preferred_element_type=jnp.float32).reshape(weighted.shape)
    return part_x + part_y + part_z


def restrict(field, interp):
    size_x, size_y, size_z = field.shape
    precise = lax.Precision.HIGHEST
    section_x = jnp.einsum("ai,eayz->eiyz", interp, field.reshape(size_x // 8, 8, size_y, size_z), precision=precise).reshape(size_x // 4, size_y, size_z)
    section_y = jnp.einsum("ai,xeaz->xeiz", interp, section_x.reshape(size_x // 4, size_y // 8, 8, size_z), precision=precise).reshape(size_x // 4, size_y // 4, size_z)
    section_z = jnp.einsum("ai,xyea->xyei", interp, section_y.reshape(size_x // 4, size_y // 4, size_z // 8, 8), precision=precise)
    return section_z.reshape(size_x // 4, size_y // 4, size_z // 4)


def prolong(coarse, interp):
    size_x, size_y, size_z = coarse.shape
    precise = lax.Precision.HIGHEST
    section_z = jnp.einsum("ai,xyei->xyea", interp, coarse.reshape(size_x, size_y, size_z // 2, 2), precision=precise).reshape(size_x, size_y, size_z * 4)
    section_y = jnp.einsum("ai,xeiz->xeaz", interp, section_z.reshape(size_x, size_y // 2, 2, size_z * 4), precision=precise).reshape(size_x, size_y * 4, size_z * 4)
    section_x = jnp.einsum("ai,eiyz->eayz", interp, section_y.reshape(size_x // 2, 2, size_y * 4, size_z * 4), precision=precise)
    return section_x.reshape(size_x * 4, size_y * 4, size_z * 4)


def coarse_matrices(weighted, interp, slopes):
    size_x, size_y, size_z = weighted.shape
    precise = lax.Precision.HIGHEST
    shaped = weighted.reshape(size_x // 8, 8, size_y // 8, 8, size_z // 8, 8)
    interp_t = interp.T
    mass_pair = jnp.asarray(interp_t[:, None, :] * interp_t[None, :, :], jnp.float32)
    grad_pair = jnp.asarray(slopes[:, None, None] * slopes[None, :, None] * np.ones((1, 1, 8)), jnp.float32)
    form = "xaybzc,ipa,jqb,krc->ijkpqrxyz"
    total = jnp.einsum(form, shaped, grad_pair, mass_pair, mass_pair, precision=precise)
    total = total + jnp.einsum(form, shaped, mass_pair, grad_pair, mass_pair, precision=precise)
    total = total + jnp.einsum(form, shaped, mass_pair, mass_pair, grad_pair, precision=precise)
    return total.reshape(8, 8, -1)


def coarse_diagonal(galerkin, ex_n, ey_n, ez_n):
    eye_table = jnp.eye(8, dtype=jnp.float32)
    flat = jnp.sum(galerkin * eye_table[:, :, None], axis=1)
    return flat.reshape(2, 2, 2, ex_n, ey_n, ez_n).transpose(3, 0, 4, 1, 5, 2).reshape(2 * ex_n, 2 * ey_n, 2 * ez_n)


def coarse_apply(galerkin, coarse):
    size_x, size_y, size_z = coarse.shape
    ex_n, ey_n, ez_n = size_x // 2, size_y // 2, size_z // 2
    flat = coarse.reshape(ex_n, 2, ey_n, 2, ez_n, 2).transpose(1, 3, 5, 0, 2, 4).reshape(8, -1)
    result = jnp.sum(galerkin * flat[None, :, :], axis=1)
    return result.reshape(2, 2, 2, ex_n, ey_n, ez_n).transpose(3, 0, 4, 1, 5, 2).reshape(coarse.shape)


def reference(rhs_local, coefficient):
    derivative_np, weights, interp_np, slopes = tables()
    derivative = jnp.asarray(derivative_np, jnp.float32)
    interp = jnp.asarray(interp_np, jnp.float32)
    z_block = min(EZ, 16)
    z_matrix = jnp.asarray(np.kron(np.eye(z_block), derivative_np), jnp.float32)
    size_x, size_y, size_z = rhs_local.shape
    weighted = coefficient * weight_field(size_x, size_y, size_z, weights)
    fmask = box_mask(size_x, size_y, size_z)
    w_blocks = weighted.reshape(N_DOM, size_x // N_DOM, size_y, size_z)

    def apply_block(pair_in):
        return local_operator(pair_in[0], pair_in[1], derivative, z_matrix)

    def operate(field):
        pieces = lax.map(apply_block, (field.reshape(w_blocks.shape), w_blocks))
        return fmask * assemble_all(pieces.reshape(field.shape)[None], 8)[0]

    def galerkin_block(block_in):
        return coarse_matrices(block_in, interp_np, slopes)

    summed = assemble_all(jnp.stack([rhs_local, diagonal_local(weighted, derivative, z_matrix)]), 8)
    residual = fmask * summed[0]
    inverse = fmask / summed[1]
    theta = 1.1
    delta = 0.9
    sigma_val = theta / delta
    rho_prev = 1.0 / sigma_val
    rho_next = 1.0 / (2.0 * sigma_val - rho_prev)
    step_one = inverse * residual / theta
    res_one = residual - operate(step_one)
    second = step_one + rho_next * rho_prev * step_one + (2.0 * rho_next / delta) * inverse * res_one
    res_two = residual - operate(second)
    galerkin = lax.map(galerkin_block, w_blocks)
    galerkin = galerkin.transpose(1, 2, 0, 3).reshape(8, 8, -1)
    coarse_stack = assemble_all(jnp.stack([restrict(res_two, interp), coarse_diagonal(galerkin, MX // 2, MY // 2, MZ // 2)]), 2)
    cmask = box_mask(MX, MY, MZ)
    coarse_rhs = cmask * coarse_stack[0]
    coarse_diag = coarse_stack[1]
    coarse_one = (2.0 / 3.0) * coarse_rhs / coarse_diag
    image_c = cmask * assemble_all(coarse_apply(galerkin, coarse_one)[None], 2)[0]
    coarse_solution = coarse_one + (2.0 / 3.0) * (coarse_rhs - image_c) / coarse_diag
    preconditioned = second + fmask * prolong(coarse_solution, interp)
    return preconditioned, coarse_solution
```

```python
import functools

import jax
import jax.numpy as jnp
import numpy as np
from jax import lax
from jax.experimental import pallas as pl
from jax.experimental.pallas import tpu as pltpu
from jax.sharding import PartitionSpec as P

MESH = pl.DeviceIdType.MESH
HIGHEST = lax.Precision.HIGHEST
F32 = jnp.float32
BF16 = jnp.bfloat16

NEAR = [(dx, dy) for dx in (-1, 0, 1) for dy in (-1, 0, 1) if (dx, dy) != (0, 0)]
WIDE = [(dx, dy) for dx in (-2, -1, 0, 1, 2) for dy in (-1, 0, 1) if (dx, dy) != (0, 0)]
FAR = [pair for pair in WIDE if pair not in NEAR]
SIDE = [pair for pair in NEAR if pair[1] == 0]
ROWS = [pair for pair in NEAR if pair[0] == 0]
EDGE = [pair for pair in NEAR if pair[0] != 0 and pair[1] != 0]


def opposite(table, pair):
    return table.index((-pair[0], -pair[1]))


def tables():
    degree = 7
    points = np.array(
        [
            -1.0,
            -0.8717401485096066,
            -0.5917001814331423,
            -0.2092992179024789,
            0.2092992179024789,
            0.5917001814331423,
            0.8717401485096066,
            1.0,
        ]
    )
    previous = np.ones(points.shape)
    values = points.copy()
    for level in range(1, degree):
        following = ((2 * level + 1) * points * values - level * previous) / (level + 1)
        previous = values
        values = following
    weights = 2.0 / (degree * (degree + 1) * values**2)
    derivative = np.zeros((8, 8))
    for row_at in range(8):
        for col_at in range(8):
            if row_at != col_at:
                derivative[row_at, col_at] = values[row_at] / (
                    values[col_at] * (points[row_at] - points[col_at])
                )
    derivative[0, 0] = -degree * (degree + 1) / 4.0
    derivative[7, 7] = degree * (degree + 1) / 4.0
    interp = np.stack([(1.0 - points) / 2.0, (1.0 + points) / 2.0], axis=1)
    return derivative, weights, interp


DER, WTS, INT = tables()
MASS = [INT[:, 0] * INT[:, 0], INT[:, 0] * INT[:, 1], INT[:, 1] * INT[:, 1]]


def moment_maps(elements, order, slope):
    maps = np.zeros((len(order), elements + 1, 8 * elements))
    for at, offset in enumerate(order):
        for e in range(elements):
            nodes = slice(8 * e, 8 * e + 8)
            if offset == 0:
                maps[at, e, nodes] += 0.25 if slope else MASS[0]
                maps[at, e + 1, nodes] += 0.25 if slope else MASS[2]
            elif offset == 1:
                maps[at, e, nodes] += -0.25 if slope else MASS[1]
            else:
                maps[at, e + 1, nodes] += -0.25 if slope else MASS[1]
    return maps


def unique_interp(elements):
    maps = np.zeros((8 * elements, elements + 1))
    for e in range(elements):
        maps[8 * e : 8 * e + 8, e] = INT[:, 0]
        maps[8 * e : 8 * e + 8, e + 1] = INT[:, 1]
    return maps


def unique_copies(elements):
    maps = np.zeros((2 * elements, elements + 1))
    for e in range(elements):
        maps[2 * e, e] = 1.0
        maps[2 * e + 1, e + 1] = 1.0
    return maps


def shifted(matrix):
    return np.stack(
        [np.array([matrix[a, (a - k) % 8] for a in range(8)]) for k in range(8)]
    )


def constants(ey, ez):
    parts = {}

    def spread(cols):
        return np.repeat(cols[..., None], 128, axis=-1)

    parts["grad_y"] = spread(shifted(DER)).reshape(64, 128)
    parts["back_y"] = spread(shifted(DER.T)).reshape(64, 128)
    parts["square_y"] = spread(shifted((DER * DER).T)).reshape(64, 128)
    parts["weight"] = WTS[:, None] * np.tile(WTS, 16)[None, :]
    order_z = (0, 1, -1)
    for name, slope in (("moment_m", False), ("moment_s", True)):
        block = np.zeros((128, 128))
        for at, one in enumerate(moment_maps(ez, order_z, slope)):
            block[:, 32 * at : 32 * at + ez + 1] = one.T
        parts[name] = block
    order_y = (-1, 0, 1)
    mass_y = np.zeros((3, 8, 8 * ey))
    mass_y[:, : ey + 1] = moment_maps(ey, order_y, False)
    slope_y = np.zeros((3, 8, 8 * ey))
    slope_y[:, : ey + 1] = moment_maps(ey, order_y, True)
    mass_y = mass_y.reshape(24, 8 * ey)
    slope_y = slope_y.reshape(24, 8 * ey)
    for name, sign in (("mix_plus", 0.25), ("mix_minus", -0.25)):
        block = np.zeros((24, 128))
        block[:, : 24 * ey] = np.concatenate([slope_y, mass_y, sign * mass_y], axis=1)
        parts[name] = block
    low = unique_interp(ey)
    block = np.zeros((16, 128))
    block[: ey + 1, : 8 * ey] = low.T
    block[8 : 8 + ey + 1, 8 * ey : 16 * ey] = low.T
    parts["rest_y"] = block
    block = np.zeros((128, 128))
    block[:, : ez + 1] = unique_interp(ez)
    parts["rest_z"] = block
    block = np.zeros((128, 128))
    block[: ez + 1, :] = unique_interp(ez).T
    parts["prol_z"] = block
    block = np.zeros((128, 128))
    block[: ez + 1, : 2 * ez] = unique_copies(ez).T
    parts["copy_z"] = block
    block = np.zeros((80, 128))
    for side in range(2):
        block[32 * side : 32 * side + 32, 8 * side : 8 * side + ey + 1] = low
        block[64 + 8 * side : 72 + 8 * side, 8 * side : 8 * side + ey + 1] = unique_copies(ey)
    parts["prol_y"] = block
    spots = {}
    at = 0
    for name, block in parts.items():
        spots[name] = (at, block.shape[0])
        at += block.shape[0]
    flat = np.concatenate(list(parts.values())).astype(np.float32)

    def halves(matrix):
        matrix = jnp.asarray(matrix, F32)
        high = matrix.astype(BF16)
        low = (matrix - high.astype(F32)).astype(BF16)
        top = jnp.concatenate([high, low], axis=1)
        return jnp.concatenate(
            [top, jnp.concatenate([high, jnp.zeros_like(low)], axis=1)], axis=0
        )

    eye = np.eye(ez)
    mats = jnp.stack(
        [halves(np.kron(eye, m)) for m in (DER.T, DER, DER * DER)]
    )
    return spots, jnp.asarray(flat), mats


def kernel(
    spots, n_dom, n_sub, coef_hbm, rhs_hbm, flat_hbm, mats_hbm, out_ref, coarse_ref,
    coef, rhs, flat, mats, weighted, field, held, fmask, fmult, inverse, pmine,
    xs1, ys1, es1, xs2, ys2, es2, ds, cs,
    xr1, yr1, er1, xr2, yr2, er2, pr, dr, cr,
    load_sem, s1, r1, sp, rp, sd, rd, s2, r2, s3, r3,
):
    dom = lax.axis_index("dom")
    sub = lax.axis_index("sub")

    def present(pair):
        dx, dy = pair
        conds = []
        if dx < 0:
            conds.append(dom >= -dx)
        if dx > 0:
            conds.append(dom < n_dom - dx)
        if dy < 0:
            conds.append(sub >= 1)
        if dy > 0:
            conds.append(sub < n_sub - 1)
        return functools.reduce(jnp.logical_and, conds)

    def target(pair):
        return (dom + pair[0], sub + pair[1])

    def piece(name):
        start, count = spots[name]
        return flat[start : start + count, :]

    for buffer in (xr1, yr1, er1, xr2, yr2, er2, pr, dr, cr):
        buffer[...] = jnp.zeros_like(buffer)

    barrier = pltpu.get_barrier_semaphore()
    for pair in WIDE:

        @pl.when(present(pair))
        def _(pair=pair):
            pl.semaphore_signal(barrier, inc=1, device_id=target(pair), device_id_type=MESH)

    loads = []
    for at, (source, dest) in enumerate(
        ((coef_hbm, coef), (flat_hbm, flat), (mats_hbm, mats), (rhs_hbm, rhs))
    ):
        load = pltpu.make_async_copy(source, dest, load_sem.at[at])
        load.start()
        loads.append(load)

    row = lax.broadcasted_iota(jnp.int32, (256, 128), 0)
    lane = lax.broadcasted_iota(jnp.int32, (256, 128), 1)
    x_at = lax.shift_right_logical(row, 5)
    y_at = row & 31
    place_x = dom * 8 + x_at
    place_y = sub * 32 + y_at
    inside = (
        (place_x > 0) & (place_x < 8 * n_dom - 1)
        & (place_y > 0) & (place_y < 32 * n_sub - 1)
        & (lane > 0) & (lane < 127)
    )
    mask = jnp.where(inside, 1.0, 0.0)
    fmask[...] = mask
    b_at = row & 7
    c_at = lane & 7
    twice = jnp.where((x_at == 0) | (x_at == 7), 2.0, 1.0)
    twice = twice * jnp.where((b_at == 0) | (b_at == 7), 2.0, 1.0)
    fmult[...] = mask * twice * jnp.where((c_at == 0) | (c_at == 7), 2.0, 1.0)

    lane8 = lax.broadcasted_iota(jnp.int32, (8, 128), 1)
    sub8 = lax.broadcasted_iota(jnp.int32, (8, 128), 0)
    z_low = ((lane8 & 7) == 0) & (lane8 > 0)
    z_high = ((lane8 & 7) == 7) & (lane8 < 127)

    def fold(v):
        v = v.reshape(32, 8, 128)
        v = v + jnp.where(
            z_high[None], pltpu.roll(v, 127, 2),
            jnp.where(z_low[None], pltpu.roll(v, 1, 2), 0.0),
        )
        v4 = v.reshape(8, 4, 8, 128)
        up = pltpu.roll(v, 1, 1).reshape(8, 4, 8, 128)
        down = pltpu.roll(v, 7, 1).reshape(8, 4, 8, 128)
        none = jnp.zeros((8, 1, 8, 128), F32)
        up = jnp.concatenate([none, up[:, :3]], axis=1)
        down = jnp.concatenate([down[:, 1:], none], axis=1)
        v4 = v4 + jnp.where(
            (sub8 == 0)[None, None], up, jnp.where((sub8 == 7)[None, None], down, 0.0)
        )
        return v4.reshape(256, 128)

    def along_x(v, matrix, sign):
        planes = v.reshape(8, 32, 128)
        even = [planes[b] + planes[7 - b] for b in range(4)]
        odd = [planes[b] - planes[7 - b] for b in range(4)]
        low = []
        high = []
        for a in range(4):
            p = sum(float(matrix[a, b] + matrix[a, 7 - b]) / 2 * even[b] for b in range(4))
            q = sum(float(matrix[a, b] - matrix[a, 7 - b]) / 2 * odd[b] for b in range(4))
            low.append(p + q)
            high.append(p - q if sign > 0 else q - p)
        return jnp.stack(low + high[::-1]).reshape(256, 128)

    def along_y(v, name):
        v = v.reshape(32, 8, 128)
        cols = piece(name).reshape(8, 8, 128)
        total = cols[0][None] * v
        for k in range(1, 8):
            total = total + cols[k][None] * pltpu.roll(v, k, 1)
        return total.reshape(256, 128)

    def along_z(v, at):
        high = v.astype(BF16)
        low = (v - high.astype(F32)).astype(BF16)
        both = jnp.concatenate([high, low], axis=1)
        wide = jnp.dot(both, mats[at], preferred_element_type=F32)
        return wide[:, :128] + wide[:, 128:]

    def local_operator(u):
        w = weighted[...]
        back = along_z(w * along_z(u, 0), 1)
        back = back + along_x(w * along_x(u, DER, -1), DER.T, -1)
        return back + along_y(w * along_y(u, "grad_y"), "back_y")

    def send(table, pair, source, landing, s_sem, r_sem):
        at = opposite(table, pair)

        @pl.when(present(pair))
        def _():
            pltpu.make_async_remote_copy(
                src_ref=source,
                dst_ref=landing.at[at],
                send_sem=s_sem.at[table.index(pair)],
                recv_sem=r_sem.at[at],
                device_id=target(pair),
                device_id_type=MESH,
            ).start()

    def settle(table, pair, source, landing, s_sem, r_sem, sent):
        at = table.index(pair)

        @pl.when(present(pair))
        def _():
            copy = pltpu.make_async_remote_copy(
                src_ref=source,
                dst_ref=landing.at[at],
                send_sem=s_sem.at[at],
                recv_sem=r_sem.at[at],
                device_id=target(pair),
                device_id_type=MESH,
            )
            if sent:
                copy.wait_send()
            else:
                copy.wait_recv()

    def corner_rows(low, high):
        tiles = {}
        for dx, dy in EDGE:
            face = low if dy < 0 else high
            keep = 0 if dx < 0 else 7
            goal = 7 if dx < 0 else 0
            tiles[(dx, dy)] = jnp.where(sub8 == goal, pltpu.roll(face, (goal - keep) % 8, 0), 0.0)
        return tiles

    def pack(refs, fields, xs, ys, es):
        for f in range(fields):
            ref = refs.at[f]
            low = ref[pl.ds(0, 8, stride=32), :]
            high = ref[pl.ds(31, 8, stride=32), :]
            xs[0, f] = ref[0:32, :]
            xs[1, f] = ref[224:256, :]
            ys[0, f] = low
            ys[1, f] = high
            tiles = corner_rows(low, high)
            for at, pair in enumerate(EDGE):
                es[at, f] = tiles[pair]

    def exchange(xs, ys, es, xr, yr, er, s_sem, r_sem):
        plan = []
        for pair in EDGE:
            plan.append((EDGE, pair, es.at[EDGE.index(pair)], er, s_sem.at[2], r_sem.at[2]))
        for pair in SIDE:
            plan.append((SIDE, pair, xs.at[SIDE.index(pair)], xr, s_sem.at[0], r_sem.at[0]))
        for pair in ROWS:
            plan.append((ROWS, pair, ys.at[ROWS.index(pair)], yr, s_sem.at[1], r_sem.at[1]))
        for item in plan:
            send(*item)
        return plan

    def unpack(refs, fields, xr, yr, er):
        for f in range(fields):
            ref = refs.at[f]
            ref[0:32, :] += xr[0, f]
            ref[224:256, :] += xr[1, f]
            for at, start in ((0, 0), (1, 31)):
                dy = ROWS[at][1]
                extra = yr[at, f]
                for number, pair in enumerate(EDGE):
                    if pair[1] == dy:
                        extra = extra + er[number, f]
                ref[pl.ds(start, 8, stride=32), :] += extra

    loads[0].wait()
    loads[1].wait()
    w_yz = piece("weight")
    planes = []
    c4 = coef[...].reshape(8, 4, 8, 128)
    for a in range(8):
        planes.append((c4[a] * (w_yz * float(WTS[a]))[None]).reshape(32, 128))
    w = jnp.concatenate(planes, axis=0)
    weighted[...] = w
    loads[2].wait()
    square = (DER * DER).T
    field[1] = fold(along_z(w, 2) + along_x(w, square, 1) + along_y(w, "square_y"))
    loads[3].wait()
    field[0] = fold(rhs[...].reshape(256, 128))
    pack(field, 2, xs1, ys1, es1)

    count_x = 1
    for offset in (1, 2):
        count_x = count_x + jnp.where(dom >= offset, 1, 0) + jnp.where(dom < n_dom - offset, 1, 0)
    count_y = 1 + jnp.where(sub >= 1, 1, 0) + jnp.where(sub < n_sub - 1, 1, 0)
    pl.semaphore_wait(barrier, count_x * count_y - 1)

    plans = exchange(xs1, ys1, es1, xr1, yr1, er1, s1, r1)
    first = list(plans)

    w3 = weighted[...].reshape(8, 32, 128)
    moments = [sum(float(m[a]) * w3[a] for a in range(8) if m[a] != 0.0) for m in MASS]
    moments.append(moments[0] + 2.0 * moments[1] + moments[2])
    stack = jnp.concatenate(moments, axis=0)
    mass_z = jnp.dot(stack, piece("moment_m"), precision=HIGHEST, preferred_element_type=F32)
    slope_z = jnp.dot(stack, piece("moment_s"), precision=HIGHEST, preferred_element_type=F32)
    none = jnp.zeros((32, 128), F32)
    for at in range(3):
        part = slice(32 * at, 32 * at + 32)
        parts = jnp.concatenate([mass_z[part], slope_z[part], mass_z[96:128], none], axis=0)
        mix = piece("mix_minus" if at == 1 else "mix_plus")
        pmine[at] = jnp.dot(mix, parts, precision=HIGHEST, preferred_element_type=F32)
    ds[0] = pmine[0, 8:16, :]
    ds[1] = pmine[2, 8:16, :]
    stencil = [(NEAR, pair, pmine, pr, sp, rp) for pair in NEAR]
    diags = [(FAR, pair, ds, dr, sd, rd) for pair in FAR]
    for item in stencil + diags:
        send(*item)

    for item in first:
        settle(*item, False)
    unpack(field, 2, xr1, yr1, er1)

    residual = fmask[...] * field[0]
    inv = fmask[...] / field[1]
    inverse[...] = inv
    field[0] = residual
    theta = 1.1
    delta = 0.9
    sigma = theta / delta
    rho0 = 1.0 / sigma
    rho1 = 1.0 / (2.0 * sigma - rho0)
    step_one = inv * residual / theta
    out_ref[...] = step_one.reshape(8, 32, 128)
    held[0] = fold(local_operator(step_one))
    pack(held, 1, xs2, ys2, es2)
    second_plan = exchange(xs2, ys2, es2, xr2, yr2, er2, s2, r2)

    for item in stencil + diags:
        settle(*item, False)

    def block(dx, dy, at):
        if (dx, dy) == (0, 0):
            return pmine[at]
        return pr[NEAR.index((dx, dy)), at]

    row_low = sub8 < 2
    row_mid = sub8 == 2

    def extend(parts):
        rows = []
        for v in range(4):
            sums = []
            for dy in (-1, 0, 1):
                one = parts(v - 2, dy, 1)
                two = parts(v - 1, dy, 0)
                sums.append(one + two)
            rim = jnp.where(row_low, sums[2], jnp.where(row_mid, 0.0, sums[0]))
            rows.append(pltpu.roll(sums[1], 1, 0) + pltpu.roll(rim, 5, 0))
        return rows

    def diag_part(dx, dy, vx):
        if abs(dx) == 2:
            return dr[FAR.index((dx, dy)), vx]
        return block(dx, dy, 2 * vx)[8:16]

    ext_diag = extend(diag_part)
    vertex_y = sub * 4 + sub8 - 1
    good_yz = (vertex_y > 0) & (vertex_y < 4 * n_sub) & (sub8 < 7) & (lane8 > 0) & (lane8 < 16)
    scales = []
    for v in range(4):
        vertex_x = dom + v - 1
        good = good_yz & (vertex_x > 0) & (vertex_x < n_dom)
        scales.append(jnp.where(good, (2.0 / 3.0) / jnp.where(good, ext_diag[v], 1.0), 0.0))

    row_is_0 = (sub8 == 0)[None]
    row_is_4 = (sub8 == 4)[None]
    joined = {}
    for dx in (-1, 0, 1):
        for at in range(3):
            rim = jnp.where(
                row_is_0, block(dx, 1, at).reshape(3, 8, 128),
                jnp.where(row_is_4, block(dx, -1, at).reshape(3, 8, 128), 0.0),
            )
            joined[(dx, at)] = block(dx, 0, at).reshape(3, 8, 128) + pltpu.roll(rim, 4, 1)
    stencils = [
        [joined[(-1, 1)], joined[(0, 0)] + joined[(-1, 2)], joined[(0, 1)]],
        [joined[(0, 1)], joined[(0, 2)] + joined[(1, 0)], joined[(1, 1)]],
    ]
    for vx in range(2):
        for at in range(3):
            mats_at = vx * 3 + at
            cs[1 + mats_at] = stencils[vx][at]

    for item in second_plan:
        settle(*item, False)
    unpack(held, 1, xr2, yr2, er2)
    residual = field[0]
    step_one = out_ref[...].reshape(256, 128)
    res_one = residual - fmask[...] * held[0]
    second = (1.0 + rho1 * rho0) * step_one + (2.0 * rho1 / delta) * inverse[...] * res_one
    out_ref[...] = second.reshape(8, 32, 128)

    defect = residual - fmult[...] * local_operator(second)
    d3 = defect.reshape(8, 32, 128)
    halves = jnp.concatenate(
        [sum(float(INT[a, i]) * d3[a] for a in range(8) if INT[a, i] != 0.0) for i in range(2)]
        + [jnp.zeros((64, 128), F32)],
        axis=0,
    )
    coarse = jnp.dot(piece("rest_y"), halves, precision=HIGHEST, preferred_element_type=F32)
    coarse = jnp.dot(coarse, piece("rest_z"), precision=HIGHEST, preferred_element_type=F32)
    cs[0, 0:2] = coarse.reshape(2, 8, 128)
    last = [(WIDE, pair, cs.at[0, pl.ds(0, 2)], cr, s3, r3) for pair in WIDE]
    for item in last:
        send(*item)
    for item in last:
        settle(*item, False)

    def rhs_part(dx, dy, vx):
        if (dx, dy) == (0, 0):
            return cs[0, vx]
        return cr[WIDE.index((dx, dy)), vx]

    ext_rhs = extend(rhs_part)
    ones = [scales[v] * ext_rhs[v] for v in range(4)]
    packed = [c + pltpu.roll(c, 31, 1) + pltpu.roll(c, 65, 1) for c in ones]
    around = [[c, pltpu.roll(c, 7, 0), pltpu.roll(c, 6, 0)] for c in packed]
    results = []
    for vx in range(2):
        total = jnp.zeros((8, 128), F32)
        for at in range(3):
            block3 = cs[1 + vx * 3 + at]
            for dy in range(3):
                total = total + block3[dy] * around[vx + at][dy]
        image = total + pltpu.roll(total, 96, 1) + pltpu.roll(total, 64, 1)
        one = pltpu.roll(ones[vx + 1], 7, 0)
        scale = pltpu.roll(scales[vx + 1], 7, 0)
        right = pltpu.roll(ext_rhs[vx + 1], 7, 0)
        results.append(one + scale * (right - image))
    both = jnp.concatenate(results, axis=0)
    nodes = jnp.dot(both, piece("prol_z"), precision=HIGHEST, preferred_element_type=F32)
    copies = jnp.dot(both, piece("copy_z"), precision=HIGHEST, preferred_element_type=F32)
    prol_y = piece("prol_y")[:, 0:16]
    fine = jnp.dot(prol_y[0:64], nodes, precision=HIGHEST, preferred_element_type=F32)
    copies = jnp.dot(prol_y[64:80], copies, precision=HIGHEST, preferred_element_type=F32)
    coarse_ref[...] = copies.reshape(2, 8, 128)[:, :, 0:32]
    for a in range(8):
        grown = float(INT[a, 0]) * fine[0:32] + float(INT[a, 1]) * fine[32:64]
        out_ref[a] = out_ref[a] + fmask[32 * a : 32 * a + 32, :] * grown

    for item in first + stencil + diags + second_plan + last:
        settle(*item, True)


def solution(mesh):
    n_dom = mesh.shape["dom"]
    n_sub = mesh.shape["sub"]

    def shards(rhs_local, coefficient):
        spots, flat, mats = constants(4, 16)
        any_space = pl.BlockSpec(memory_space=pl.ANY)
        vmem = pl.BlockSpec(memory_space=pltpu.VMEM)

        def space(*shape):
            return pltpu.VMEM(shape, F32)

        dma = pltpu.SemaphoreType.DMA
        return pl.pallas_call(
            functools.partial(kernel, spots, n_dom, n_sub),
            out_shape=(
                jax.ShapeDtypeStruct((8, 32, 128), F32),
                jax.ShapeDtypeStruct((2, 8, 32), F32),
            ),
            in_specs=[any_space] * 4,
            out_specs=(vmem, vmem),
            scratch_shapes=[
                space(8, 32, 128),
                space(8, 32, 128),
                pltpu.VMEM(flat.shape, F32),
                pltpu.VMEM(mats.shape, BF16),
                space(256, 128),
                space(2, 256, 128),
                space(1, 256, 128),
                space(256, 128),
                space(256, 128),
                space(256, 128),
                space(3, 24, 128),
                space(2, 2, 32, 128),
                space(2, 2, 8, 128),
                space(4, 2, 8, 128),
                space(2, 1, 32, 128),
                space(2, 1, 8, 128),
                space(4, 1, 8, 128),
                space(2, 8, 128),
                space(7, 3, 8, 128),
                space(2, 2, 32, 128),
                space(2, 2, 8, 128),
                space(4, 2, 8, 128),
                space(2, 1, 32, 128),
                space(2, 1, 8, 128),
                space(4, 1, 8, 128),
                space(8, 3, 24, 128),
                space(6, 2, 8, 128),
                space(14, 2, 8, 128),
                dma((4,)),
                dma((3, 4)),
                dma((3, 4)),
                dma((8,)),
                dma((8,)),
                dma((6,)),
                dma((6,)),
                dma((3, 4)),
                dma((3, 4)),
                dma((14,)),
                dma((14,)),
            ],
            compiler_params=pltpu.CompilerParams(collective_id=0, has_side_effects=True),
        )(coefficient, rhs_local, flat, mats)

    return jax.shard_map(
        shards,
        mesh=mesh,
        in_specs=(P("dom", "sub", None), P("dom", "sub", None)),
        out_specs=(P("dom", "sub", None), P("dom", "sub", None)),
        check_vma=False,
    )
```

```python
import functools

import jax
import jax.numpy as jnp
import numpy as np
from jax import lax
from jax.experimental import pallas as pl
from jax.experimental.pallas import tpu as pltpu
from jax.sharding import PartitionSpec as P

MESH = pl.DeviceIdType.MESH
HIGHEST = lax.Precision.HIGHEST
F32 = jnp.float32
BF16 = jnp.bfloat16

NEAR = [(dx, dy) for dx in (-1, 0, 1) for dy in (-1, 0, 1) if (dx, dy) != (0, 0)]
WIDE = [(dx, dy) for dx in (-2, -1, 0, 1, 2) for dy in (-1, 0, 1) if (dx, dy) != (0, 0)]
SIDE = [pair for pair in NEAR if pair[1] == 0]
RIMS = [pair for pair in NEAR if pair[1] != 0]


def opposite(table, pair):
    return table.index((-pair[0], -pair[1]))


def tables():
    degree = 7
    points = np.array(
        [
            -1.0,
            -0.8717401485096066,
            -0.5917001814331423,
            -0.2092992179024789,
            0.2092992179024789,
            0.5917001814331423,
            0.8717401485096066,
            1.0,
        ]
    )
    previous = np.ones(points.shape)
    values = points.copy()
    for level in range(1, degree):
        following = ((2 * level + 1) * points * values - level * previous) / (level + 1)
        previous = values
        values = following
    weights = 2.0 / (degree * (degree + 1) * values**2)
    derivative = np.zeros((8, 8))
    for row_at in range(8):
        for col_at in range(8):
            if row_at != col_at:
                derivative[row_at, col_at] = values[row_at] / (
                    values[col_at] * (points[row_at] - points[col_at])
                )
    derivative[0, 0] = -degree * (degree + 1) / 4.0
    derivative[7, 7] = degree * (degree + 1) / 4.0
    interp = np.stack([(1.0 - points) / 2.0, (1.0 + points) / 2.0], axis=1)
    return derivative, weights, interp


DER, WTS, INT = tables()
MASS = [INT[:, 0] * INT[:, 0], INT[:, 0] * INT[:, 1], INT[:, 1] * INT[:, 1]]


def moment_maps(elements, order, slope):
    maps = np.zeros((len(order), elements + 1, 8 * elements))
    for at, offset in enumerate(order):
        for e in range(elements):
            nodes = slice(8 * e, 8 * e + 8)
            if offset == 0:
                maps[at, e, nodes] += 0.25 if slope else MASS[0]
                maps[at, e + 1, nodes] += 0.25 if slope else MASS[2]
            elif offset == 1:
                maps[at, e, nodes] += -0.25 if slope else MASS[1]
            else:
                maps[at, e + 1, nodes] += -0.25 if slope else MASS[1]
    return maps


def unique_interp(elements):
    maps = np.zeros((8 * elements, elements + 1))
    for e in range(elements):
        maps[8 * e : 8 * e + 8, e] = INT[:, 0]
        maps[8 * e : 8 * e + 8, e + 1] = INT[:, 1]
    return maps


def unique_copies(elements):
    maps = np.zeros((2 * elements, elements + 1))
    for e in range(elements):
        maps[2 * e, e] = 1.0
        maps[2 * e + 1, e + 1] = 1.0
    return maps


def split(matrix):
    high = jnp.asarray(matrix, F32).astype(BF16)
    return high, (jnp.asarray(matrix, F32) - high.astype(F32)).astype(BF16)


def right_halves(matrix):
    high, low = split(matrix)
    top = jnp.concatenate([high, low], axis=1)
    return jnp.concatenate([top, jnp.concatenate([high, jnp.zeros_like(low)], axis=1)], axis=0)


def left_halves(matrix):
    high, low = split(matrix)
    return jnp.concatenate([high, low, high, low], axis=1)


def wide(block):
    return jnp.pad(block, ((0, 0), (0, 256 - block.shape[1])))


def spots_of(parts):
    spots = {}
    at = 0
    for name, block in parts.items():
        spots[name] = (at, block.shape[0])
        at += block.shape[0]
    return spots, jnp.concatenate(list(parts.values()))


def constants(ey, ez):
    square = DER * DER
    eye8 = np.eye(8)
    eye = np.eye(ez)
    early = {
        "square_z": right_halves(np.kron(eye, square)),
        "square_xy": left_halves(np.kron(square.T, eye8) + np.kron(eye8, square.T)),
    }
    low = unique_interp(ey)
    place = np.zeros((4, 8, 8, 16))
    for side in range(2):
        place[..., 8 * side : 8 * side + ey + 1] = (
            INT[:, side][None, :, None, None] * low.reshape(ey, 8, ey + 1)[:, None]
        )
    place = place.reshape(256, 16)
    rest_z = np.zeros((128, 128))
    rest_z[:, : ez + 1] = unique_interp(ez)
    rest_z[:, 32 : 32 + ez + 1] = unique_interp(ez)
    prol_z = np.zeros((128, 128))
    prol_z[: ez + 1, :] = unique_interp(ez).T
    copy_z = np.zeros((128, 128))
    copy_z[: ez + 1, : 2 * ez] = unique_copies(ez).T
    copy_y = np.zeros((16, 16))
    for side in range(2):
        copy_y[8 * side : 8 * side + 8, 8 * side : 8 * side + ey + 1] = unique_copies(ey)
    rest_xy = split(place.T)
    late = {
        "grad_z": right_halves(np.kron(eye, DER.T)),
        "back_z": right_halves(np.kron(eye, DER)),
        "rest_z": right_halves(rest_z),
        "prol_z": right_halves(prol_z),
        "copy_z": wide(jnp.concatenate([split(copy_z)[0]] * 2)),
        "prol_xy": wide(left_halves(place)),
        "grad_xy": jnp.concatenate(
            [left_halves(np.kron(DER, eye8)), left_halves(np.kron(eye8, DER))]
        ),
        "back_x": left_halves(np.kron(DER.T, eye8)),
        "back_y": left_halves(np.kron(eye8, DER.T)),
        "rest_xy": jnp.concatenate([rest_xy[0], rest_xy[1]]),
        "copy_y": wide(left_halves(copy_y)),
    }
    flat = {}
    for name, slope in (("moment_m", False), ("moment_s", True)):
        block = np.zeros((128, 128))
        for at, one in enumerate(moment_maps(ez, (0, 1, -1), slope)):
            block[:, 32 * at : 32 * at + ez + 1] = one.T
        flat[name] = jnp.asarray(block, F32)
    order_y = (-1, 0, 1)
    mass_y = np.zeros((3, 8, 8 * ey))
    mass_y[:, : ey + 1] = moment_maps(ey, order_y, False)
    slope_y = np.zeros((3, 8, 8 * ey))
    slope_y[:, : ey + 1] = moment_maps(ey, order_y, True)
    mass_y = mass_y.reshape(24, 8 * ey)
    slope_y = slope_y.reshape(24, 8 * ey)
    for name, sign in (("mix_plus", 0.25), ("mix_minus", -0.25)):
        block = np.zeros((24, 128))
        block[:, : 24 * ey] = np.concatenate([slope_y, mass_y, sign * mass_y], axis=1)
        flat[name] = jnp.asarray(block, F32)
    return spots_of(early), spots_of(late), spots_of(flat)


def kernel(
    tables_at, n_dom, n_sub, coef_hbm, rhs_hbm, early_hbm, late_hbm, flat_hbm,
    out_ref, coarse_ref,
    coef, rhs, early, late, flat, weighted, field, held, fmask, fmult, inverse, step,
    pmine, ptile, dtile, ctile, stencil,
    xs1, vs1, xs2, vs2,
    xr1, vr1, xr2, vr2, px, pt, dr, cr,
    load_sem, s_sem, r_sem,
):
    early_at, late_at, flat_at = tables_at
    dom = lax.axis_index("dom")
    sub = lax.axis_index("sub")

    loads = []
    for at, (source, dest) in enumerate(
        ((coef_hbm, coef), (early_hbm, early), (rhs_hbm, rhs), (flat_hbm, flat), (late_hbm, late))
    ):
        load = pltpu.make_async_copy(source, dest, load_sem.at[at])
        load.start()
        loads.append(load)

    def present(pair):
        dx, dy = pair
        conds = []
        if dx < 0:
            conds.append(dom >= -dx)
        if dx > 0:
            conds.append(dom < n_dom - dx)
        if dy < 0:
            conds.append(sub >= 1)
        if dy > 0:
            conds.append(sub < n_sub - 1)
        return functools.reduce(jnp.logical_and, conds)

    def target(pair):
        return (dom + pair[0], sub + pair[1])

    for buffer in (xr1, vr1, xr2, vr2, px, pt, dr, cr):
        buffer[...] = jnp.zeros_like(buffer)

    barrier = pltpu.get_barrier_semaphore()
    for pair in WIDE:

        @pl.when(present(pair))
        def _(pair=pair):
            pl.semaphore_signal(barrier, inc=1, device_id=target(pair), device_id_type=MESH)

    near_x = jnp.where(dom >= 1, 1, 0) + jnp.where(dom < n_dom - 1, 1, 0)
    near_y = jnp.where(sub >= 1, 1, 0) + jnp.where(sub < n_sub - 1, 1, 0)
    far_x = near_x + jnp.where(dom >= 2, 1, 0) + jnp.where(dom < n_dom - 2, 1, 0)
    n_side = near_x
    n_rims = near_y * (1 + near_x)
    n_wide = (1 + far_x) * (1 + near_y) - 1

    row = lax.broadcasted_iota(jnp.int32, (256, 128), 0)
    lane = lax.broadcasted_iota(jnp.int32, (256, 128), 1)
    x_at = lax.shift_right_logical(row, 3) & 7
    b_at = row & 7
    c_at = lane & 7
    place_x = dom * 8 + x_at
    place_y = sub * 32 + lax.shift_right_logical(row, 6) * 8 + b_at
    inside = (
        (place_x > 0) & (place_x < 8 * n_dom - 1)
        & (place_y > 0) & (place_y < 32 * n_sub - 1)
        & (lane > 0) & (lane < 127)
    )
    mask = jnp.where(inside, 1.0, 0.0)
    fmask[...] = mask
    twice = jnp.where((x_at == 0) | (x_at == 7), 2.0, 1.0)
    twice = twice * jnp.where((b_at == 0) | (b_at == 7), 2.0, 1.0)
    fmult[...] = mask * twice * jnp.where((c_at == 0) | (c_at == 7), 2.0, 1.0)

    lane8 = lax.broadcasted_iota(jnp.int32, (8, 128), 1)
    sub8 = lax.broadcasted_iota(jnp.int32, (8, 128), 0)
    z_low = ((lane8 & 7) == 0) & (lane8 > 0)
    z_high = ((lane8 & 7) == 7) & (lane8 < 127)

    def weights_along(spot):
        value = jnp.where((spot == 0) | (spot == 7), float(WTS[0]), float(WTS[1]))
        value = jnp.where((spot == 2) | (spot == 5), float(WTS[2]), value)
        return jnp.where((spot == 3) | (spot == 4), float(WTS[3]), value)

    def fold(v):
        v = v.reshape(32, 8, 128)
        v = v + jnp.where(
            z_high[None], pltpu.roll(v, 127, 2),
            jnp.where(z_low[None], pltpu.roll(v, 1, 2), 0.0),
        )
        up = pltpu.roll(v, 1, 1)
        down = pltpu.roll(v, 7, 1)
        none = jnp.zeros((8, 8, 128), F32)
        up = jnp.concatenate([none, up[:24]], axis=0)
        down = jnp.concatenate([down[8:], none], axis=0)
        v = v + jnp.where((sub8 == 0)[None], up, jnp.where((sub8 == 7)[None], down, 0.0))
        return v.reshape(256, 128)

    def halves(v):
        high = v.astype(BF16)
        return high, (v - high.astype(F32)).astype(BF16)

    def dot(left, right):
        return jnp.dot(left, right, preferred_element_type=F32)

    def early_part(name):
        start, count = early_at[name]
        return early[start : start + count, :]

    def late_part(name):
        start, count = late_at[name]
        return late[start : start + count, :]

    def flat_part(name):
        start, count = flat_at[name]
        return flat[start : start + count, :]

    def times_right(pair, matrix):
        both = dot(jnp.concatenate(pair, axis=1), matrix)
        return both[:, :128] + both[:, 128:]

    def stacked(pair):
        high, low = [
            jnp.concatenate([v[64 * j : 64 * j + 64] for j in range(4)], axis=1) for v in pair
        ]
        return jnp.concatenate([high, high, low, low], axis=0)

    def rows_of(v):
        return jnp.concatenate([v[:, 128 * j : 128 * j + 128] for j in range(4)], axis=0)

    def local_operator(u):
        w = weighted[...]
        pair = halves(u)
        both = dot(late_part("grad_xy"), stacked(pair))
        flux_z = halves(w * times_right(pair, late_part("grad_z")))
        flux_x = halves(w * rows_of(both[0:64]))
        flux_y = halves(w * rows_of(both[64:128]))
        back = dot(late_part("back_x"), stacked(flux_x))
        back = back + dot(late_part("back_y"), stacked(flux_y))
        return rows_of(back) + times_right(flux_z, late_part("back_z"))

    def send(table, pair, source, landing, group):
        at = table.index((-pair[0], -pair[1]))

        @pl.when(present(pair))
        def _():
            pltpu.make_async_remote_copy(
                src_ref=source,
                dst_ref=landing.at[at],
                send_sem=s_sem.at[group],
                recv_sem=r_sem.at[group],
                device_id=target(pair),
                device_id_type=MESH,
            ).start()

    counts = {"side": (n_side, (1, 2)), "rims": (n_rims, (1, 2, 3, 4, 6)), "wide": (n_wide, (1, 2, 3, 5, 7, 8, 9, 11, 14))}

    def settle(kind, landing, group, sent):
        count, options = counts[kind]
        for one in options:

            @pl.when(count == one)
            def _(one=one):
                copy = pltpu.make_async_remote_copy(
                    src_ref=landing.at[pl.ds(0, one)],
                    dst_ref=landing.at[pl.ds(0, one)],
                    send_sem=s_sem.at[group],
                    recv_sem=r_sem.at[group],
                    device_id=(dom, sub),
                    device_id_type=MESH,
                )
                if sent:
                    copy.wait_send()
                else:
                    copy.wait_recv()

    def pack(refs, fields, xs, vs):
        for f in range(fields):
            ref = refs.at[f]
            faces = {-1: ref[pl.ds(0, 8, stride=8), :], 1: ref[pl.ds(199, 8, stride=8), :]}
            for j in range(4):
                xs[0, f, 8 * j : 8 * j + 8] = ref[64 * j : 64 * j + 8, :]
                xs[1, f, 8 * j : 8 * j + 8] = ref[64 * j + 56 : 64 * j + 64, :]
            for at, (dx, dy) in enumerate(RIMS):
                face = faces[dy]
                if dx < 0:
                    face = jnp.where(sub8 == 7, pltpu.roll(face, 7, 0), 0.0)
                if dx > 0:
                    face = jnp.where(sub8 == 0, pltpu.roll(face, 1, 0), 0.0)
                vs[at, f] = face

    def exchange(xs, vs, xr, vr, group):
        for pair in RIMS:
            if pair[0] != 0:
                send(RIMS, pair, vs.at[RIMS.index(pair)], vr, group + 1)
        for pair in SIDE:
            send(SIDE, pair, xs.at[SIDE.index(pair)], xr, group)
        for pair in RIMS:
            if pair[0] == 0:
                send(RIMS, pair, vs.at[RIMS.index(pair)], vr, group + 1)

    def unpack(refs, fields, xr, vr):
        for f in range(fields):
            ref = refs.at[f]
            for j in range(4):
                ref[64 * j : 64 * j + 8, :] += xr[0, f, 8 * j : 8 * j + 8]
                ref[64 * j + 56 : 64 * j + 64, :] += xr[1, f, 8 * j : 8 * j + 8]
            for dy, start in ((-1, 0), (1, 199)):
                a, b, c = [vr[RIMS.index((dx, dy)), f] for dx in (-1, 0, 1)]
                ref[pl.ds(start, 8, stride=8), :] += a + b + c

    def in_order(ref):
        v = ref[...].reshape(8, 4, 8, 128)
        return jnp.concatenate([v[:, j] for j in range(4)], axis=0).reshape(256, 128)

    table = weights_along(x_at) * weights_along(b_at) * weights_along(c_at)
    loads[0].wait()
    w = in_order(coef) * table
    weighted[...] = w
    loads[1].wait()
    pair = halves(w)
    diagonal = rows_of(dot(early_part("square_xy"), stacked(pair)))
    field[1] = fold(diagonal + times_right(pair, early_part("square_z")))
    loads[2].wait()
    field[0] = fold(in_order(rhs))
    pack(field, 2, xs1, vs1)

    pl.semaphore_wait(barrier, n_wide)
    exchange(xs1, vs1, xr1, vr1, 0)

    loads[3].wait()
    w4 = weighted[...].reshape(4, 8, 8, 128)
    planes = [w4[:, a].reshape(32, 128) for a in range(8)]
    moments = [sum(float(m[a]) * planes[a] for a in range(8) if m[a] != 0.0) for m in MASS]
    moments.append(moments[0] + 2.0 * moments[1] + moments[2])
    stack = jnp.concatenate(moments, axis=0)
    mass_z = jnp.dot(stack, flat_part("moment_m"), precision=HIGHEST, preferred_element_type=F32)
    slope_z = jnp.dot(stack, flat_part("moment_s"), precision=HIGHEST, preferred_element_type=F32)
    none = jnp.zeros((32, 128), F32)
    mine = []
    for at in range(3):
        part = slice(32 * at, 32 * at + 32)
        parts = jnp.concatenate([mass_z[part], slope_z[part], mass_z[96:128], none], axis=0)
        mix = flat_part("mix_minus" if at == 1 else "mix_plus")
        one = jnp.dot(mix, parts, precision=HIGHEST, preferred_element_type=F32)
        pmine[at] = one
        mine.append(one.reshape(3, 8, 128))
    dtile[...] = jnp.where(lane8 < 32, mine[0][1], pltpu.roll(mine[2][1], 32, 1))
    for tile, vertex, first in ((0, 0, 1), (1, 4, 0)):
        total = jnp.zeros((8, 128), F32)
        for c in range(3):
            for d in range(2):
                goal = 2 * c + d
                moved = pltpu.roll(mine[c][first + d], (goal - vertex) % 8, 0)
                total = jnp.where(sub8 == goal, moved, total)
        ptile[tile] = total
    send(SIDE, (-1, 0), pmine.at[pl.ds(0, 2)], px, 2)
    send(SIDE, (1, 0), pmine.at[pl.ds(1, 2)], px, 2)
    for pair in RIMS:
        send(RIMS, pair, ptile.at[0 if pair[1] < 0 else 1], pt, 3)
    for pair in WIDE:
        send(WIDE, pair, dtile, dr, 4)
    loads[4].wait()

    settle("side", xr1, 0, False)
    settle("rims", vr1, 1, False)
    unpack(field, 2, xr1, vr1)

    residual = fmask[...] * field[0]
    inv = fmask[...] / field[1]
    inverse[...] = inv
    field[0] = residual
    theta = 1.1
    delta = 0.9
    sigma = theta / delta
    rho0 = 1.0 / sigma
    rho1 = 1.0 / (2.0 * sigma - rho0)
    step_one = inv * residual / theta
    step[...] = step_one
    held[0] = fold(local_operator(step_one))
    pack(held, 1, xs2, vs2)
    exchange(xs2, vs2, xr2, vr2, 5)

    settle("side", px, 2, False)
    settle("rims", pt, 3, False)
    settle("wide", dr, 4, False)

    row_low = sub8 < 2
    row_mid = sub8 == 2

    def extend(own, received):
        moved = []
        for dx in (-2, -1, 0, 1, 2):
            mid = own if dx == 0 else received[WIDE.index((dx, 0))]
            below = received[WIDE.index((dx, -1))]
            above = received[WIDE.index((dx, 1))]
            rim = jnp.where(row_low, above, jnp.where(row_mid, 0.0, below))
            moved.append(pltpu.roll(mid, 1, 0) + pltpu.roll(rim, 5, 0))
        return [moved[v + 1] + pltpu.roll(moved[v], 96, 1) for v in range(4)]

    ext_diag = extend(dtile[...], dr)
    vertex_y = sub * 4 + sub8 - 1
    good_yz = (vertex_y > 0) & (vertex_y < 4 * n_sub) & (sub8 < 7) & (lane8 > 0) & (lane8 < 16)
    scales = []
    for v in range(4):
        vertex_x = dom + v - 1
        good = good_yz & (vertex_x > 0) & (vertex_x < n_dom)
        scales.append(jnp.where(good, (2.0 / 3.0) / jnp.where(good, ext_diag[v], 1.0), 0.0))

    def joined(dx, c):
        if dx == 0:
            base = pmine[c]
        else:
            base = px[SIDE.index((dx, 0)), c if dx > 0 else c - 1]
        base = base.reshape(3, 8, 128)
        below = pt[RIMS.index((dx, -1))]
        above = pt[RIMS.index((dx, 1))]
        out = []
        for d in range(3):
            total = base[d]
            if d < 2:
                moved = pltpu.roll(below, (-2 * c - d) % 8, 0)
                total = total + jnp.where(sub8 == 0, moved, 0.0)
            if d > 0:
                moved = pltpu.roll(above, (4 - 2 * c - (d - 1)) % 8, 0)
                total = total + jnp.where(sub8 == 4, moved, 0.0)
            out.append(total)
        return out

    cross = joined(0, 1)
    own_low = [a + b for a, b in zip(joined(0, 0), joined(-1, 2), strict=True)]
    own_high = [a + b for a, b in zip(joined(0, 2), joined(1, 0), strict=True)]
    for vx, blocks in enumerate(
        ((joined(-1, 1), own_low, cross), (cross, own_high, joined(1, 1)))
    ):
        for at in range(3):
            for d in range(3):
                stencil[vx * 9 + at * 3 + d] = blocks[at][d]
    for v in range(4):
        stencil[18 + v] = scales[v]

    settle("side", xr2, 5, False)
    settle("rims", vr2, 6, False)
    unpack(held, 1, xr2, vr2)
    residual = field[0]
    step_one = step[...]
    res_one = residual - fmask[...] * held[0]
    second = (1.0 + rho1 * rho0) * step_one + (2.0 * rho1 / delta) * inverse[...] * res_one
    step[...] = second

    defect = residual - fmult[...] * local_operator(second)
    part = dot(late_part("rest_xy"), jnp.concatenate(halves(defect), axis=1))
    part = part[0:16, :128] + part[0:16, 128:] + part[16:32, :128]
    coarse = times_right(halves(part), late_part("rest_z"))
    ctile[...] = jnp.where(lane8 < 32, coarse[0:8], coarse[8:16])
    for pair in sorted(WIDE, key=lambda p: -abs(p[0]) - abs(p[1])):
        send(WIDE, pair, ctile, cr, 7)

    settle("side", xr1, 0, True)
    settle("rims", vr1, 1, True)
    settle("side", px, 2, True)
    settle("rims", pt, 3, True)
    settle("wide", dr, 4, True)
    settle("side", xr2, 5, True)
    settle("rims", vr2, 6, True)
    settle("wide", cr, 7, False)

    ext_rhs = extend(ctile[...], cr)
    scales = [stencil[18 + v] for v in range(4)]
    ones = [scales[v] * ext_rhs[v] for v in range(4)]
    packed = [c + pltpu.roll(c, 31, 1) + pltpu.roll(c, 65, 1) for c in ones]
    around = [[c, pltpu.roll(c, 7, 0), pltpu.roll(c, 6, 0)] for c in packed]
    results = []
    for vx in range(2):
        total = jnp.zeros((8, 128), F32)
        for at in range(3):
            for d in range(3):
                total = total + stencil[vx * 9 + at * 3 + d] * around[vx + at][d]
        image = total + pltpu.roll(total, 96, 1) + pltpu.roll(total, 64, 1)
        one = pltpu.roll(ones[vx + 1], 7, 0)
        scale = pltpu.roll(scales[vx + 1], 7, 0)
        right = pltpu.roll(ext_rhs[vx + 1], 7, 0)
        results.append(one + scale * (right - image))
    pair = halves(jnp.concatenate(results, axis=0))
    nodes = halves(times_right(pair, late_part("prol_z")))
    nodes = jnp.concatenate([nodes[0], nodes[0], nodes[1], nodes[1]], axis=0)
    fine = step[...] + fmask[...] * dot(late_part("prol_xy")[:, 0:64], nodes)
    fine = fine.reshape(4, 8, 8, 128)
    for j in range(4):
        out_ref[:, 8 * j : 8 * j + 8, :] = fine[j]
    copies = halves(dot(jnp.concatenate(pair, axis=1), late_part("copy_z")[:, 0:128]))
    copies = jnp.concatenate([copies[0], copies[0], copies[1], copies[1]], axis=0)
    copies = dot(late_part("copy_y")[:, 0:64], copies)
    coarse_ref[...] = copies.reshape(2, 8, 128)[:, :, 0:32]

    settle("wide", cr, 7, True)


def finish(fine, coarse, fine_out, coarse_out, sem):
    one = pltpu.make_async_copy(fine, fine_out, sem.at[0])
    two = pltpu.make_async_copy(coarse, coarse_out, sem.at[1])
    one.start()
    two.start()
    one.wait()
    two.wait()


def solution(mesh):
    n_dom = mesh.shape["dom"]
    n_sub = mesh.shape["sub"]

    def shards(rhs_local, coefficient):
        (early_at, early), (late_at, late), (flat_at, flat) = constants(4, 16)
        any_space = pl.BlockSpec(memory_space=pl.ANY)
        vmem = pl.BlockSpec(memory_space=pltpu.VMEM)
        outs = (
            jax.ShapeDtypeStruct((8, 32, 128), F32),
            jax.ShapeDtypeStruct((2, 8, 32), F32),
        )

        def space(*shape):
            return pltpu.VMEM(shape, F32)

        dma = pltpu.SemaphoreType.DMA
        operands = [
            pltpu.with_memory_space_constraint(v, pltpu.HBM)
            for v in (coefficient, rhs_local, early, late, flat)
        ]
        fine, coarse = pl.pallas_call(
            functools.partial(kernel, (early_at, late_at, flat_at), n_dom, n_sub),
            out_shape=outs,
            in_specs=[any_space] * 5,
            out_specs=(vmem, vmem),
            scratch_shapes=[
                space(8, 32, 128),
                space(8, 32, 128),
                pltpu.VMEM(early.shape, BF16),
                pltpu.VMEM(late.shape, BF16),
                pltpu.VMEM(flat.shape, F32),
                space(256, 128),
                space(2, 256, 128),
                space(1, 256, 128),
                space(256, 128),
                space(256, 128),
                space(256, 128),
                space(256, 128),
                space(3, 24, 128),
                space(2, 8, 128),
                space(8, 128),
                space(8, 128),
                space(22, 8, 128),
                space(2, 2, 32, 128),
                space(6, 2, 8, 128),
                space(2, 1, 32, 128),
                space(6, 1, 8, 128),
                space(2, 2, 32, 128),
                space(6, 2, 8, 128),
                space(2, 1, 32, 128),
                space(6, 1, 8, 128),
                space(2, 2, 24, 128),
                space(6, 8, 128),
                space(14, 8, 128),
                space(14, 8, 128),
                dma((5,)),
                dma((8,)),
                dma((8,)),
            ],
            compiler_params=pltpu.CompilerParams(
                collective_id=0, has_side_effects=True, vmem_limit_bytes=8 * 2**20
            ),
        )(*operands)
        return pl.pallas_call(
            finish,
            out_shape=outs,
            in_specs=[vmem, vmem],
            out_specs=(any_space, any_space),
            scratch_shapes=[dma((2,))],
            compiler_params=pltpu.CompilerParams(vmem_limit_bytes=2**20),
        )(fine, coarse)

    return jax.shard_map(
        shards,
        mesh=mesh,
        in_specs=(P("dom", "sub", None), P("dom", "sub", None)),
        out_specs=(P("dom", "sub", None), P("dom", "sub", None)),
        check_vma=False,
    )
```

```python
import functools

import jax
import jax.numpy as jnp
import numpy as np
from jax import lax
from jax.experimental import pallas as pl
from jax.experimental.pallas import tpu as pltpu
from jax.sharding import PartitionSpec as P

MESH = pl.DeviceIdType.MESH
HIGHEST = lax.Precision.HIGHEST
F32 = jnp.float32
BF16 = jnp.bfloat16

NEAR = [(dx, dy) for dx in (-1, 0, 1) for dy in (-1, 0, 1) if (dx, dy) != (0, 0)]
WIDE = [(dx, dy) for dx in (-2, -1, 0, 1, 2) for dy in (-1, 0, 1) if (dx, dy) != (0, 0)]
REACH = [(dx, dy) for dx in range(-3, 4) for dy in (-1, 0, 1) if (dx, dy) != (0, 0)]
SIDE = [pair for pair in NEAR if pair[1] == 0]
RIMS = [pair for pair in NEAR if pair[1] != 0]
EDGE = [pair for pair in RIMS if pair[0] != 0]
ROWS = [pair for pair in RIMS if pair[0] == 0]


def opposite(table, pair):
    return table.index((-pair[0], -pair[1]))


def tables():
    degree = 7
    points = np.array(
        [
            -1.0,
            -0.8717401485096066,
            -0.5917001814331423,
            -0.2092992179024789,
            0.2092992179024789,
            0.5917001814331423,
            0.8717401485096066,
            1.0,
        ]
    )
    previous = np.ones(points.shape)
    values = points.copy()
    for level in range(1, degree):
        following = ((2 * level + 1) * points * values - level * previous) / (level + 1)
        previous = values
        values = following
    weights = 2.0 / (degree * (degree + 1) * values**2)
    derivative = np.zeros((8, 8))
    for row_at in range(8):
        for col_at in range(8):
            if row_at != col_at:
                derivative[row_at, col_at] = values[row_at] / (
                    values[col_at] * (points[row_at] - points[col_at])
                )
    derivative[0, 0] = -degree * (degree + 1) / 4.0
    derivative[7, 7] = degree * (degree + 1) / 4.0
    interp = np.stack([(1.0 - points) / 2.0, (1.0 + points) / 2.0], axis=1)
    return derivative, weights, interp


DER, WTS, INT = tables()
TWICE = np.array([2.0, 1.0, 1.0, 1.0, 1.0, 1.0, 1.0, 2.0])
HATS = [TWICE * INT[:, 0], TWICE * INT[:, 1]]


def face_moments(face):
    near = 0 if face == 0 else 1
    return [DER[:, face] * (DER @ HATS[i]) for i in (near, 1 - near)]
MASS = [INT[:, 0] * INT[:, 0], INT[:, 0] * INT[:, 1], INT[:, 1] * INT[:, 1]]


def moment_maps(elements, order, slope):
    maps = np.zeros((len(order), elements + 1, 8 * elements))
    for at, offset in enumerate(order):
        for e in range(elements):
            nodes = slice(8 * e, 8 * e + 8)
            if offset == 0:
                maps[at, e, nodes] += 0.25 if slope else MASS[0]
                maps[at, e + 1, nodes] += 0.25 if slope else MASS[2]
            elif offset == 1:
                maps[at, e, nodes] += -0.25 if slope else MASS[1]
            else:
                maps[at, e + 1, nodes] += -0.25 if slope else MASS[1]
    return maps


def unique_interp(elements):
    maps = np.zeros((8 * elements, elements + 1))
    for e in range(elements):
        maps[8 * e : 8 * e + 8, e] = INT[:, 0]
        maps[8 * e : 8 * e + 8, e + 1] = INT[:, 1]
    return maps


def unique_copies(elements):
    maps = np.zeros((2 * elements, elements + 1))
    for e in range(elements):
        maps[2 * e, e] = 1.0
        maps[2 * e + 1, e + 1] = 1.0
    return maps


def split(matrix):
    high = jnp.asarray(matrix, F32).astype(BF16)
    return high, (jnp.asarray(matrix, F32) - high.astype(F32)).astype(BF16)


def right_halves(matrix):
    high, low = split(matrix)
    top = jnp.concatenate([high, low], axis=1)
    return jnp.concatenate([top, jnp.concatenate([high, jnp.zeros_like(low)], axis=1)], axis=0)


def left_halves(matrix):
    high, low = split(matrix)
    return jnp.concatenate([high, low, high], axis=1)


def wide(block):
    return jnp.pad(block, ((0, 0), (0, 256 - block.shape[1])))


def spots_of(parts):
    spots = {}
    at = 0
    for name, block in parts.items():
        spots[name] = (at, block.shape[0])
        at += block.shape[0]
    return spots, jnp.concatenate(list(parts.values()))


def constants(ey, ez):
    square = DER * DER
    eye8 = np.eye(8)
    eye = np.eye(ez)
    early = {
        "square_z": right_halves(np.kron(eye, square)),
        "square_xy": wide(left_halves(np.kron(square.T, eye8) + np.kron(eye8, square.T))),
    }
    low = unique_interp(ey)
    place = np.zeros((4, 8, 8, 16))
    for side in range(2):
        place[..., 8 * side : 8 * side + ey + 1] = (
            INT[:, side][None, :, None, None] * low.reshape(ey, 8, ey + 1)[:, None]
        )
    place = place.reshape(256, 16)
    rest_z = np.zeros((128, 128))
    rest_z[:, : ez + 1] = unique_interp(ez)
    for at in (32, 64, 96):
        rest_z[:, at : at + ez + 1] = unique_interp(ez)
    prol_z = np.zeros((128, 128))
    prol_z[: ez + 1, :] = unique_interp(ez).T
    copy_z = np.zeros((128, 128))
    copy_z[: ez + 1, : 2 * ez] = unique_copies(ez).T
    copy_y = np.zeros((16, 16))
    for side in range(2):
        copy_y[8 * side : 8 * side + 8, 8 * side : 8 * side + ey + 1] = unique_copies(ey)
    own = np.zeros((32, 256))
    for side in range(2):
        own[8 * (side + 1) + 1 : 8 * (side + 1) + 2 + ey] = place.T[8 * side : 8 * side + ey + 1]
    rest_xy = split(own)
    spill = np.zeros((4, 8, 256))
    low_m = low * np.tile(TWICE, ey)[:, None]
    for side in range(2):
        for at, v in ((0, 1 + side), (64, 3 * side)):
            spill[v, 1 : ey + 2, at + 32 * side : at + 32 * side + 32] = low_m.T
        for at, r in ((128, 1 + ey * side), (144, (ey + 2) * side)):
            for vx in range(2):
                spill[1 + vx, r, at + 8 * side : at + 8 * side + 8] = HATS[vx]
    for at, (dx, dy) in enumerate(EDGE):
        near_v, far_v = (1, 0) if dx < 0 else (2, 3)
        near_r, far_r = (1, 0) if dy < 0 else (1 + ey, 2 + ey)
        spill[near_v, near_r, 160 + at] = 1.0
        spill[far_v, near_r, 168 + at] = 1.0
        spill[near_v, far_r, 176 + at] = 1.0
    spill = split(spill.reshape(32, 256))
    rest_z = np.zeros((128, 128))
    rest_z[:, : ez + 1] = unique_interp(ez)
    for at in (32, 64, 96):
        rest_z[:, at : at + ez + 1] = unique_interp(ez)
    prol_z = np.zeros((128, 128))
    prol_z[: ez + 1, :] = unique_interp(ez).T
    copy_z = np.zeros((128, 128))
    copy_z[: ez + 1, : 2 * ez] = unique_copies(ez).T
    copy_y = np.zeros((16, 16))
    for side in range(2):
        copy_y[8 * side : 8 * side + 8, 8 * side : 8 * side + ey + 1] = unique_copies(ey)
    own = np.zeros((32, 256))
    for side in range(2):
        own[8 * (side + 1) + 1 : 8 * (side + 1) + 2 + ey] = place.T[8 * side : 8 * side + ey + 1]
    rest_xy = split(own)
    spill = np.zeros((4, 8, 256))
    low_m = low * np.tile(TWICE, ey)[:, None]
    for side in range(2):
        for at, v in ((0, 1 + side), (64, 3 * side)):
            spill[v, 1 : ey + 2, at + 32 * side : at + 32 * side + 32] = low_m.T
        for at, r in ((128, 1 + ey * side), (144, (ey + 2) * side)):
            for vx in range(2):
                spill[1 + vx, r, at + 8 * side : at + 8 * side + 8] = HATS[vx]
    for at, (dx, dy) in enumerate(EDGE):
        near_v, far_v = (1, 0) if dx < 0 else (2, 3)
        near_r, far_r = (1, 0) if dy < 0 else (1 + ey, 2 + ey)
        spill[near_v, near_r, 160 + at] = 1.0
        spill[far_v, near_r, 168 + at] = 1.0
        spill[near_v, far_r, 176 + at] = 1.0
    spill = split(spill.reshape(32, 256))
    moment_y = np.zeros((2, 2, 8, 8, 8))
    for side in range(2):
        for at, one in enumerate(face_moments(7 * side)):
            moment_y[side, at] = np.eye(8)[:, :, None] * one[None, None, :]
    moment_y = moment_y.reshape(32, 64)
    late = {
        "grad_z": right_halves(np.kron(eye, DER.T)),
        "back_z": right_halves(np.kron(eye, DER)),
        "rest_z": right_halves(rest_z),
        "prol_z": right_halves(prol_z),
        "copy_z": wide(jnp.concatenate([split(copy_z)[0]] * 2)),
        "prol_xy": wide(left_halves(place)),
        "grad_xy": wide(
            jnp.concatenate([left_halves(np.kron(DER, eye8)), left_halves(np.kron(eye8, DER))])
        ),
        "back_y": wide(left_halves(np.kron(eye8, DER.T))),
        "rest_xy": jnp.concatenate([rest_xy[0], rest_xy[1]]),
        "spill": jnp.concatenate([spill[0], spill[1]]),
        "copy_y": wide(left_halves(copy_y)),
    }
    flat = {}
    for name, slope in (("moment_m", False), ("moment_s", True)):
        block = np.zeros((128, 128))
        for at, one in enumerate(moment_maps(ez, (0, 1, -1), slope)):
            block[:, 32 * at : 32 * at + ez + 1] = one.T
        flat[name] = jnp.asarray(block, F32)
    order_y = (-1, 0, 1)
    mass_y = np.zeros((3, 8, 8 * ey))
    mass_y[:, : ey + 1] = moment_maps(ey, order_y, False)
    slope_y = np.zeros((3, 8, 8 * ey))
    slope_y[:, : ey + 1] = moment_maps(ey, order_y, True)
    mass_y = mass_y.reshape(24, 8 * ey)
    slope_y = slope_y.reshape(24, 8 * ey)
    for name, sign in (("mix_plus", 0.25), ("mix_minus", -0.25)):
        block = np.zeros((24, 128))
        block[:, : 24 * ey] = np.concatenate([slope_y, mass_y, sign * mass_y], axis=1)
        flat[name] = jnp.asarray(block, F32)
    return spots_of(early), spots_of(late), spots_of(flat)


def kernel(
    tables_at, n_dom, n_sub, coef_hbm, rhs_hbm, early_hbm, late_hbm, flat_hbm,
    out_ref, coarse_ref,
    coef, rhs, early, late, flat, weighted, field, held, fmask, fmult, inverse, step,
    pmine, ptile, dtile, ctile, stencil, gfield, fside, frow, fedge,
    xs1, vs1, xs2, vs2,
    xr1, vr1, xr2, vr2, px, pt, dr, cr, fx, fy, fe,
    load_sem, s_sem, r_sem,
):
    early_at, late_at, flat_at = tables_at
    dom = lax.axis_index("dom")
    sub = lax.axis_index("sub")

    loads = []
    for at, (source, dest) in enumerate(
        ((coef_hbm, coef), (early_hbm, early), (rhs_hbm, rhs), (flat_hbm, flat), (late_hbm, late))
    ):
        load = pltpu.make_async_copy(source, dest, load_sem.at[at])
        load.start()
        loads.append(load)

    def present(pair):
        dx, dy = pair
        conds = []
        if dx < 0:
            conds.append(dom >= -dx)
        if dx > 0:
            conds.append(dom < n_dom - dx)
        if dy < 0:
            conds.append(sub >= 1)
        if dy > 0:
            conds.append(sub < n_sub - 1)
        return functools.reduce(jnp.logical_and, conds)

    def target(pair):
        return (dom + pair[0], sub + pair[1])

    for buffer in (xr1, vr1, xr2, vr2, px, pt, dr, cr, fx, fy, fe):
        buffer[...] = jnp.zeros_like(buffer)

    barrier = pltpu.get_barrier_semaphore()
    for pair in sorted(REACH, key=lambda p: abs(p[0]) + abs(p[1])):

        @pl.when(present(pair))
        def _(pair=pair):
            pl.semaphore_signal(barrier, inc=1, device_id=target(pair), device_id_type=MESH)

    near_x = jnp.where(dom >= 1, 1, 0) + jnp.where(dom < n_dom - 1, 1, 0)
    near_y = jnp.where(sub >= 1, 1, 0) + jnp.where(sub < n_sub - 1, 1, 0)
    far_x = near_x + jnp.where(dom >= 2, 1, 0) + jnp.where(dom < n_dom - 2, 1, 0)
    n_side = near_x
    n_rims = near_y * (1 + near_x)
    n_wide = (1 + far_x) * (1 + near_y) - 1
    reach_x = far_x + jnp.where(dom >= 3, 1, 0) + jnp.where(dom < n_dom - 3, 1, 0)
    n_reach = (1 + reach_x) * (1 + near_y) - 1

    row = lax.broadcasted_iota(jnp.int32, (256, 128), 0)
    lane = lax.broadcasted_iota(jnp.int32, (256, 128), 1)
    x_at = lax.shift_right_logical(row, 3) & 7
    b_at = row & 7
    c_at = lane & 7
    place_x = dom * 8 + x_at
    place_y = sub * 32 + lax.shift_right_logical(row, 6) * 8 + b_at
    inside = (
        (place_x > 0) & (place_x < 8 * n_dom - 1)
        & (place_y > 0) & (place_y < 32 * n_sub - 1)
        & (lane > 0) & (lane < 127)
    )
    mask = jnp.where(inside, 1.0, 0.0)
    fmask[...] = mask
    twice = jnp.where((x_at == 0) | (x_at == 7), 2.0, 1.0)
    twice = twice * jnp.where((b_at == 0) | (b_at == 7), 2.0, 1.0)
    fmult[...] = mask * twice * jnp.where((c_at == 0) | (c_at == 7), 2.0, 1.0)

    lane8 = lax.broadcasted_iota(jnp.int32, (8, 128), 1)
    sub8 = lax.broadcasted_iota(jnp.int32, (8, 128), 0)
    z_low = ((lane8 & 7) == 0) & (lane8 > 0)
    z_high = ((lane8 & 7) == 7) & (lane8 < 127)

    def weights_along(spot):
        value = jnp.where((spot == 0) | (spot == 7), float(WTS[0]), float(WTS[1]))
        value = jnp.where((spot == 2) | (spot == 5), float(WTS[2]), value)
        return jnp.where((spot == 3) | (spot == 4), float(WTS[3]), value)

    def fold(v):
        v = v.reshape(32, 8, 128)
        v = v + jnp.where(
            z_high[None], pltpu.roll(v, 127, 2),
            jnp.where(z_low[None], pltpu.roll(v, 1, 2), 0.0),
        )
        up = pltpu.roll(v, 1, 1)
        down = pltpu.roll(v, 7, 1)
        none = jnp.zeros((8, 8, 128), F32)
        up = jnp.concatenate([none, up[:24]], axis=0)
        down = jnp.concatenate([down[8:], none], axis=0)
        v = v + jnp.where((sub8 == 0)[None], up, jnp.where((sub8 == 7)[None], down, 0.0))
        return v.reshape(256, 128)

    def halves(v):
        high = v.astype(BF16)
        return high, (v - high.astype(F32)).astype(BF16)

    def dot(left, right):
        return jnp.dot(left, right, preferred_element_type=F32)

    def early_part(name):
        start, count = early_at[name]
        return early[start : start + count, :]

    def late_part(name):
        start, count = late_at[name]
        return late[start : start + count, :]

    def flat_part(name):
        start, count = flat_at[name]
        return flat[start : start + count, :]

    def times_right(pair, matrix):
        both = dot(jnp.concatenate(pair, axis=1), matrix)
        return both[:, :128] + both[:, 128:]

    def stacked(pair):
        high, low = [
            jnp.concatenate([v[at : at + 64] for at in range(0, v.shape[0], 64)], axis=1) for v in pair
        ]
        return jnp.concatenate([high, high, low], axis=0)

    def rows_of(v):
        return jnp.concatenate([v[:, at : at + 128] for at in range(0, v.shape[1], 128)], axis=0)

    def back_x(v):
        v = v.reshape(4, 8, 8, 128)
        matrix = DER.T
        even = [v[:, b] + v[:, 7 - b] for b in range(4)]
        odd = [v[:, b] - v[:, 7 - b] for b in range(4)]
        planes = [None] * 8
        for a in range(4):
            p = sum(float(matrix[a, b] + matrix[a, 7 - b]) / 2 * even[b] for b in range(4))
            q = sum(float(matrix[a, b] - matrix[a, 7 - b]) / 2 * odd[b] for b in range(4))
            planes[a] = p + q
            planes[7 - a] = q - p
        return jnp.stack(planes, axis=1).reshape(256, 128)

    def with_faces(u, faces, w_rows, w_z):
        w = weighted[...]
        pair = halves(jnp.concatenate([u, faces], axis=0))
        both = dot(late_part("grad_xy")[:, 0:192], stacked(pair))
        all_z = times_right(pair, late_part("grad_z"))
        all_y = rows_of(both[64:128])
        flux_z = halves(jnp.concatenate([w * all_z[0:256], w_z * all_z[256:384]], axis=0))
        flux_y = halves(jnp.concatenate([w * all_y[0:256], w_rows * all_y[256:384]], axis=0))
        back = rows_of(dot(late_part("back_y")[:, 0:192], stacked(flux_y)))
        back = back + times_right(flux_z, late_part("back_z"))
        return back[0:256] + back_x(w * rows_of(both[0:64, 0:512])), back[256:384]

    def local_operator(u):
        w = weighted[...]
        pair = halves(u)
        both = dot(late_part("grad_xy")[:, 0:192], stacked(pair))
        flux_z = halves(w * times_right(pair, late_part("grad_z")))
        flux_y = halves(w * rows_of(both[64:128]))
        back = rows_of(dot(late_part("back_y")[:, 0:192], stacked(flux_y)))
        back = back + times_right(flux_z, late_part("back_z"))
        return back + back_x(w * rows_of(both[0:64]))

    def send(table, pair, source, landing, group):
        at = table.index((-pair[0], -pair[1]))

        @pl.when(present(pair))
        def _():
            pltpu.make_async_remote_copy(
                src_ref=source,
                dst_ref=landing.at[at],
                send_sem=s_sem.at[group],
                recv_sem=r_sem.at[group],
                device_id=target(pair),
                device_id_type=MESH,
            ).start()

    counts = {"side": (n_side, (1, 2)), "rows": (near_y, (1, 2)), "edge": (near_x * near_y, (1, 2, 4)), "rims": (n_rims, (1, 2, 3, 4, 6)), "wide": (n_wide, (1, 2, 3, 5, 7, 8, 9, 11, 14)), "reach": (n_reach, (7, 9, 11, 13, 14, 17, 20))}

    def settle(kind, landing, group, sent):
        count, options = counts[kind]
        for one in options:

            @pl.when(count == one)
            def _(one=one):
                copy = pltpu.make_async_remote_copy(
                    src_ref=landing.at[pl.ds(0, one)],
                    dst_ref=landing.at[pl.ds(0, one)],
                    send_sem=s_sem.at[group],
                    recv_sem=r_sem.at[group],
                    device_id=(dom, sub),
                    device_id_type=MESH,
                )
                if sent:
                    copy.wait_send()
                else:
                    copy.wait_recv()

    def pack(refs, fields, xs, vs):
        for f in range(fields):
            ref = refs.at[f]
            faces = {-1: ref[pl.ds(0, 8, stride=8), :], 1: ref[pl.ds(199, 8, stride=8), :]}
            for j in range(4):
                xs[0, f, 8 * j : 8 * j + 8] = ref[64 * j : 64 * j + 8, :]
                xs[1, f, 8 * j : 8 * j + 8] = ref[64 * j + 56 : 64 * j + 64, :]
            for at, (dx, dy) in enumerate(RIMS):
                face = faces[dy]
                if dx < 0:
                    face = jnp.where(sub8 == 7, pltpu.roll(face, 7, 0), 0.0)
                if dx > 0:
                    face = jnp.where(sub8 == 0, pltpu.roll(face, 1, 0), 0.0)
                vs[at, f] = face

    def exchange(xs, vs, xr, vr, group):
        for pair in RIMS:
            if pair[0] != 0:
                send(RIMS, pair, vs.at[RIMS.index(pair)], vr, group + 1)
        for pair in SIDE:
            send(SIDE, pair, xs.at[SIDE.index(pair)], xr, group)
        for pair in RIMS:
            if pair[0] == 0:
                send(RIMS, pair, vs.at[RIMS.index(pair)], vr, group + 1)

    def unpack(refs, fields, xr, vr):
        for f in range(fields):
            ref = refs.at[f]
            for j in range(4):
                ref[64 * j : 64 * j + 8, :] += xr[0, f, 8 * j : 8 * j + 8]
                ref[64 * j + 56 : 64 * j + 64, :] += xr[1, f, 8 * j : 8 * j + 8]
            for dy, start in ((-1, 0), (1, 199)):
                a, b, c = [vr[RIMS.index((dx, dy)), f] for dx in (-1, 0, 1)]
                ref[pl.ds(start, 8, stride=8), :] += a + b + c

    def in_order(ref):
        v = ref[...].reshape(8, 4, 8, 128)
        return jnp.concatenate([v[:, j] for j in range(4)], axis=0).reshape(256, 128)

    table = weights_along(x_at) * weights_along(b_at) * weights_along(c_at)
    loads[0].wait()
    w = in_order(coef) * table
    weighted[...] = w
    loads[1].wait()
    loads[2].wait()
    field[0] = fold(in_order(rhs))
    w4 = w.reshape(4, 8, 8, 128)
    planes = [w4[:, a].reshape(32, 128) for a in range(8)]
    for side in range(2):
        one, two = face_moments(7 * side)
        rows = [weighted[pl.ds(192 * side + b, 8, stride=8), :] for b in range(8)]
        fside[side, 0:32] = sum(float(one[a]) * planes[a] for a in range(8))
        fside[side, 32:64] = sum(float(two[a]) * planes[a] for a in range(8))
        fside[side, 64:96] = planes[7 * side]
        frow[side, 0] = sum(float(one[b]) * rows[b] for b in range(8))
        frow[side, 1] = sum(float(two[b]) * rows[b] for b in range(8))
        frow[side, 2] = rows[7 * side]
    fedge[...] = jnp.zeros_like(fedge)
    for at, (dx, dy) in enumerate(EDGE):
        x_side, y_side = (dx + 1) // 2, (dy + 1) // 2
        spot, line = 31 * y_side, 7 * x_side
        fedge[at, 0:1] = 2.0 * (fside[x_side, spot : spot + 1] + frow[y_side, 0, line : line + 1])
        fedge[at, 1:2] = 2.0 * fside[x_side, 32 + spot : 33 + spot]
        fedge[at, 2:3] = 2.0 * frow[y_side, 1, line : line + 1]
        fedge[at, 3:4] = 4.0 * frow[y_side, 2, line : line + 1]
    pair = halves(w)
    diagonal = rows_of(dot(early_part("square_xy")[:, 0:192], stacked(pair)))
    field[1] = fold(diagonal + times_right(pair, early_part("square_z")))
    pack(field, 2, xs1, vs1)

    pl.semaphore_wait(barrier, n_reach)
    exchange(xs1, vs1, xr1, vr1, 0)
    for at, pair in enumerate(SIDE):
        send(SIDE, pair, fside.at[at], fx, 2)
    for at, pair in enumerate(ROWS):
        send(ROWS, pair, frow.at[at], fy, 3)
    for at, pair in enumerate(EDGE):
        send(EDGE, pair, fedge.at[at], fe, 4)

    loads[3].wait()
    w4 = weighted[...].reshape(4, 8, 8, 128)
    planes = [w4[:, a].reshape(32, 128) for a in range(8)]
    moments = [sum(float(m[a]) * planes[a] for a in range(8) if m[a] != 0.0) for m in MASS]
    moments.append(moments[0] + 2.0 * moments[1] + moments[2])
    stack = jnp.concatenate(moments, axis=0)
    mass_z = jnp.dot(stack, flat_part("moment_m"), precision=HIGHEST, preferred_element_type=F32)
    slope_z = jnp.dot(stack, flat_part("moment_s"), precision=HIGHEST, preferred_element_type=F32)
    none = jnp.zeros((32, 128), F32)
    mine = []
    for at in range(3):
        part = slice(32 * at, 32 * at + 32)
        parts = jnp.concatenate([mass_z[part], slope_z[part], mass_z[96:128], none], axis=0)
        mix = flat_part("mix_minus" if at == 1 else "mix_plus")
        one = jnp.dot(mix, parts, precision=HIGHEST, preferred_element_type=F32)
        pmine[at] = one
        mine.append(one.reshape(3, 8, 128))
    dtile[...] = jnp.where(lane8 < 32, mine[0][1], pltpu.roll(mine[2][1], 32, 1))
    for side, vertex, first in ((0, 0, 1), (1, 4, 0)):
        total = jnp.zeros((8, 128), F32)
        for c in range(3):
            for d in range(2):
                goal = 2 * c + d
                moved = pltpu.roll(mine[c][first + d], (goal - vertex) % 8, 0)
                total = jnp.where(sub8 == goal, moved, total)
        ptile[side] = total
    send(SIDE, (-1, 0), pmine.at[pl.ds(0, 2)], px, 5)
    send(SIDE, (1, 0), pmine.at[pl.ds(1, 2)], px, 5)
    for pair in RIMS:
        send(RIMS, pair, ptile.at[(pair[1] + 1) // 2], pt, 6)
    for pair in WIDE:
        send(WIDE, pair, dtile, dr, 7)
    loads[4].wait()

    settle("side", xr1, 0, False)
    settle("rims", vr1, 1, False)
    unpack(field, 2, xr1, vr1)

    residual = fmask[...] * field[0]
    inv = fmask[...] / field[1]
    inverse[...] = inv
    field[0] = residual
    theta = 1.1
    delta = 0.9
    sigma = theta / delta
    rho0 = 1.0 / sigma
    rho1 = 1.0 / (2.0 * sigma - rho0)
    step_one = inv * residual / theta
    step[...] = step_one
    held[0] = fold(local_operator(step_one))
    pack(held, 1, xs2, vs2)
    exchange(xs2, vs2, xr2, vr2, 8)

    factor = 2.0 * rho1 / delta
    g = factor * inverse[...] * held[0]
    gfield[...] = g
    start = (1.0 + rho1 * rho0) * step_one + factor * inv * residual
    step[...] = start
    settle("side", fx, 2, False)
    settle("rows", fy, 3, False)
    settle("edge", fe, 4, False)
    faces = []
    for first in (0, 56):
        for j in range(4):
            faces.append(g[64 * j + first : 64 * j + first + 8])
    rims = [gfield[pl.ds(0, 8, stride=8), :], gfield[pl.ds(199, 8, stride=8), :]]
    corner = jnp.zeros((8, 128), F32)
    lines = [jnp.zeros((8, 128), F32) for _ in range(4)]
    for at, (dx, dy) in enumerate(EDGE):
        line = 0 if dx < 0 else 7
        moved = pltpu.roll(rims[(dy + 1) // 2], (at - line) % 8, 0)
        corner = jnp.where(sub8 == at, moved, corner)
        given = fe[at]
        for k in range(4):
            lines[k] = jnp.where(sub8 == at, pltpu.roll(given, (at - k) % 8, 0), lines[k])
    none40 = jnp.zeros((40, 128), F32)
    faces = jnp.concatenate(faces + rims + [corner, none40], axis=0)
    two = [2.0 * fx[0, 64:96], 2.0 * fx[1, 64:96], 2.0 * fy[0, 2], 2.0 * fy[1, 2]]
    w_rows = jnp.concatenate(two + [jnp.zeros((48, 128), F32)], axis=0)
    w_z = jnp.concatenate(two + [lines[3], none40], axis=0)
    image, face_image = with_faces(start - g, faces, w_rows, w_z)
    defect = residual - fmult[...] * image
    near_w = [fx[0, 0:32], fx[1, 0:32], fy[0, 0], fy[1, 0], lines[0]]
    far_w = [fx[0, 32:64], fx[1, 32:64], fy[0, 1], fy[1, 1]]
    near = jnp.concatenate(near_w, axis=0) * faces[0:88] + face_image[0:88]
    far = jnp.concatenate(far_w, axis=0) * faces[0:80]
    parts = [
        near[0:64], far[0:64], near[64:80], far[64:80], near[80:88],
        lines[1] * corner, lines[2] * corner, jnp.zeros((72, 128), F32),
    ]
    twice_z = jnp.where(((lane8 & 7) == 0) | ((lane8 & 7) == 7), 2.0, 1.0)
    parts = jnp.concatenate(parts, axis=0).reshape(32, 8, 128) * twice_z[None]
    part = dot(late_part("rest_xy"), jnp.concatenate(halves(defect), axis=1))
    part = part + dot(late_part("spill"), jnp.concatenate(halves(parts.reshape(256, 128)), axis=1))
    part = part[0:32, :128] + part[0:32, 128:] + part[32:64, :128]
    coarse = times_right(halves(part), late_part("rest_z"))
    tile = jnp.where(lane8 < 64, jnp.where(lane8 < 32, coarse[0:8], coarse[8:16]), jnp.where(lane8 < 96, coarse[16:24], coarse[24:32]))
    ctile[...] = tile
    for pair in sorted(REACH, key=lambda p: -abs(p[0]) - abs(p[1])):
        send(REACH, pair, ctile, cr, 10)

    settle("side", px, 5, False)
    settle("rims", pt, 6, False)
    settle("wide", dr, 7, False)
    row_low = sub8 < 2
    row_mid = sub8 == 2

    def extend(own, received):
        moved = []
        for dx in (-2, -1, 0, 1, 2):
            mid = own if dx == 0 else received[WIDE.index((dx, 0))]
            below = received[WIDE.index((dx, -1))]
            above = received[WIDE.index((dx, 1))]
            rim = jnp.where(row_low, above, jnp.where(row_mid, 0.0, below))
            moved.append(pltpu.roll(mid, 1, 0) + pltpu.roll(rim, 5, 0))
        return [moved[v + 1] + pltpu.roll(moved[v], 96, 1) for v in range(4)]

    ext_diag = extend(dtile[...], dr)
    vertex_y = sub * 4 + sub8 - 1
    good_yz = (vertex_y > 0) & (vertex_y < 4 * n_sub) & (sub8 < 7) & (lane8 > 0) & (lane8 < 16)
    scales = []
    for v in range(4):
        vertex_x = dom + v - 1
        good = good_yz & (vertex_x > 0) & (vertex_x < n_dom)
        scales.append(jnp.where(good, (2.0 / 3.0) / jnp.where(good, ext_diag[v], 1.0), 0.0))

    def joined(dx, c):
        if dx == 0:
            base = pmine[c]
        else:
            base = px[SIDE.index((dx, 0)), c if dx > 0 else c - 1]
        base = base.reshape(3, 8, 128)
        below = pt[RIMS.index((dx, -1))]
        above = pt[RIMS.index((dx, 1))]
        out = []
        for d in range(3):
            total = base[d]
            if d < 2:
                moved = pltpu.roll(below, (-2 * c - d) % 8, 0)
                total = total + jnp.where(sub8 == 0, moved, 0.0)
            if d > 0:
                moved = pltpu.roll(above, (4 - 2 * c - (d - 1)) % 8, 0)
                total = total + jnp.where(sub8 == 4, moved, 0.0)
            out.append(total)
        return out

    cross = joined(0, 1)
    own_low = [a + b for a, b in zip(joined(0, 0), joined(-1, 2), strict=True)]
    own_high = [a + b for a, b in zip(joined(0, 2), joined(1, 0), strict=True)]
    for vx, blocks in enumerate(
        ((joined(-1, 1), own_low, cross), (cross, own_high, joined(1, 1)))
    ):
        for at in range(3):
            for d in range(3):
                stencil[vx * 9 + at * 3 + d] = blocks[at][d]
    for v in range(4):
        stencil[18 + v] = scales[v]

    settle("side", xr2, 8, False)
    settle("rims", vr2, 9, False)
    unpack(held, 1, xr2, vr2)
    step[...] = step[...] - factor * inverse[...] * held[0]

    settle("side", xr1, 0, True)
    settle("rims", vr1, 1, True)
    settle("side", fx, 2, True)
    settle("rows", fy, 3, True)
    settle("edge", fe, 4, True)
    settle("side", px, 5, True)
    settle("rims", pt, 6, True)
    settle("wide", dr, 7, True)
    settle("side", xr2, 8, True)
    settle("rims", vr2, 9, True)
    settle("reach", cr, 10, False)

    moved = {}
    mid_rows = (sub8 > 3) & (sub8 < 7)
    for dx in range(-3, 4):
        mid = ctile[...] if dx == 0 else cr[REACH.index((dx, 0))]
        below = cr[REACH.index((dx, -1))]
        above = cr[REACH.index((dx, 1))]
        rim = jnp.where(sub8 < 3, above, jnp.where(mid_rows, below, 0.0))
        moved[dx] = mid + pltpu.roll(rim, 4, 0)
    whole = moved[0] + pltpu.roll(jnp.where(lane8 < 96, moved[1], moved[-3]), 32, 1)
    whole = whole + pltpu.roll(jnp.where(lane8 < 64, moved[2], moved[-2]), 64, 1)
    whole = whole + pltpu.roll(jnp.where(lane8 >= 32, moved[-1], moved[3]), 96, 1)
    ext_rhs = [whole] + [pltpu.roll(whole, 128 - 32 * v, 1) for v in (1, 2, 3)]
    scales = [stencil[18 + v] for v in range(4)]
    ones = [scales[v] * ext_rhs[v] for v in range(4)]
    packed = [c + pltpu.roll(c, 31, 1) + pltpu.roll(c, 65, 1) for c in ones]
    around = [[c, pltpu.roll(c, 7, 0), pltpu.roll(c, 6, 0)] for c in packed]
    results = []
    for vx in range(2):
        total = jnp.zeros((8, 128), F32)
        for at in range(3):
            for d in range(3):
                total = total + stencil[vx * 9 + at * 3 + d] * around[vx + at][d]
        image = total + pltpu.roll(total, 96, 1) + pltpu.roll(total, 64, 1)
        one = pltpu.roll(ones[vx + 1], 7, 0)
        scale = pltpu.roll(scales[vx + 1], 7, 0)
        right = pltpu.roll(ext_rhs[vx + 1], 7, 0)
        results.append(one + scale * (right - image))
    pair = halves(jnp.concatenate(results, axis=0))
    nodes = halves(times_right(pair, late_part("prol_z")))
    nodes = jnp.concatenate([nodes[0], nodes[0], nodes[1]], axis=0)
    fine = step[...] + fmask[...] * dot(late_part("prol_xy")[:, 0:48], nodes)
    fine = fine.reshape(4, 8, 8, 128)
    for j in range(4):
        out_ref[:, 8 * j : 8 * j + 8, :] = fine[j]
    copies = halves(dot(jnp.concatenate(pair, axis=1), late_part("copy_z")[:, 0:128]))
    copies = jnp.concatenate([copies[0], copies[0], copies[1]], axis=0)
    copies = dot(late_part("copy_y")[:, 0:48], copies)
    coarse_ref[...] = copies.reshape(2, 8, 128)[:, :, 0:32]

    settle("reach", cr, 10, True)


def finish(fine, coarse, fine_out, coarse_out, sem):
    one = pltpu.make_async_copy(fine, fine_out, sem.at[0])
    two = pltpu.make_async_copy(coarse, coarse_out, sem.at[1])
    one.start()
    two.start()
    one.wait()
    two.wait()


def solution(mesh):
    n_dom = mesh.shape["dom"]
    n_sub = mesh.shape["sub"]

    def shards(rhs_local, coefficient):
        (early_at, early), (late_at, late), (flat_at, flat) = constants(4, 16)
        any_space = pl.BlockSpec(memory_space=pl.ANY)
        vmem = pl.BlockSpec(memory_space=pltpu.VMEM)
        outs = (
            jax.ShapeDtypeStruct((8, 32, 128), F32),
            jax.ShapeDtypeStruct((2, 8, 32), F32),
        )

        def space(*shape):
            return pltpu.VMEM(shape, F32)

        dma = pltpu.SemaphoreType.DMA
        operands = [
            pltpu.with_memory_space_constraint(v, pltpu.HBM)
            for v in (coefficient, rhs_local, early, late, flat)
        ]
        fine, coarse = pl.pallas_call(
            functools.partial(kernel, (early_at, late_at, flat_at), n_dom, n_sub),
            out_shape=outs,
            in_specs=[any_space] * 5,
            out_specs=(vmem, vmem),
            scratch_shapes=[
                space(8, 32, 128),
                space(8, 32, 128),
                pltpu.VMEM(early.shape, BF16),
                pltpu.VMEM(late.shape, BF16),
                pltpu.VMEM(flat.shape, F32),
                space(256, 128),
                space(2, 256, 128),
                space(1, 256, 128),
                space(256, 128),
                space(256, 128),
                space(256, 128),
                space(256, 128),
                space(3, 24, 128),
                space(2, 8, 128),
                space(8, 128),
                space(8, 128),
                space(22, 8, 128),
                space(256, 128),
                space(2, 96, 128),
                space(2, 3, 8, 128),
                space(4, 8, 128),
                space(2, 2, 32, 128),
                space(6, 2, 8, 128),
                space(2, 1, 32, 128),
                space(6, 1, 8, 128),
                space(2, 2, 32, 128),
                space(6, 2, 8, 128),
                space(2, 1, 32, 128),
                space(6, 1, 8, 128),
                space(2, 2, 24, 128),
                space(6, 8, 128),
                space(14, 8, 128),
                space(20, 8, 128),
                space(2, 96, 128),
                space(2, 3, 8, 128),
                space(4, 8, 128),
                dma((5,)),
                dma((11,)),
                dma((11,)),
            ],
            compiler_params=pltpu.CompilerParams(
                collective_id=0, has_side_effects=True, vmem_limit_bytes=8 * 2**20
            ),
        )(*operands)
        return pl.pallas_call(
            finish,
            out_shape=outs,
            in_specs=[vmem, vmem],
            out_specs=(any_space, any_space),
            scratch_shapes=[dma((2,))],
            compiler_params=pltpu.CompilerParams(vmem_limit_bytes=2**20),
        )(fine, coarse)

    return jax.shard_map(
        shards,
        mesh=mesh,
        in_specs=(P("dom", "sub", None), P("dom", "sub", None)),
        out_specs=(P("dom", "sub", None), P("dom", "sub", None)),
        check_vma=False,
    )
```

```python
import functools

import jax
import jax.numpy as jnp
import numpy as np
from jax import lax
from jax.experimental import pallas as pl
from jax.experimental.pallas import tpu as pltpu
from jax.sharding import PartitionSpec as P

MESH = pl.DeviceIdType.MESH
HIGHEST = lax.Precision.HIGHEST
F32 = jnp.float32
BF16 = jnp.bfloat16

NEAR = [(dx, dy) for dx in (-1, 0, 1) for dy in (-1, 0, 1) if (dx, dy) != (0, 0)]
WIDE = [(dx, dy) for dx in (-2, -1, 0, 1, 2) for dy in (-1, 0, 1) if (dx, dy) != (0, 0)]
REACH = [(dx, dy) for dx in range(-3, 4) for dy in (-1, 0, 1) if (dx, dy) != (0, 0)]
SIDE = [pair for pair in NEAR if pair[1] == 0]
RIMS = [pair for pair in NEAR if pair[1] != 0]
EDGE = [pair for pair in RIMS if pair[0] != 0]
ROWS = [pair for pair in RIMS if pair[0] == 0]


def opposite(table, pair):
    return table.index((-pair[0], -pair[1]))


def tables():
    degree = 7
    points = np.array(
        [
            -1.0,
            -0.8717401485096066,
            -0.5917001814331423,
            -0.2092992179024789,
            0.2092992179024789,
            0.5917001814331423,
            0.8717401485096066,
            1.0,
        ]
    )
    previous = np.ones(points.shape)
    values = points.copy()
    for level in range(1, degree):
        following = ((2 * level + 1) * points * values - level * previous) / (level + 1)
        previous = values
        values = following
    weights = 2.0 / (degree * (degree + 1) * values**2)
    derivative = np.zeros((8, 8))
    for row_at in range(8):
        for col_at in range(8):
            if row_at != col_at:
                derivative[row_at, col_at] = values[row_at] / (
                    values[col_at] * (points[row_at] - points[col_at])
                )
    derivative[0, 0] = -degree * (degree + 1) / 4.0
    derivative[7, 7] = degree * (degree + 1) / 4.0
    interp = np.stack([(1.0 - points) / 2.0, (1.0 + points) / 2.0], axis=1)
    return derivative, weights, interp


DER, WTS, INT = tables()
TWICE = np.array([2.0, 1.0, 1.0, 1.0, 1.0, 1.0, 1.0, 2.0])
HATS = [TWICE * INT[:, 0], TWICE * INT[:, 1]]


def face_moments(face):
    near = 0 if face == 0 else 1
    return [DER[:, face] * (DER @ HATS[i]) for i in (near, 1 - near)]
MASS = [INT[:, 0] * INT[:, 0], INT[:, 0] * INT[:, 1], INT[:, 1] * INT[:, 1]]


def moment_maps(elements, order, slope):
    maps = np.zeros((len(order), elements + 1, 8 * elements))
    for at, offset in enumerate(order):
        for e in range(elements):
            nodes = slice(8 * e, 8 * e + 8)
            if offset == 0:
                maps[at, e, nodes] += 0.25 if slope else MASS[0]
                maps[at, e + 1, nodes] += 0.25 if slope else MASS[2]
            elif offset == 1:
                maps[at, e, nodes] += -0.25 if slope else MASS[1]
            else:
                maps[at, e + 1, nodes] += -0.25 if slope else MASS[1]
    return maps


def unique_interp(elements):
    maps = np.zeros((8 * elements, elements + 1))
    for e in range(elements):
        maps[8 * e : 8 * e + 8, e] = INT[:, 0]
        maps[8 * e : 8 * e + 8, e + 1] = INT[:, 1]
    return maps


def unique_copies(elements):
    maps = np.zeros((2 * elements, elements + 1))
    for e in range(elements):
        maps[2 * e, e] = 1.0
        maps[2 * e + 1, e + 1] = 1.0
    return maps


def split(matrix):
    high = jnp.asarray(matrix, F32).astype(BF16)
    return high, (jnp.asarray(matrix, F32) - high.astype(F32)).astype(BF16)


def right_halves(matrix):
    high, low = split(matrix)
    top = jnp.concatenate([high, low], axis=1)
    return jnp.concatenate([top, jnp.concatenate([high, jnp.zeros_like(low)], axis=1)], axis=0)


def left_halves(matrix):
    high, low = split(matrix)
    return jnp.concatenate([high, low, high], axis=1)


def wide(block):
    return jnp.pad(block, ((0, 0), (0, 256 - block.shape[1])))


def spots_of(parts):
    spots = {}
    at = 0
    for name, block in parts.items():
        spots[name] = (at, block.shape[0])
        at += block.shape[0]
    return spots, jnp.concatenate(list(parts.values()))


def constants(ey, ez):
    square = DER * DER
    eye8 = np.eye(8)
    eye = np.eye(ez)
    early = {
        "square_z": right_halves(np.kron(eye, square)),
        "square_xy": wide(left_halves(np.kron(square.T, eye8) + np.kron(eye8, square.T))),
    }
    low = unique_interp(ey)
    place = np.zeros((4, 8, 8, 16))
    for side in range(2):
        place[..., 8 * side : 8 * side + ey + 1] = (
            INT[:, side][None, :, None, None] * low.reshape(ey, 8, ey + 1)[:, None]
        )
    place = place.reshape(256, 16)
    rest_z = np.zeros((128, 128))
    rest_z[:, : ez + 1] = unique_interp(ez)
    for at in (32, 64, 96):
        rest_z[:, at : at + ez + 1] = unique_interp(ez)
    prol_z = np.zeros((128, 128))
    prol_z[: ez + 1, :] = unique_interp(ez).T
    copy_z = np.zeros((128, 128))
    copy_z[: ez + 1, : 2 * ez] = unique_copies(ez).T
    copy_y = np.zeros((16, 16))
    for side in range(2):
        copy_y[8 * side : 8 * side + 8, 8 * side : 8 * side + ey + 1] = unique_copies(ey)
    own = np.zeros((32, 256))
    for side in range(2):
        own[8 * (side + 1) + 1 : 8 * (side + 1) + 2 + ey] = place.T[8 * side : 8 * side + ey + 1]
    rest_xy = split(own)
    spill = np.zeros((4, 8, 256))
    low_m = low * np.tile(TWICE, ey)[:, None]
    for side in range(2):
        for at, v in ((0, 1 + side), (64, 3 * side)):
            spill[v, 1 : ey + 2, at + 32 * side : at + 32 * side + 32] = low_m.T
        for at, r in ((128, 1 + ey * side), (144, (ey + 2) * side)):
            for vx in range(2):
                spill[1 + vx, r, at + 8 * side : at + 8 * side + 8] = HATS[vx]
    for at, (dx, dy) in enumerate(EDGE):
        near_v, far_v = (1, 0) if dx < 0 else (2, 3)
        near_r, far_r = (1, 0) if dy < 0 else (1 + ey, 2 + ey)
        spill[near_v, near_r, 160 + at] = 1.0
        spill[far_v, near_r, 168 + at] = 1.0
        spill[near_v, far_r, 176 + at] = 1.0
    spill = split(spill.reshape(32, 256))
    rest_z = np.zeros((128, 128))
    rest_z[:, : ez + 1] = unique_interp(ez)
    for at in (32, 64, 96):
        rest_z[:, at : at + ez + 1] = unique_interp(ez)
    prol_z = np.zeros((128, 128))
    prol_z[: ez + 1, :] = unique_interp(ez).T
    copy_z = np.zeros((128, 128))
    copy_z[: ez + 1, : 2 * ez] = unique_copies(ez).T
    copy_y = np.zeros((16, 16))
    for side in range(2):
        copy_y[8 * side : 8 * side + 8, 8 * side : 8 * side + ey + 1] = unique_copies(ey)
    own = np.zeros((32, 256))
    for side in range(2):
        own[8 * (side + 1) + 1 : 8 * (side + 1) + 2 + ey] = place.T[8 * side : 8 * side + ey + 1]
    rest_xy = split(own)
    spill = np.zeros((4, 8, 256))
    low_m = low * np.tile(TWICE, ey)[:, None]
    for side in range(2):
        for at, v in ((0, 1 + side), (64, 3 * side)):
            spill[v, 1 : ey + 2, at + 32 * side : at + 32 * side + 32] = low_m.T
        for at, r in ((128, 1 + ey * side), (144, (ey + 2) * side)):
            for vx in range(2):
                spill[1 + vx, r, at + 8 * side : at + 8 * side + 8] = HATS[vx]
    for at, (dx, dy) in enumerate(EDGE):
        near_v, far_v = (1, 0) if dx < 0 else (2, 3)
        near_r, far_r = (1, 0) if dy < 0 else (1 + ey, 2 + ey)
        spill[near_v, near_r, 160 + at] = 1.0
        spill[far_v, near_r, 168 + at] = 1.0
        spill[near_v, far_r, 176 + at] = 1.0
    spill = split(spill.reshape(32, 256))
    moment_y = np.zeros((2, 2, 8, 8, 8))
    for side in range(2):
        for at, one in enumerate(face_moments(7 * side)):
            moment_y[side, at] = np.eye(8)[:, :, None] * one[None, None, :]
    moment_y = moment_y.reshape(32, 64)
    late = {
        "grad_z": right_halves(np.kron(eye, DER.T)),
        "back_z": right_halves(np.kron(eye, DER)),
        "rest_z": right_halves(rest_z),
        "prol_z": right_halves(prol_z),
        "copy_z": wide(jnp.concatenate([split(copy_z)[0]] * 2)),
        "prol_xy": wide(left_halves(place)),
        "grad_xy": wide(
            jnp.concatenate([left_halves(np.kron(DER, eye8)), left_halves(np.kron(eye8, DER))])
        ),
        "back_y": wide(left_halves(np.kron(eye8, DER.T))),
        "rest_xy": jnp.concatenate([rest_xy[0], rest_xy[1]]),
        "spill": jnp.concatenate([spill[0], spill[1]]),
        "copy_y": wide(left_halves(copy_y)),
    }
    flat = {}
    for name, slope in (("moment_m", False), ("moment_s", True)):
        block = np.zeros((128, 128))
        for at, one in enumerate(moment_maps(ez, (0, 1, -1), slope)):
            block[:, 32 * at : 32 * at + ez + 1] = one.T
        flat[name] = jnp.asarray(block, F32)
    order_y = (-1, 0, 1)
    mass_y = np.zeros((3, 8, 8 * ey))
    mass_y[:, : ey + 1] = moment_maps(ey, order_y, False)
    slope_y = np.zeros((3, 8, 8 * ey))
    slope_y[:, : ey + 1] = moment_maps(ey, order_y, True)
    mass_y = mass_y.reshape(24, 8 * ey)
    slope_y = slope_y.reshape(24, 8 * ey)
    for name, sign in (("mix_plus", 0.25), ("mix_minus", -0.25)):
        block = np.zeros((24, 128))
        block[:, : 24 * ey] = np.concatenate([slope_y, mass_y, sign * mass_y], axis=1)
        flat[name] = jnp.asarray(block, F32)
    return spots_of(early), spots_of(late), spots_of(flat)


def kernel(
    tables_at, n_dom, n_sub, coef_hbm, rhs_hbm, early_hbm, late_hbm, flat_hbm,
    out_ref, coarse_ref,
    coef, rhs, early, late, flat, weighted, field, held, fmask, fmult, inverse, step,
    pmine, ptile, dtile, ctile, stencil, gfield, fside, frow, fedge,
    xs1, vs1, xs2, vs2,
    xr1, vr1, xr2, vr2, px, pt, dr, cr, fx, fy, fe,
    load_sem, s_sem, r_sem, ready,
):
    early_at, late_at, flat_at = tables_at
    dom = lax.axis_index("dom")
    sub = lax.axis_index("sub")

    loads = []
    for at, (source, dest) in enumerate(
        ((coef_hbm, coef), (early_hbm, early), (rhs_hbm, rhs), (flat_hbm, flat), (late_hbm, late))
    ):
        load = pltpu.make_async_copy(source, dest, load_sem.at[at])
        load.start()
        loads.append(load)

    def present(pair):
        dx, dy = pair
        conds = []
        if dx < 0:
            conds.append(dom >= -dx)
        if dx > 0:
            conds.append(dom < n_dom - dx)
        if dy < 0:
            conds.append(sub >= 1)
        if dy > 0:
            conds.append(sub < n_sub - 1)
        return functools.reduce(jnp.logical_and, conds)

    def target(pair):
        return (dom + pair[0], sub + pair[1])

    for buffer in (xr1, vr1, xr2, vr2, px, pt, dr, cr, fx, fy, fe):
        buffer[...] = jnp.zeros_like(buffer)

    barrier = pltpu.get_barrier_semaphore()
    for pair in NEAR:

        @pl.when(present(pair))
        def _(pair=pair):
            pl.semaphore_signal(barrier, inc=1, device_id=target(pair), device_id_type=MESH)

    near_x = jnp.where(dom >= 1, 1, 0) + jnp.where(dom < n_dom - 1, 1, 0)
    near_y = jnp.where(sub >= 1, 1, 0) + jnp.where(sub < n_sub - 1, 1, 0)
    far_x = near_x + jnp.where(dom >= 2, 1, 0) + jnp.where(dom < n_dom - 2, 1, 0)
    n_side = near_x
    n_rims = near_y * (1 + near_x)
    n_wide = (1 + far_x) * (1 + near_y) - 1
    reach_x = far_x + jnp.where(dom >= 3, 1, 0) + jnp.where(dom < n_dom - 3, 1, 0)
    n_reach = (1 + reach_x) * (1 + near_y) - 1

    row = lax.broadcasted_iota(jnp.int32, (256, 128), 0)
    lane = lax.broadcasted_iota(jnp.int32, (256, 128), 1)
    x_at = lax.shift_right_logical(row, 3) & 7
    b_at = row & 7
    c_at = lane & 7
    place_x = dom * 8 + x_at
    place_y = sub * 32 + lax.shift_right_logical(row, 6) * 8 + b_at
    inside = (
        (place_x > 0) & (place_x < 8 * n_dom - 1)
        & (place_y > 0) & (place_y < 32 * n_sub - 1)
        & (lane > 0) & (lane < 127)
    )
    mask = jnp.where(inside, 1.0, 0.0)
    fmask[...] = mask
    twice = jnp.where((x_at == 0) | (x_at == 7), 2.0, 1.0)
    twice = twice * jnp.where((b_at == 0) | (b_at == 7), 2.0, 1.0)
    fmult[...] = mask * twice * jnp.where((c_at == 0) | (c_at == 7), 2.0, 1.0)

    lane8 = lax.broadcasted_iota(jnp.int32, (8, 128), 1)
    sub8 = lax.broadcasted_iota(jnp.int32, (8, 128), 0)
    z_low = ((lane8 & 7) == 0) & (lane8 > 0)
    z_high = ((lane8 & 7) == 7) & (lane8 < 127)

    def weights_along(spot):
        value = jnp.where((spot == 0) | (spot == 7), float(WTS[0]), float(WTS[1]))
        value = jnp.where((spot == 2) | (spot == 5), float(WTS[2]), value)
        return jnp.where((spot == 3) | (spot == 4), float(WTS[3]), value)

    def fold(v):
        v = v.reshape(32, 8, 128)
        v = v + jnp.where(
            z_high[None], pltpu.roll(v, 127, 2),
            jnp.where(z_low[None], pltpu.roll(v, 1, 2), 0.0),
        )
        up = pltpu.roll(v, 1, 1)
        down = pltpu.roll(v, 7, 1)
        none = jnp.zeros((8, 8, 128), F32)
        up = jnp.concatenate([none, up[:24]], axis=0)
        down = jnp.concatenate([down[8:], none], axis=0)
        v = v + jnp.where((sub8 == 0)[None], up, jnp.where((sub8 == 7)[None], down, 0.0))
        return v.reshape(256, 128)

    def halves(v):
        high = v.astype(BF16)
        return high, (v - high.astype(F32)).astype(BF16)

    def dot(left, right):
        return jnp.dot(left, right, preferred_element_type=F32)

    def early_part(name):
        start, count = early_at[name]
        return early[start : start + count, :]

    def late_part(name):
        start, count = late_at[name]
        return late[start : start + count, :]

    def flat_part(name):
        start, count = flat_at[name]
        return flat[start : start + count, :]

    def times_right(pair, matrix):
        both = dot(jnp.concatenate(pair, axis=1), matrix)
        return both[:, :128] + both[:, 128:]

    def stacked(pair):
        high, low = [
            jnp.concatenate([v[at : at + 64] for at in range(0, v.shape[0], 64)], axis=1) for v in pair
        ]
        return jnp.concatenate([high, high, low], axis=0)

    def rows_of(v):
        return jnp.concatenate([v[:, at : at + 128] for at in range(0, v.shape[1], 128)], axis=0)

    def back_x(v):
        v = v.reshape(4, 8, 8, 128)
        matrix = DER.T
        even = [v[:, b] + v[:, 7 - b] for b in range(4)]
        odd = [v[:, b] - v[:, 7 - b] for b in range(4)]
        planes = [None] * 8
        for a in range(4):
            p = sum(float(matrix[a, b] + matrix[a, 7 - b]) / 2 * even[b] for b in range(4))
            q = sum(float(matrix[a, b] - matrix[a, 7 - b]) / 2 * odd[b] for b in range(4))
            planes[a] = p + q
            planes[7 - a] = q - p
        return jnp.stack(planes, axis=1).reshape(256, 128)

    def with_faces(u, faces, w_rows, w_z):
        w = weighted[...]
        pair = halves(jnp.concatenate([u, faces], axis=0))
        both = dot(late_part("grad_xy")[:, 0:192], stacked(pair))
        all_z = times_right(pair, late_part("grad_z"))
        all_y = rows_of(both[64:128])
        flux_z = halves(jnp.concatenate([w * all_z[0:256], w_z * all_z[256:384]], axis=0))
        flux_y = halves(jnp.concatenate([w * all_y[0:256], w_rows * all_y[256:384]], axis=0))
        back = rows_of(dot(late_part("back_y")[:, 0:192], stacked(flux_y)))
        back = back + times_right(flux_z, late_part("back_z"))
        return back[0:256] + back_x(w * rows_of(both[0:64, 0:512])), back[256:384]

    def local_operator(u):
        w = weighted[...]
        pair = halves(u)
        both = dot(late_part("grad_xy")[:, 0:192], stacked(pair))
        flux_z = halves(w * times_right(pair, late_part("grad_z")))
        flux_y = halves(w * rows_of(both[64:128]))
        back = rows_of(dot(late_part("back_y")[:, 0:192], stacked(flux_y)))
        back = back + times_right(flux_z, late_part("back_z"))
        return back + back_x(w * rows_of(both[0:64]))

    def send(table, pair, source, landing, group):
        at = table.index((-pair[0], -pair[1]))

        @pl.when(present(pair))
        def _():
            pltpu.make_async_remote_copy(
                src_ref=source,
                dst_ref=landing.at[at],
                send_sem=s_sem.at[group],
                recv_sem=r_sem.at[group],
                device_id=target(pair),
                device_id_type=MESH,
            ).start()

    counts = {"side": (n_side, (1, 2)), "rows": (near_y, (1, 2)), "edge": (near_x * near_y, (1, 2, 4)), "rims": (n_rims, (1, 2, 3, 4, 6)), "wide": (n_wide, (1, 2, 3, 5, 7, 8, 9, 11, 14)), "reach": (n_reach, (7, 9, 11, 13, 14, 17, 20))}

    def settle(kind, landing, group, sent):
        count, options = counts[kind]
        for one in options:

            @pl.when(count == one)
            def _(one=one):
                copy = pltpu.make_async_remote_copy(
                    src_ref=landing.at[pl.ds(0, one)],
                    dst_ref=landing.at[pl.ds(0, one)],
                    send_sem=s_sem.at[group],
                    recv_sem=r_sem.at[group],
                    device_id=(dom, sub),
                    device_id_type=MESH,
                )
                if sent:
                    copy.wait_send()
                else:
                    copy.wait_recv()

    def pack(refs, fields, xs, vs):
        for f in range(fields):
            ref = refs.at[f]
            faces = {-1: ref[pl.ds(0, 8, stride=8), :], 1: ref[pl.ds(199, 8, stride=8), :]}
            for j in range(4):
                xs[0, f, 8 * j : 8 * j + 8] = ref[64 * j : 64 * j + 8, :]
                xs[1, f, 8 * j : 8 * j + 8] = ref[64 * j + 56 : 64 * j + 64, :]
            for at, (dx, dy) in enumerate(RIMS):
                face = faces[dy]
                if dx < 0:
                    face = jnp.where(sub8 == 7, pltpu.roll(face, 7, 0), 0.0)
                if dx > 0:
                    face = jnp.where(sub8 == 0, pltpu.roll(face, 1, 0), 0.0)
                vs[at, f] = face

    def exchange(xs, vs, xr, vr, group):
        for pair in RIMS:
            if pair[0] != 0:
                send(RIMS, pair, vs.at[RIMS.index(pair)], vr, group + 1)
        for pair in SIDE:
            send(SIDE, pair, xs.at[SIDE.index(pair)], xr, group)
        for pair in RIMS:
            if pair[0] == 0:
                send(RIMS, pair, vs.at[RIMS.index(pair)], vr, group + 1)

    def unpack(refs, fields, xr, vr):
        for f in range(fields):
            ref = refs.at[f]
            for j in range(4):
                ref[64 * j : 64 * j + 8, :] += xr[0, f, 8 * j : 8 * j + 8]
                ref[64 * j + 56 : 64 * j + 64, :] += xr[1, f, 8 * j : 8 * j + 8]
            for dy, start in ((-1, 0), (1, 199)):
                a, b, c = [vr[RIMS.index((dx, dy)), f] for dx in (-1, 0, 1)]
                ref[pl.ds(start, 8, stride=8), :] += a + b + c

    def in_order(ref):
        v = ref[...].reshape(8, 4, 8, 128)
        return jnp.concatenate([v[:, j] for j in range(4)], axis=0).reshape(256, 128)

    table = weights_along(x_at) * weights_along(b_at) * weights_along(c_at)
    loads[0].wait()
    w = in_order(coef) * table
    weighted[...] = w
    loads[1].wait()
    loads[2].wait()
    field[0] = fold(in_order(rhs))
    w4 = w.reshape(4, 8, 8, 128)
    planes = [w4[:, a].reshape(32, 128) for a in range(8)]
    for side in range(2):
        one, two = face_moments(7 * side)
        rows = [weighted[pl.ds(192 * side + b, 8, stride=8), :] for b in range(8)]
        fside[side, 0:32] = sum(float(one[a]) * planes[a] for a in range(8))
        fside[side, 32:64] = sum(float(two[a]) * planes[a] for a in range(8))
        fside[side, 64:96] = planes[7 * side]
        frow[side, 0] = sum(float(one[b]) * rows[b] for b in range(8))
        frow[side, 1] = sum(float(two[b]) * rows[b] for b in range(8))
        frow[side, 2] = rows[7 * side]
    fedge[...] = jnp.zeros_like(fedge)
    for at, (dx, dy) in enumerate(EDGE):
        x_side, y_side = (dx + 1) // 2, (dy + 1) // 2
        spot, line = 31 * y_side, 7 * x_side
        fedge[at, 0:1] = 2.0 * (fside[x_side, spot : spot + 1] + frow[y_side, 0, line : line + 1])
        fedge[at, 1:2] = 2.0 * fside[x_side, 32 + spot : 33 + spot]
        fedge[at, 2:3] = 2.0 * frow[y_side, 1, line : line + 1]
        fedge[at, 3:4] = 4.0 * frow[y_side, 2, line : line + 1]
    pair = halves(w)
    diagonal = rows_of(dot(early_part("square_xy")[:, 0:192], stacked(pair)))
    field[1] = fold(diagonal + times_right(pair, early_part("square_z")))
    pack(field, 2, xs1, vs1)

    pl.semaphore_wait(barrier, (1 + near_x) * (1 + near_y) - 1)
    exchange(xs1, vs1, xr1, vr1, 0)

    def announce(stage):
        for pair in SIDE:

            @pl.when(present(pair))
            def _(pair=pair):
                pl.semaphore_signal(
                    ready.at[stage], inc=1, device_id=target(pair), device_id_type=MESH
                )

    announce(0)
    for at, pair in enumerate(SIDE):
        send(SIDE, pair, fside.at[at], fx, 2)
    for at, pair in enumerate(ROWS):
        send(ROWS, pair, frow.at[at], fy, 3)
    for at, pair in enumerate(EDGE):
        send(EDGE, pair, fedge.at[at], fe, 4)

    loads[3].wait()
    w4 = weighted[...].reshape(4, 8, 8, 128)
    planes = [w4[:, a].reshape(32, 128) for a in range(8)]
    moments = [sum(float(m[a]) * planes[a] for a in range(8) if m[a] != 0.0) for m in MASS]
    moments.append(moments[0] + 2.0 * moments[1] + moments[2])
    stack = jnp.concatenate(moments, axis=0)
    mass_z = jnp.dot(stack, flat_part("moment_m"), precision=HIGHEST, preferred_element_type=F32)
    slope_z = jnp.dot(stack, flat_part("moment_s"), precision=HIGHEST, preferred_element_type=F32)
    none = jnp.zeros((32, 128), F32)
    mine = []
    for at in range(3):
        part = slice(32 * at, 32 * at + 32)
        parts = jnp.concatenate([mass_z[part], slope_z[part], mass_z[96:128], none], axis=0)
        mix = flat_part("mix_minus" if at == 1 else "mix_plus")
        one = jnp.dot(mix, parts, precision=HIGHEST, preferred_element_type=F32)
        pmine[at] = one
        mine.append(one.reshape(3, 8, 128))
    dtile[...] = jnp.where(lane8 < 32, mine[0][1], pltpu.roll(mine[2][1], 32, 1))
    for side, vertex, first in ((0, 0, 1), (1, 4, 0)):
        total = jnp.zeros((8, 128), F32)
        for c in range(3):
            for d in range(2):
                goal = 2 * c + d
                moved = pltpu.roll(mine[c][first + d], (goal - vertex) % 8, 0)
                total = jnp.where(sub8 == goal, moved, total)
        ptile[side] = total
    send(SIDE, (-1, 0), pmine.at[pl.ds(0, 2)], px, 5)
    send(SIDE, (1, 0), pmine.at[pl.ds(1, 2)], px, 5)
    for pair in RIMS:
        send(RIMS, pair, ptile.at[(pair[1] + 1) // 2], pt, 6)
    pl.semaphore_wait(ready.at[0], near_x)
    announce(1)
    for pair in WIDE:
        send(WIDE, pair, dtile, dr, 7)
    loads[4].wait()

    settle("side", xr1, 0, False)
    settle("rims", vr1, 1, False)
    unpack(field, 2, xr1, vr1)

    residual = fmask[...] * field[0]
    inv = fmask[...] / field[1]
    inverse[...] = inv
    field[0] = residual
    theta = 1.1
    delta = 0.9
    sigma = theta / delta
    rho0 = 1.0 / sigma
    rho1 = 1.0 / (2.0 * sigma - rho0)
    step_one = inv * residual / theta
    step[...] = step_one
    held[0] = fold(local_operator(step_one))
    pack(held, 1, xs2, vs2)
    exchange(xs2, vs2, xr2, vr2, 8)

    factor = 2.0 * rho1 / delta
    g = factor * inverse[...] * held[0]
    gfield[...] = g
    start = (1.0 + rho1 * rho0) * step_one + factor * inv * residual
    step[...] = start
    settle("side", fx, 2, False)
    settle("rows", fy, 3, False)
    settle("edge", fe, 4, False)
    faces = []
    for first in (0, 56):
        for j in range(4):
            faces.append(g[64 * j + first : 64 * j + first + 8])
    rims = [gfield[pl.ds(0, 8, stride=8), :], gfield[pl.ds(199, 8, stride=8), :]]
    corner = jnp.zeros((8, 128), F32)
    lines = [jnp.zeros((8, 128), F32) for _ in range(4)]
    for at, (dx, dy) in enumerate(EDGE):
        line = 0 if dx < 0 else 7
        moved = pltpu.roll(rims[(dy + 1) // 2], (at - line) % 8, 0)
        corner = jnp.where(sub8 == at, moved, corner)
        given = fe[at]
        for k in range(4):
            lines[k] = jnp.where(sub8 == at, pltpu.roll(given, (at - k) % 8, 0), lines[k])
    none40 = jnp.zeros((40, 128), F32)
    faces = jnp.concatenate(faces + rims + [corner, none40], axis=0)
    two = [2.0 * fx[0, 64:96], 2.0 * fx[1, 64:96], 2.0 * fy[0, 2], 2.0 * fy[1, 2]]
    w_rows = jnp.concatenate(two + [jnp.zeros((48, 128), F32)], axis=0)
    w_z = jnp.concatenate(two + [lines[3], none40], axis=0)
    image, face_image = with_faces(start - g, faces, w_rows, w_z)
    defect = residual - fmult[...] * image
    near_w = [fx[0, 0:32], fx[1, 0:32], fy[0, 0], fy[1, 0], lines[0]]
    far_w = [fx[0, 32:64], fx[1, 32:64], fy[0, 1], fy[1, 1]]
    near = jnp.concatenate(near_w, axis=0) * faces[0:88] + face_image[0:88]
    far = jnp.concatenate(far_w, axis=0) * faces[0:80]
    parts = [
        near[0:64], far[0:64], near[64:80], far[64:80], near[80:88],
        lines[1] * corner, lines[2] * corner, jnp.zeros((72, 128), F32),
    ]
    twice_z = jnp.where(((lane8 & 7) == 0) | ((lane8 & 7) == 7), 2.0, 1.0)
    parts = jnp.concatenate(parts, axis=0).reshape(32, 8, 128) * twice_z[None]
    part = dot(late_part("rest_xy"), jnp.concatenate(halves(defect), axis=1))
    part = part + dot(late_part("spill"), jnp.concatenate(halves(parts.reshape(256, 128)), axis=1))
    part = part[0:32, :128] + part[0:32, 128:] + part[32:64, :128]
    coarse = times_right(halves(part), late_part("rest_z"))
    tile = jnp.where(lane8 < 64, jnp.where(lane8 < 32, coarse[0:8], coarse[8:16]), jnp.where(lane8 < 96, coarse[16:24], coarse[24:32]))
    ctile[...] = tile
    pl.semaphore_wait(ready.at[1], near_x)
    for pair in sorted(REACH, key=lambda p: -abs(p[0]) - abs(p[1])):
        send(REACH, pair, ctile, cr, 10)

    settle("side", px, 5, False)
    settle("rims", pt, 6, False)
    settle("wide", dr, 7, False)
    row_low = sub8 < 2
    row_mid = sub8 == 2

    def extend(own, received):
        moved = []
        for dx in (-2, -1, 0, 1, 2):
            mid = own if dx == 0 else received[WIDE.index((dx, 0))]
            below = received[WIDE.index((dx, -1))]
            above = received[WIDE.index((dx, 1))]
            rim = jnp.where(row_low, above, jnp.where(row_mid, 0.0, below))
            moved.append(pltpu.roll(mid, 1, 0) + pltpu.roll(rim, 5, 0))
        return [moved[v + 1] + pltpu.roll(moved[v], 96, 1) for v in range(4)]

    ext_diag = extend(dtile[...], dr)
    vertex_y = sub * 4 + sub8 - 1
    good_yz = (vertex_y > 0) & (vertex_y < 4 * n_sub) & (sub8 < 7) & (lane8 > 0) & (lane8 < 16)
    scales = []
    for v in range(4):
        vertex_x = dom + v - 1
        good = good_yz & (vertex_x > 0) & (vertex_x < n_dom)
        scales.append(jnp.where(good, (2.0 / 3.0) / jnp.where(good, ext_diag[v], 1.0), 0.0))

    def joined(dx, c):
        if dx == 0:
            base = pmine[c]
        else:
            base = px[SIDE.index((dx, 0)), c if dx > 0 else c - 1]
        base = base.reshape(3, 8, 128)
        below = pt[RIMS.index((dx, -1))]
        above = pt[RIMS.index((dx, 1))]
        out = []
        for d in range(3):
            total = base[d]
            if d < 2:
                moved = pltpu.roll(below, (-2 * c - d) % 8, 0)
                total = total + jnp.where(sub8 == 0, moved, 0.0)
            if d > 0:
                moved = pltpu.roll(above, (4 - 2 * c - (d - 1)) % 8, 0)
                total = total + jnp.where(sub8 == 4, moved, 0.0)
            out.append(total)
        return out

    cross = joined(0, 1)
    own_low = [a + b for a, b in zip(joined(0, 0), joined(-1, 2), strict=True)]
    own_high = [a + b for a, b in zip(joined(0, 2), joined(1, 0), strict=True)]
    for vx, blocks in enumerate(
        ((joined(-1, 1), own_low, cross), (cross, own_high, joined(1, 1)))
    ):
        for at in range(3):
            for d in range(3):
                stencil[vx * 9 + at * 3 + d] = blocks[at][d]
    for v in range(4):
        stencil[18 + v] = scales[v]

    settle("side", xr2, 8, False)
    settle("rims", vr2, 9, False)
    unpack(held, 1, xr2, vr2)
    step[...] = step[...] - factor * inverse[...] * held[0]

    settle("side", xr1, 0, True)
    settle("rims", vr1, 1, True)
    settle("side", fx, 2, True)
    settle("rows", fy, 3, True)
    settle("edge", fe, 4, True)
    settle("side", px, 5, True)
    settle("rims", pt, 6, True)
    settle("wide", dr, 7, True)
    settle("side", xr2, 8, True)
    settle("rims", vr2, 9, True)
    settle("reach", cr, 10, False)

    moved = {}
    mid_rows = (sub8 > 3) & (sub8 < 7)
    for dx in range(-3, 4):
        mid = ctile[...] if dx == 0 else cr[REACH.index((dx, 0))]
        below = cr[REACH.index((dx, -1))]
        above = cr[REACH.index((dx, 1))]
        rim = jnp.where(sub8 < 3, above, jnp.where(mid_rows, below, 0.0))
        moved[dx] = mid + pltpu.roll(rim, 4, 0)
    whole = moved[0] + pltpu.roll(jnp.where(lane8 < 96, moved[1], moved[-3]), 32, 1)
    whole = whole + pltpu.roll(jnp.where(lane8 < 64, moved[2], moved[-2]), 64, 1)
    whole = whole + pltpu.roll(jnp.where(lane8 >= 32, moved[-1], moved[3]), 96, 1)
    ext_rhs = [whole] + [pltpu.roll(whole, 128 - 32 * v, 1) for v in (1, 2, 3)]
    scales = [stencil[18 + v] for v in range(4)]
    ones = [scales[v] * ext_rhs[v] for v in range(4)]
    packed = [c + pltpu.roll(c, 31, 1) + pltpu.roll(c, 65, 1) for c in ones]
    around = [[c, pltpu.roll(c, 7, 0), pltpu.roll(c, 6, 0)] for c in packed]
    results = []
    for vx in range(2):
        total = jnp.zeros((8, 128), F32)
        for at in range(3):
            for d in range(3):
                total = total + stencil[vx * 9 + at * 3 + d] * around[vx + at][d]
        image = total + pltpu.roll(total, 96, 1) + pltpu.roll(total, 64, 1)
        one = pltpu.roll(ones[vx + 1], 7, 0)
        scale = pltpu.roll(scales[vx + 1], 7, 0)
        right = pltpu.roll(ext_rhs[vx + 1], 7, 0)
        results.append(one + scale * (right - image))
    pair = halves(jnp.concatenate(results, axis=0))
    nodes = halves(times_right(pair, late_part("prol_z")))
    nodes = jnp.concatenate([nodes[0], nodes[0], nodes[1]], axis=0)
    fine = step[...] + fmask[...] * dot(late_part("prol_xy")[:, 0:48], nodes)
    fine = fine.reshape(4, 8, 8, 128)
    for j in range(4):
        out_ref[:, 8 * j : 8 * j + 8, :] = fine[j]
    copies = halves(dot(jnp.concatenate(pair, axis=1), late_part("copy_z")[:, 0:128]))
    copies = jnp.concatenate([copies[0], copies[0], copies[1]], axis=0)
    copies = dot(late_part("copy_y")[:, 0:48], copies)
    coarse_ref[...] = copies.reshape(2, 8, 128)[:, :, 0:32]

    settle("reach", cr, 10, True)


def finish(fine, coarse, fine_out, coarse_out, sem):
    one = pltpu.make_async_copy(fine, fine_out, sem.at[0])
    two = pltpu.make_async_copy(coarse, coarse_out, sem.at[1])
    one.start()
    two.start()
    one.wait()
    two.wait()


def solution(mesh):
    n_dom = mesh.shape["dom"]
    n_sub = mesh.shape["sub"]

    def shards(rhs_local, coefficient):
        (early_at, early), (late_at, late), (flat_at, flat) = constants(4, 16)
        any_space = pl.BlockSpec(memory_space=pl.ANY)
        vmem = pl.BlockSpec(memory_space=pltpu.VMEM)
        outs = (
            jax.ShapeDtypeStruct((8, 32, 128), F32),
            jax.ShapeDtypeStruct((2, 8, 32), F32),
        )

        def space(*shape):
            return pltpu.VMEM(shape, F32)

        dma = pltpu.SemaphoreType.DMA
        operands = [
            pltpu.with_memory_space_constraint(v, pltpu.HBM)
            for v in (coefficient, rhs_local, early, late, flat)
        ]
        fine, coarse = pl.pallas_call(
            functools.partial(kernel, (early_at, late_at, flat_at), n_dom, n_sub),
            out_shape=outs,
            in_specs=[any_space] * 5,
            out_specs=(vmem, vmem),
            scratch_shapes=[
                space(8, 32, 128),
                space(8, 32, 128),
                pltpu.VMEM(early.shape, BF16),
                pltpu.VMEM(late.shape, BF16),
                pltpu.VMEM(flat.shape, F32),
                space(256, 128),
                space(2, 256, 128),
                space(1, 256, 128),
                space(256, 128),
                space(256, 128),
                space(256, 128),
                space(256, 128),
                space(3, 24, 128),
                space(2, 8, 128),
                space(8, 128),
                space(8, 128),
                space(22, 8, 128),
                space(256, 128),
                space(2, 96, 128),
                space(2, 3, 8, 128),
                space(4, 8, 128),
                space(2, 2, 32, 128),
                space(6, 2, 8, 128),
                space(2, 1, 32, 128),
                space(6, 1, 8, 128),
                space(2, 2, 32, 128),
                space(6, 2, 8, 128),
                space(2, 1, 32, 128),
                space(6, 1, 8, 128),
                space(2, 2, 24, 128),
                space(6, 8, 128),
                space(14, 8, 128),
                space(20, 8, 128),
                space(2, 96, 128),
                space(2, 3, 8, 128),
                space(4, 8, 128),
                dma((5,)),
                dma((11,)),
                dma((11,)),
                pltpu.SemaphoreType.REGULAR((2,)),
            ],
            compiler_params=pltpu.CompilerParams(
                collective_id=0, has_side_effects=True, vmem_limit_bytes=8 * 2**20
            ),
        )(*operands)
        return pl.pallas_call(
            finish,
            out_shape=outs,
            in_specs=[vmem, vmem],
            out_specs=(any_space, any_space),
            scratch_shapes=[dma((2,))],
            compiler_params=pltpu.CompilerParams(vmem_limit_bytes=2**20),
        )(fine, coarse)

    return jax.shard_map(
        shards,
        mesh=mesh,
        in_specs=(P("dom", "sub", None), P("dom", "sub", None)),
        out_specs=(P("dom", "sub", None), P("dom", "sub", None)),
        check_vma=False,
    )
```

```python
import functools

import jax
import jax.numpy as jnp
import numpy as np
from jax import lax
from jax.experimental import pallas as pl
from jax.experimental.pallas import tpu as pltpu
from jax.sharding import PartitionSpec as P

MESH = pl.DeviceIdType.MESH
HIGHEST = lax.Precision.HIGHEST
F32 = jnp.float32
BF16 = jnp.bfloat16

NEAR = [(dx, dy) for dx in (-1, 0, 1) for dy in (-1, 0, 1) if (dx, dy) != (0, 0)]
WIDE = [(dx, dy) for dx in (-2, -1, 0, 1, 2) for dy in (-1, 0, 1) if (dx, dy) != (0, 0)]
REACH = [(dx, dy) for dx in range(-3, 4) for dy in (-1, 0, 1) if (dx, dy) != (0, 0)]
SIDE = [pair for pair in NEAR if pair[1] == 0]
RIMS = [pair for pair in NEAR if pair[1] != 0]
EDGE = [pair for pair in RIMS if pair[0] != 0]
ROWS = [pair for pair in RIMS if pair[0] == 0]


def opposite(table, pair):
    return table.index((-pair[0], -pair[1]))


def tables():
    degree = 7
    points = np.array(
        [
            -1.0,
            -0.8717401485096066,
            -0.5917001814331423,
            -0.2092992179024789,
            0.2092992179024789,
            0.5917001814331423,
            0.8717401485096066,
            1.0,
        ]
    )
    previous = np.ones(points.shape)
    values = points.copy()
    for level in range(1, degree):
        following = ((2 * level + 1) * points * values - level * previous) / (level + 1)
        previous = values
        values = following
    weights = 2.0 / (degree * (degree + 1) * values**2)
    derivative = np.zeros((8, 8))
    for row_at in range(8):
        for col_at in range(8):
            if row_at != col_at:
                derivative[row_at, col_at] = values[row_at] / (
                    values[col_at] * (points[row_at] - points[col_at])
                )
    derivative[0, 0] = -degree * (degree + 1) / 4.0
    derivative[7, 7] = degree * (degree + 1) / 4.0
    interp = np.stack([(1.0 - points) / 2.0, (1.0 + points) / 2.0], axis=1)
    return derivative, weights, interp


DER, WTS, INT = tables()
TWICE = np.array([2.0, 1.0, 1.0, 1.0, 1.0, 1.0, 1.0, 2.0])
HATS = [TWICE * INT[:, 0], TWICE * INT[:, 1]]


def face_moments(face):
    near = 0 if face == 0 else 1
    return [DER[:, face] * (DER @ HATS[i]) for i in (near, 1 - near)]
MASS = [INT[:, 0] * INT[:, 0], INT[:, 0] * INT[:, 1], INT[:, 1] * INT[:, 1]]


def moment_maps(elements, order, slope):
    maps = np.zeros((len(order), elements + 1, 8 * elements))
    for at, offset in enumerate(order):
        for e in range(elements):
            nodes = slice(8 * e, 8 * e + 8)
            if offset == 0:
                maps[at, e, nodes] += 0.25 if slope else MASS[0]
                maps[at, e + 1, nodes] += 0.25 if slope else MASS[2]
            elif offset == 1:
                maps[at, e, nodes] += -0.25 if slope else MASS[1]
            else:
                maps[at, e + 1, nodes] += -0.25 if slope else MASS[1]
    return maps


def unique_interp(elements):
    maps = np.zeros((8 * elements, elements + 1))
    for e in range(elements):
        maps[8 * e : 8 * e + 8, e] = INT[:, 0]
        maps[8 * e : 8 * e + 8, e + 1] = INT[:, 1]
    return maps


def unique_copies(elements):
    maps = np.zeros((2 * elements, elements + 1))
    for e in range(elements):
        maps[2 * e, e] = 1.0
        maps[2 * e + 1, e + 1] = 1.0
    return maps


def split(matrix):
    high = jnp.asarray(matrix, F32).astype(BF16)
    return high, (jnp.asarray(matrix, F32) - high.astype(F32)).astype(BF16)


def right_halves(matrix):
    high, low = split(matrix)
    top = jnp.concatenate([high, low], axis=1)
    return jnp.concatenate([top, jnp.concatenate([high, jnp.zeros_like(low)], axis=1)], axis=0)


def left_halves(matrix):
    high, low = split(matrix)
    return jnp.concatenate([high, low, high], axis=1)


def wide(block):
    return jnp.pad(block, ((0, 0), (0, 256 - block.shape[1])))


def spots_of(parts):
    spots = {}
    at = 0
    for name, block in parts.items():
        spots[name] = (at, block.shape[0])
        at += block.shape[0]
    return spots, jnp.concatenate(list(parts.values()))


def constants(ey, ez):
    square = DER * DER
    eye8 = np.eye(8)
    eye = np.eye(ez)
    early = {
        "square_z": right_halves(np.kron(eye, square)),
        "square_xy": wide(left_halves(np.kron(square.T, eye8) + np.kron(eye8, square.T))),
    }
    low = unique_interp(ey)
    place = np.zeros((4, 8, 8, 16))
    for side in range(2):
        place[..., 8 * side : 8 * side + ey + 1] = (
            INT[:, side][None, :, None, None] * low.reshape(ey, 8, ey + 1)[:, None]
        )
    place = place.reshape(256, 16)
    rest_z = np.zeros((128, 128))
    rest_z[:, : ez + 1] = unique_interp(ez)
    for at in (32, 64, 96):
        rest_z[:, at : at + ez + 1] = unique_interp(ez)
    prol_z = np.zeros((128, 128))
    prol_z[: ez + 1, :] = unique_interp(ez).T
    copy_z = np.zeros((128, 128))
    copy_z[: ez + 1, : 2 * ez] = unique_copies(ez).T
    copy_y = np.zeros((16, 16))
    for side in range(2):
        copy_y[8 * side : 8 * side + 8, 8 * side : 8 * side + ey + 1] = unique_copies(ey)
    own = np.zeros((32, 256))
    for side in range(2):
        own[8 * (side + 1) + 1 : 8 * (side + 1) + 2 + ey] = place.T[8 * side : 8 * side + ey + 1]
    rest_xy = split(own)
    spill = np.zeros((4, 8, 256))
    low_m = low * np.tile(TWICE, ey)[:, None]
    for side in range(2):
        for at, v in ((0, 1 + side), (64, 3 * side)):
            spill[v, 1 : ey + 2, at + 32 * side : at + 32 * side + 32] = low_m.T
        for at, r in ((128, 1 + ey * side), (144, (ey + 2) * side)):
            for vx in range(2):
                spill[1 + vx, r, at + 8 * side : at + 8 * side + 8] = HATS[vx]
    for at, (dx, dy) in enumerate(EDGE):
        near_v, far_v = (1, 0) if dx < 0 else (2, 3)
        near_r, far_r = (1, 0) if dy < 0 else (1 + ey, 2 + ey)
        spill[near_v, near_r, 160 + at] = 1.0
        spill[far_v, near_r, 168 + at] = 1.0
        spill[near_v, far_r, 176 + at] = 1.0
    spill = split(spill.reshape(32, 256))
    rest_z = np.zeros((128, 128))
    rest_z[:, : ez + 1] = unique_interp(ez)
    for at in (32, 64, 96):
        rest_z[:, at : at + ez + 1] = unique_interp(ez)
    prol_z = np.zeros((128, 128))
    prol_z[: ez + 1, :] = unique_interp(ez).T
    copy_z = np.zeros((128, 128))
    copy_z[: ez + 1, : 2 * ez] = unique_copies(ez).T
    copy_y = np.zeros((16, 16))
    for side in range(2):
        copy_y[8 * side : 8 * side + 8, 8 * side : 8 * side + ey + 1] = unique_copies(ey)
    own = np.zeros((32, 256))
    for side in range(2):
        own[8 * (side + 1) + 1 : 8 * (side + 1) + 2 + ey] = place.T[8 * side : 8 * side + ey + 1]
    rest_xy = split(own)
    spill = np.zeros((4, 8, 256))
    low_m = low * np.tile(TWICE, ey)[:, None]
    for side in range(2):
        for at, v in ((0, 1 + side), (64, 3 * side)):
            spill[v, 1 : ey + 2, at + 32 * side : at + 32 * side + 32] = low_m.T
        for at, r in ((128, 1 + ey * side), (144, (ey + 2) * side)):
            for vx in range(2):
                spill[1 + vx, r, at + 8 * side : at + 8 * side + 8] = HATS[vx]
    for at, (dx, dy) in enumerate(EDGE):
        near_v, far_v = (1, 0) if dx < 0 else (2, 3)
        near_r, far_r = (1, 0) if dy < 0 else (1 + ey, 2 + ey)
        spill[near_v, near_r, 160 + at] = 1.0
        spill[far_v, near_r, 168 + at] = 1.0
        spill[near_v, far_r, 176 + at] = 1.0
    spill = split(spill.reshape(32, 256))
    moment_y = np.zeros((2, 2, 8, 8, 8))
    for side in range(2):
        for at, one in enumerate(face_moments(7 * side)):
            moment_y[side, at] = np.eye(8)[:, :, None] * one[None, None, :]
    moment_y = moment_y.reshape(32, 64)
    late = {
        "grad_z": right_halves(np.kron(eye, DER.T)),
        "back_z": right_halves(np.kron(eye, DER)),
        "rest_z": right_halves(rest_z),
        "prol_z": right_halves(prol_z),
        "copy_z": wide(jnp.concatenate([split(copy_z)[0]] * 2)),
        "prol_xy": wide(left_halves(place)),
        "grad_xy": wide(
            jnp.concatenate([left_halves(np.kron(DER, eye8)), left_halves(np.kron(eye8, DER))])
        ),
        "back_y": wide(left_halves(np.kron(eye8, DER.T))),
        "rest_xy": jnp.concatenate([rest_xy[0], rest_xy[1]]),
        "spill": jnp.concatenate([spill[0], spill[1]]),
        "copy_y": wide(left_halves(copy_y)),
    }
    flat = {}
    for name, slope in (("moment_m", False), ("moment_s", True)):
        block = np.zeros((128, 128))
        for at, one in enumerate(moment_maps(ez, (0, 1, -1), slope)):
            block[:, 32 * at : 32 * at + ez + 1] = one.T
        flat[name] = jnp.asarray(block, F32)
    order_y = (-1, 0, 1)
    mass_y = np.zeros((3, 8, 8 * ey))
    mass_y[:, : ey + 1] = moment_maps(ey, order_y, False)
    slope_y = np.zeros((3, 8, 8 * ey))
    slope_y[:, : ey + 1] = moment_maps(ey, order_y, True)
    mass_y = mass_y.reshape(24, 8 * ey)
    slope_y = slope_y.reshape(24, 8 * ey)
    for name, sign in (("mix_plus", 0.25), ("mix_minus", -0.25)):
        block = np.zeros((24, 128))
        block[:, : 24 * ey] = np.concatenate([slope_y, mass_y, sign * mass_y], axis=1)
        flat[name] = jnp.asarray(block, F32)
    return spots_of(early), spots_of(late), spots_of(flat)


def kernel(
    tables_at, n_dom, n_sub, coef_hbm, rhs_hbm, early_hbm, late_hbm, flat_hbm,
    out_ref, coarse_ref,
    coef, rhs, early, late, flat, weighted, field, held, fmask, fmult, inverse, step,
    pmine, ptile, dtile, ctile, stencil, gfield, fside, frow, fedge,
    xs1, vs1, xs2, vs2,
    xr1, vr1, xr2, vr2, px, pt, dr, cr, fx, fy, fe,
    load_sem, s_sem, r_sem, ready,
):
    early_at, late_at, flat_at = tables_at
    dom = lax.axis_index("dom")
    sub = lax.axis_index("sub")

    loads = []
    for at, (source, dest) in enumerate(
        ((coef_hbm, coef), (early_hbm, early), (rhs_hbm, rhs), (flat_hbm, flat), (late_hbm, late))
    ):
        load = pltpu.make_async_copy(source, dest, load_sem.at[at])
        load.start()
        loads.append(load)

    def present(pair):
        dx, dy = pair
        conds = []
        if dx < 0:
            conds.append(dom >= -dx)
        if dx > 0:
            conds.append(dom < n_dom - dx)
        if dy < 0:
            conds.append(sub >= 1)
        if dy > 0:
            conds.append(sub < n_sub - 1)
        return functools.reduce(jnp.logical_and, conds)

    def target(pair):
        return (dom + pair[0], sub + pair[1])

    for buffer in (xr1, vr1, xr2, vr2, px, pt, dr, cr, fx, fy, fe):
        buffer[...] = jnp.zeros_like(buffer)

    barrier = pltpu.get_barrier_semaphore()
    for pair in NEAR:

        @pl.when(present(pair))
        def _(pair=pair):
            pl.semaphore_signal(barrier, inc=1, device_id=target(pair), device_id_type=MESH)

    near_x = jnp.where(dom >= 1, 1, 0) + jnp.where(dom < n_dom - 1, 1, 0)
    near_y = jnp.where(sub >= 1, 1, 0) + jnp.where(sub < n_sub - 1, 1, 0)
    far_x = near_x + jnp.where(dom >= 2, 1, 0) + jnp.where(dom < n_dom - 2, 1, 0)
    n_side = near_x
    n_rims = near_y * (1 + near_x)
    n_wide = (1 + far_x) * (1 + near_y) - 1
    reach_x = far_x + jnp.where(dom >= 3, 1, 0) + jnp.where(dom < n_dom - 3, 1, 0)
    n_reach = (1 + reach_x) * (1 + near_y) - 1

    row = lax.broadcasted_iota(jnp.int32, (256, 128), 0)
    lane = lax.broadcasted_iota(jnp.int32, (256, 128), 1)
    x_at = lax.shift_right_logical(row, 3) & 7
    b_at = row & 7
    c_at = lane & 7
    place_x = dom * 8 + x_at
    place_y = sub * 32 + lax.shift_right_logical(row, 6) * 8 + b_at
    inside = (
        (place_x > 0) & (place_x < 8 * n_dom - 1)
        & (place_y > 0) & (place_y < 32 * n_sub - 1)
        & (lane > 0) & (lane < 127)
    )
    mask = jnp.where(inside, 1.0, 0.0)
    fmask[...] = mask
    twice = jnp.where((x_at == 0) | (x_at == 7), 2.0, 1.0)
    twice = twice * jnp.where((b_at == 0) | (b_at == 7), 2.0, 1.0)
    fmult[...] = mask * twice * jnp.where((c_at == 0) | (c_at == 7), 2.0, 1.0)

    lane8 = lax.broadcasted_iota(jnp.int32, (8, 128), 1)
    sub8 = lax.broadcasted_iota(jnp.int32, (8, 128), 0)
    z_low = ((lane8 & 7) == 0) & (lane8 > 0)
    z_high = ((lane8 & 7) == 7) & (lane8 < 127)

    def weights_along(spot):
        value = jnp.where((spot == 0) | (spot == 7), float(WTS[0]), float(WTS[1]))
        value = jnp.where((spot == 2) | (spot == 5), float(WTS[2]), value)
        return jnp.where((spot == 3) | (spot == 4), float(WTS[3]), value)

    def fold(v):
        v = v.reshape(32, 8, 128)
        v = v + jnp.where(
            z_high[None], pltpu.roll(v, 127, 2),
            jnp.where(z_low[None], pltpu.roll(v, 1, 2), 0.0),
        )
        up = pltpu.roll(v, 1, 1)
        down = pltpu.roll(v, 7, 1)
        none = jnp.zeros((8, 8, 128), F32)
        up = jnp.concatenate([none, up[:24]], axis=0)
        down = jnp.concatenate([down[8:], none], axis=0)
        v = v + jnp.where((sub8 == 0)[None], up, jnp.where((sub8 == 7)[None], down, 0.0))
        return v.reshape(256, 128)

    def halves(v):
        high = v.astype(BF16)
        return high, (v - high.astype(F32)).astype(BF16)

    def dot(left, right):
        return jnp.dot(left, right, preferred_element_type=F32)

    def early_part(name):
        start, count = early_at[name]
        return early[start : start + count, :]

    def late_part(name):
        start, count = late_at[name]
        return late[start : start + count, :]

    def flat_part(name):
        start, count = flat_at[name]
        return flat[start : start + count, :]

    def times_right(pair, matrix):
        left = jnp.concatenate(pair, axis=1)
        half = left.shape[0] // 2 if left.shape[0] > 32 else left.shape[0]
        sums = []
        for at in range(0, left.shape[0], half):
            both = dot(left[at : at + half], matrix)
            sums.append(both[:, :128] + both[:, 128:])
        return jnp.concatenate(sums, axis=0)

    def stacked(pair):
        high, low = [
            jnp.concatenate([v[at : at + 64] for at in range(0, v.shape[0], 64)], axis=1) for v in pair
        ]
        return jnp.concatenate([high, high, low], axis=0)

    def rows_of(v):
        return jnp.concatenate([v[:, at : at + 128] for at in range(0, v.shape[1], 128)], axis=0)

    def back_x(v):
        v = v.reshape(4, 8, 8, 128)
        matrix = DER.T
        even = [v[:, b] + v[:, 7 - b] for b in range(4)]
        odd = [v[:, b] - v[:, 7 - b] for b in range(4)]
        planes = [None] * 8
        for a in range(4):
            p = sum(float(matrix[a, b] + matrix[a, 7 - b]) / 2 * even[b] for b in range(4))
            q = sum(float(matrix[a, b] - matrix[a, 7 - b]) / 2 * odd[b] for b in range(4))
            planes[a] = p + q
            planes[7 - a] = q - p
        return jnp.stack(planes, axis=1).reshape(256, 128)

    def with_faces(u, faces, face_weights):
        w = weighted[...]
        pair = halves(jnp.concatenate([u, faces], axis=0))
        both = dot(late_part("grad_xy")[:, 0:192], stacked(pair))
        all_z = times_right(pair, late_part("grad_z"))
        all_y = rows_of(both[64:128])
        settle("side", fx, 2, False)
        settle("rows", fy, 3, False)
        settle("edge", fe, 4, False)
        w_rows, w_z = face_weights()
        flux_z = halves(jnp.concatenate([w * all_z[0:256], w_z * all_z[256:384]], axis=0))
        flux_y = halves(jnp.concatenate([w * all_y[0:256], w_rows * all_y[256:384]], axis=0))
        back = rows_of(dot(late_part("back_y")[:, 0:192], stacked(flux_y)))
        back = back + times_right(flux_z, late_part("back_z"))
        return back[0:256] + back_x(w * rows_of(both[0:64, 0:512])), back[256:384]

    def local_operator(u):
        w = weighted[...]
        pair = halves(u)
        both = dot(late_part("grad_xy")[:, 0:192], stacked(pair))
        flux_z = halves(w * times_right(pair, late_part("grad_z")))
        flux_y = halves(w * rows_of(both[64:128]))
        back = rows_of(dot(late_part("back_y")[:, 0:192], stacked(flux_y)))
        back = back + times_right(flux_z, late_part("back_z"))
        return back + back_x(w * rows_of(both[0:64]))

    def send(table, pair, source, landing, group):
        at = table.index((-pair[0], -pair[1]))

        @pl.when(present(pair))
        def _():
            pltpu.make_async_remote_copy(
                src_ref=source,
                dst_ref=landing.at[at],
                send_sem=s_sem.at[group],
                recv_sem=r_sem.at[group],
                device_id=target(pair),
                device_id_type=MESH,
            ).start()

    counts = {"side": (n_side, (1, 2)), "rows": (near_y, (1, 2)), "edge": (near_x * near_y, (1, 2, 4)), "rims": (n_rims, (1, 2, 3, 4, 6)), "wide": (n_wide, (1, 2, 3, 5, 7, 8, 9, 11, 14)), "reach": (n_reach, (7, 9, 11, 13, 14, 17, 20))}

    def settle(kind, landing, group, sent):
        count, options = counts[kind]
        for one in options:

            @pl.when(count == one)
            def _(one=one):
                copy = pltpu.make_async_remote_copy(
                    src_ref=landing.at[pl.ds(0, one)],
                    dst_ref=landing.at[pl.ds(0, one)],
                    send_sem=s_sem.at[group],
                    recv_sem=r_sem.at[group],
                    device_id=(dom, sub),
                    device_id_type=MESH,
                )
                if sent:
                    copy.wait_send()
                else:
                    copy.wait_recv()

    def pack(refs, fields, xs, vs):
        for f in range(fields):
            ref = refs.at[f]
            faces = {-1: ref[pl.ds(0, 8, stride=8), :], 1: ref[pl.ds(199, 8, stride=8), :]}
            for j in range(4):
                xs[0, f, 8 * j : 8 * j + 8] = ref[64 * j : 64 * j + 8, :]
                xs[1, f, 8 * j : 8 * j + 8] = ref[64 * j + 56 : 64 * j + 64, :]
            for at, (dx, dy) in enumerate(RIMS):
                face = faces[dy]
                if dx < 0:
                    face = jnp.where(sub8 == 7, pltpu.roll(face, 7, 0), 0.0)
                if dx > 0:
                    face = jnp.where(sub8 == 0, pltpu.roll(face, 1, 0), 0.0)
                vs[at, f] = face

    def exchange(xs, vs, xr, vr, group):
        for pair in RIMS:
            if pair[0] != 0:
                send(RIMS, pair, vs.at[RIMS.index(pair)], vr, group + 1)
        for pair in SIDE:
            send(SIDE, pair, xs.at[SIDE.index(pair)], xr, group)
        for pair in RIMS:
            if pair[0] == 0:
                send(RIMS, pair, vs.at[RIMS.index(pair)], vr, group + 1)

    def unpack(refs, fields, xr, vr):
        for f in range(fields):
            ref = refs.at[f]
            for j in range(4):
                ref[64 * j : 64 * j + 8, :] += xr[0, f, 8 * j : 8 * j + 8]
                ref[64 * j + 56 : 64 * j + 64, :] += xr[1, f, 8 * j : 8 * j + 8]
            for dy, start in ((-1, 0), (1, 199)):
                a, b, c = [vr[RIMS.index((dx, dy)), f] for dx in (-1, 0, 1)]
                ref[pl.ds(start, 8, stride=8), :] += a + b + c

    def in_order(ref):
        v = ref[...].reshape(8, 4, 8, 128)
        return jnp.concatenate([v[:, j] for j in range(4)], axis=0).reshape(256, 128)

    table = weights_along(x_at) * weights_along(b_at) * weights_along(c_at)
    loads[0].wait()
    w = in_order(coef) * table
    weighted[...] = w
    loads[1].wait()
    loads[2].wait()
    field[0] = fold(in_order(rhs))
    w4 = w.reshape(4, 8, 8, 128)
    planes = [w4[:, a].reshape(32, 128) for a in range(8)]
    for side in range(2):
        one, two = face_moments(7 * side)
        rows = [weighted[pl.ds(192 * side + b, 8, stride=8), :] for b in range(8)]
        fside[side, 0:32] = sum(float(one[a]) * planes[a] for a in range(8))
        fside[side, 32:64] = sum(float(two[a]) * planes[a] for a in range(8))
        fside[side, 64:96] = planes[7 * side]
        frow[side, 0] = sum(float(one[b]) * rows[b] for b in range(8))
        frow[side, 1] = sum(float(two[b]) * rows[b] for b in range(8))
        frow[side, 2] = rows[7 * side]
    fedge[...] = jnp.zeros_like(fedge)
    for at, (dx, dy) in enumerate(EDGE):
        x_side, y_side = (dx + 1) // 2, (dy + 1) // 2
        spot, line = 31 * y_side, 7 * x_side
        fedge[at, 0:1] = 2.0 * (fside[x_side, spot : spot + 1] + frow[y_side, 0, line : line + 1])
        fedge[at, 1:2] = 2.0 * fside[x_side, 32 + spot : 33 + spot]
        fedge[at, 2:3] = 2.0 * frow[y_side, 1, line : line + 1]
        fedge[at, 3:4] = 4.0 * frow[y_side, 2, line : line + 1]
    pair = halves(w)
    diagonal = rows_of(dot(early_part("square_xy")[:, 0:192], stacked(pair)))
    field[1] = fold(diagonal + times_right(pair, early_part("square_z")))
    pack(field, 2, xs1, vs1)

    pl.semaphore_wait(barrier, (1 + near_x) * (1 + near_y) - 1)
    exchange(xs1, vs1, xr1, vr1, 0)

    def announce(stage):
        for pair in SIDE:

            @pl.when(present(pair))
            def _(pair=pair):
                pl.semaphore_signal(
                    ready.at[stage], inc=1, device_id=target(pair), device_id_type=MESH
                )

    announce(0)
    for at, pair in enumerate(SIDE):
        send(SIDE, pair, fside.at[at], fx, 2)
    for at, pair in enumerate(ROWS):
        send(ROWS, pair, frow.at[at], fy, 3)
    for at, pair in enumerate(EDGE):
        send(EDGE, pair, fedge.at[at], fe, 4)

    loads[3].wait()
    w4 = weighted[...].reshape(4, 8, 8, 128)
    planes = [w4[:, a].reshape(32, 128) for a in range(8)]
    moments = [sum(float(m[a]) * planes[a] for a in range(8) if m[a] != 0.0) for m in MASS]
    moments.append(moments[0] + 2.0 * moments[1] + moments[2])
    stack = jnp.concatenate(moments, axis=0)
    mass_z = jnp.dot(stack, flat_part("moment_m"), precision=HIGHEST, preferred_element_type=F32)
    slope_z = jnp.dot(stack, flat_part("moment_s"), precision=HIGHEST, preferred_element_type=F32)
    none = jnp.zeros((32, 128), F32)
    mine = []
    for at in range(3):
        part = slice(32 * at, 32 * at + 32)
        parts = jnp.concatenate([mass_z[part], slope_z[part], mass_z[96:128], none], axis=0)
        mix = flat_part("mix_minus" if at == 1 else "mix_plus")
        one = jnp.dot(mix, parts, precision=HIGHEST, preferred_element_type=F32)
        pmine[at] = one
        mine.append(one.reshape(3, 8, 128))
    dtile[...] = jnp.where(lane8 < 32, mine[0][1], pltpu.roll(mine[2][1], 32, 1))
    for side, vertex, first in ((0, 0, 1), (1, 4, 0)):
        total = jnp.zeros((8, 128), F32)
        for c in range(3):
            for d in range(2):
                goal = 2 * c + d
                moved = pltpu.roll(mine[c][first + d], (goal - vertex) % 8, 0)
                total = jnp.where(sub8 == goal, moved, total)
        ptile[side] = total
    send(SIDE, (-1, 0), pmine.at[pl.ds(0, 2)], px, 5)
    send(SIDE, (1, 0), pmine.at[pl.ds(1, 2)], px, 5)
    for pair in RIMS:
        send(RIMS, pair, ptile.at[(pair[1] + 1) // 2], pt, 6)
    pl.semaphore_wait(ready.at[0], near_x)
    announce(1)
    for pair in WIDE:
        send(WIDE, pair, dtile, dr, 7)
    loads[4].wait()

    settle("side", xr1, 0, False)
    settle("rims", vr1, 1, False)
    unpack(field, 2, xr1, vr1)

    residual = fmask[...] * field[0]
    inv = fmask[...] / field[1]
    inverse[...] = inv
    field[0] = residual
    theta = 1.1
    delta = 0.9
    sigma = theta / delta
    rho0 = 1.0 / sigma
    rho1 = 1.0 / (2.0 * sigma - rho0)
    step_one = inv * residual / theta
    step[...] = step_one
    held[0] = fold(local_operator(step_one))
    pack(held, 1, xs2, vs2)
    exchange(xs2, vs2, xr2, vr2, 8)

    factor = 2.0 * rho1 / delta
    g = factor * inverse[...] * held[0]
    gfield[...] = g
    start = (1.0 + rho1 * rho0) * step_one + factor * inv * residual
    step[...] = start
    faces = []
    for first in (0, 56):
        for j in range(4):
            faces.append(g[64 * j + first : 64 * j + first + 8])
    rims = [gfield[pl.ds(0, 8, stride=8), :], gfield[pl.ds(199, 8, stride=8), :]]
    corner = jnp.zeros((8, 128), F32)
    for at, (dx, dy) in enumerate(EDGE):
        line = 0 if dx < 0 else 7
        moved = pltpu.roll(rims[(dy + 1) // 2], (at - line) % 8, 0)
        corner = jnp.where(sub8 == at, moved, corner)
    none40 = jnp.zeros((40, 128), F32)
    faces = jnp.concatenate(faces + rims + [corner, none40], axis=0)
    lines = []

    def face_weights():
        for k in range(4):
            one = jnp.zeros((8, 128), F32)
            for at in range(4):
                one = jnp.where(sub8 == at, pltpu.roll(fe[at], (at - k) % 8, 0), one)
            lines.append(one)
        two = [2.0 * fx[0, 64:96], 2.0 * fx[1, 64:96], 2.0 * fy[0, 2], 2.0 * fy[1, 2]]
        w_rows = jnp.concatenate(two + [jnp.zeros((48, 128), F32)], axis=0)
        return w_rows, jnp.concatenate(two + [lines[3], none40], axis=0)

    image, face_image = with_faces(start - g, faces, face_weights)
    defect = residual - fmult[...] * image
    near_w = [fx[0, 0:32], fx[1, 0:32], fy[0, 0], fy[1, 0], lines[0]]
    far_w = [fx[0, 32:64], fx[1, 32:64], fy[0, 1], fy[1, 1]]
    near = jnp.concatenate(near_w, axis=0) * faces[0:88] + face_image[0:88]
    far = jnp.concatenate(far_w, axis=0) * faces[0:80]
    parts = [
        near[0:64], far[0:64], near[64:80], far[64:80], near[80:88],
        lines[1] * corner, lines[2] * corner, jnp.zeros((72, 128), F32),
    ]
    twice_z = jnp.where(((lane8 & 7) == 0) | ((lane8 & 7) == 7), 2.0, 1.0)
    parts = jnp.concatenate(parts, axis=0).reshape(32, 8, 128) * twice_z[None]
    part = dot(late_part("rest_xy"), jnp.concatenate(halves(defect), axis=1))
    part = part + dot(late_part("spill"), jnp.concatenate(halves(parts.reshape(256, 128)), axis=1))
    part = part[0:32, :128] + part[0:32, 128:] + part[32:64, :128]
    coarse = times_right(halves(part), late_part("rest_z"))
    tile = jnp.where(lane8 < 64, jnp.where(lane8 < 32, coarse[0:8], coarse[8:16]), jnp.where(lane8 < 96, coarse[16:24], coarse[24:32]))
    ctile[...] = tile
    pl.semaphore_wait(ready.at[1], near_x)
    for pair in sorted(REACH, key=lambda p: -abs(p[0]) - abs(p[1])):
        send(REACH, pair, ctile, cr, 10)

    settle("side", px, 5, False)
    settle("rims", pt, 6, False)
    settle("wide", dr, 7, False)
    row_low = sub8 < 2
    row_mid = sub8 == 2

    def extend(own, received):
        moved = []
        for dx in (-2, -1, 0, 1, 2):
            mid = own if dx == 0 else received[WIDE.index((dx, 0))]
            below = received[WIDE.index((dx, -1))]
            above = received[WIDE.index((dx, 1))]
            rim = jnp.where(row_low, above, jnp.where(row_mid, 0.0, below))
            moved.append(pltpu.roll(mid, 1, 0) + pltpu.roll(rim, 5, 0))
        return [moved[v + 1] + pltpu.roll(moved[v], 96, 1) for v in range(4)]

    ext_diag = extend(dtile[...], dr)
    vertex_y = sub * 4 + sub8 - 1
    good_yz = (vertex_y > 0) & (vertex_y < 4 * n_sub) & (sub8 < 7) & (lane8 > 0) & (lane8 < 16)
    scales = []
    for v in range(4):
        vertex_x = dom + v - 1
        good = good_yz & (vertex_x > 0) & (vertex_x < n_dom)
        scales.append(jnp.where(good, (2.0 / 3.0) / jnp.where(good, ext_diag[v], 1.0), 0.0))

    def joined(dx, c):
        if dx == 0:
            base = pmine[c]
        else:
            base = px[SIDE.index((dx, 0)), c if dx > 0 else c - 1]
        base = base.reshape(3, 8, 128)
        below = pt[RIMS.index((dx, -1))]
        above = pt[RIMS.index((dx, 1))]
        out = []
        for d in range(3):
            total = base[d]
            if d < 2:
                moved = pltpu.roll(below, (-2 * c - d) % 8, 0)
                total = total + jnp.where(sub8 == 0, moved, 0.0)
            if d > 0:
                moved = pltpu.roll(above, (4 - 2 * c - (d - 1)) % 8, 0)
                total = total + jnp.where(sub8 == 4, moved, 0.0)
            out.append(total)
        return out

    cross = joined(0, 1)
    own_low = [a + b for a, b in zip(joined(0, 0), joined(-1, 2), strict=True)]
    own_high = [a + b for a, b in zip(joined(0, 2), joined(1, 0), strict=True)]
    for vx, blocks in enumerate(
        ((joined(-1, 1), own_low, cross), (cross, own_high, joined(1, 1)))
    ):
        for at in range(3):
            for d in range(3):
                stencil[vx * 9 + at * 3 + d] = blocks[at][d]
    for v in range(4):
        stencil[18 + v] = scales[v]

    settle("side", xr2, 8, False)
    settle("rims", vr2, 9, False)
    unpack(held, 1, xr2, vr2)
    step[...] = step[...] - factor * inverse[...] * held[0]

    settle("side", xr1, 0, True)
    settle("rims", vr1, 1, True)
    settle("side", fx, 2, True)
    settle("rows", fy, 3, True)
    settle("edge", fe, 4, True)
    settle("side", px, 5, True)
    settle("rims", pt, 6, True)
    settle("wide", dr, 7, True)
    settle("side", xr2, 8, True)
    settle("rims", vr2, 9, True)
    settle("reach", cr, 10, False)

    moved = {}
    mid_rows = (sub8 > 3) & (sub8 < 7)
    for dx in range(-3, 4):
        mid = ctile[...] if dx == 0 else cr[REACH.index((dx, 0))]
        below = cr[REACH.index((dx, -1))]
        above = cr[REACH.index((dx, 1))]
        rim = jnp.where(sub8 < 3, above, jnp.where(mid_rows, below, 0.0))
        moved[dx] = mid + pltpu.roll(rim, 4, 0)
    whole = moved[0] + pltpu.roll(jnp.where(lane8 < 96, moved[1], moved[-3]), 32, 1)
    whole = whole + pltpu.roll(jnp.where(lane8 < 64, moved[2], moved[-2]), 64, 1)
    whole = whole + pltpu.roll(jnp.where(lane8 >= 32, moved[-1], moved[3]), 96, 1)
    ext_rhs = [whole] + [pltpu.roll(whole, 128 - 32 * v, 1) for v in (1, 2, 3)]
    scales = [stencil[18 + v] for v in range(4)]
    ones = [scales[v] * ext_rhs[v] for v in range(4)]
    packed = [c + pltpu.roll(c, 31, 1) + pltpu.roll(c, 65, 1) for c in ones]
    around = [[c, pltpu.roll(c, 7, 0), pltpu.roll(c, 6, 0)] for c in packed]
    results = []
    for vx in range(2):
        total = jnp.zeros((8, 128), F32)
        for at in range(3):
            for d in range(3):
                total = total + stencil[vx * 9 + at * 3 + d] * around[vx + at][d]
        image = total + pltpu.roll(total, 96, 1) + pltpu.roll(total, 64, 1)
        one = pltpu.roll(ones[vx + 1], 7, 0)
        scale = pltpu.roll(scales[vx + 1], 7, 0)
        right = pltpu.roll(ext_rhs[vx + 1], 7, 0)
        results.append(one + scale * (right - image))
    pair = halves(jnp.concatenate(results, axis=0))
    nodes = halves(times_right(pair, late_part("prol_z")))
    nodes = jnp.concatenate([nodes[0], nodes[0], nodes[1]], axis=0)
    fine = step[...] + fmask[...] * dot(late_part("prol_xy")[:, 0:48], nodes)
    fine = fine.reshape(4, 8, 8, 128)
    for j in range(4):
        out_ref[:, 8 * j : 8 * j + 8, :] = fine[j]
    copies = halves(dot(jnp.concatenate(pair, axis=1), late_part("copy_z")[:, 0:128]))
    copies = jnp.concatenate([copies[0], copies[0], copies[1]], axis=0)
    copies = dot(late_part("copy_y")[:, 0:48], copies)
    coarse_ref[...] = copies.reshape(2, 8, 128)[:, :, 0:32]

    settle("reach", cr, 10, True)


def finish(fine, coarse, fine_out, coarse_out, sem):
    one = pltpu.make_async_copy(fine, fine_out, sem.at[0])
    two = pltpu.make_async_copy(coarse, coarse_out, sem.at[1])
    one.start()
    two.start()
    one.wait()
    two.wait()


def solution(mesh):
    n_dom = mesh.shape["dom"]
    n_sub = mesh.shape["sub"]

    def shards(rhs_local, coefficient):
        (early_at, early), (late_at, late), (flat_at, flat) = constants(4, 16)
        any_space = pl.BlockSpec(memory_space=pl.ANY)
        vmem = pl.BlockSpec(memory_space=pltpu.VMEM)
        outs = (
            jax.ShapeDtypeStruct((8, 32, 128), F32),
            jax.ShapeDtypeStruct((2, 8, 32), F32),
        )

        def space(*shape):
            return pltpu.VMEM(shape, F32)

        dma = pltpu.SemaphoreType.DMA
        operands = [
            pltpu.with_memory_space_constraint(v, pltpu.HBM)
            for v in (coefficient, rhs_local, early, late, flat)
        ]
        fine, coarse = pl.pallas_call(
            functools.partial(kernel, (early_at, late_at, flat_at), n_dom, n_sub),
            out_shape=outs,
            in_specs=[any_space] * 5,
            out_specs=(vmem, vmem),
            scratch_shapes=[
                space(8, 32, 128),
                space(8, 32, 128),
                pltpu.VMEM(early.shape, BF16),
                pltpu.VMEM(late.shape, BF16),
                pltpu.VMEM(flat.shape, F32),
                space(256, 128),
                space(2, 256, 128),
                space(1, 256, 128),
                space(256, 128),
                space(256, 128),
                space(256, 128),
                space(256, 128),
                space(3, 24, 128),
                space(2, 8, 128),
                space(8, 128),
                space(8, 128),
                space(22, 8, 128),
                space(256, 128),
                space(2, 96, 128),
                space(2, 3, 8, 128),
                space(4, 8, 128),
                space(2, 2, 32, 128),
                space(6, 2, 8, 128),
                space(2, 1, 32, 128),
                space(6, 1, 8, 128),
                space(2, 2, 32, 128),
                space(6, 2, 8, 128),
                space(2, 1, 32, 128),
                space(6, 1, 8, 128),
                space(2, 2, 24, 128),
                space(6, 8, 128),
                space(14, 8, 128),
                space(20, 8, 128),
                space(2, 96, 128),
                space(2, 3, 8, 128),
                space(4, 8, 128),
                dma((5,)),
                dma((11,)),
                dma((11,)),
                pltpu.SemaphoreType.REGULAR((2,)),
            ],
            compiler_params=pltpu.CompilerParams(
                collective_id=0, has_side_effects=True, vmem_limit_bytes=8 * 2**20
            ),
        )(*operands)
        return pl.pallas_call(
            finish,
            out_shape=outs,
            in_specs=[vmem, vmem],
            out_specs=(any_space, any_space),
            scratch_shapes=[dma((2,))],
            compiler_params=pltpu.CompilerParams(vmem_limit_bytes=2**20),
        )(fine, coarse)

    return jax.shard_map(
        shards,
        mesh=mesh,
        in_specs=(P("dom", "sub", None), P("dom", "sub", None)),
        out_specs=(P("dom", "sub", None), P("dom", "sub", None)),
        check_vma=False,
    )
```

```python
import functools

import jax
import jax.numpy as jnp
import numpy as np
from jax import lax
from jax.experimental import pallas as pl
from jax.experimental.pallas import tpu as pltpu
from jax.sharding import PartitionSpec as P

MESH = pl.DeviceIdType.MESH
HIGHEST = lax.Precision.HIGHEST
F32 = jnp.float32
BF16 = jnp.bfloat16

NEAR = [(dx, dy) for dx in (-1, 0, 1) for dy in (-1, 0, 1) if (dx, dy) != (0, 0)]
WIDE = [(dx, dy) for dx in (-2, -1, 0, 1, 2) for dy in (-1, 0, 1) if (dx, dy) != (0, 0)]
REACH = [(dx, dy) for dx in range(-3, 4) for dy in (-1, 0, 1) if (dx, dy) != (0, 0)]
SIDE = [pair for pair in NEAR if pair[1] == 0]
RIMS = [pair for pair in NEAR if pair[1] != 0]
EDGE = [pair for pair in RIMS if pair[0] != 0]
ROWS = [pair for pair in RIMS if pair[0] == 0]


def opposite(table, pair):
    return table.index((-pair[0], -pair[1]))


def tables():
    degree = 7
    points = np.array(
        [
            -1.0,
            -0.8717401485096066,
            -0.5917001814331423,
            -0.2092992179024789,
            0.2092992179024789,
            0.5917001814331423,
            0.8717401485096066,
            1.0,
        ]
    )
    previous = np.ones(points.shape)
    values = points.copy()
    for level in range(1, degree):
        following = ((2 * level + 1) * points * values - level * previous) / (level + 1)
        previous = values
        values = following
    weights = 2.0 / (degree * (degree + 1) * values**2)
    derivative = np.zeros((8, 8))
    for row_at in range(8):
        for col_at in range(8):
            if row_at != col_at:
                derivative[row_at, col_at] = values[row_at] / (
                    values[col_at] * (points[row_at] - points[col_at])
                )
    derivative[0, 0] = -degree * (degree + 1) / 4.0
    derivative[7, 7] = degree * (degree + 1) / 4.0
    interp = np.stack([(1.0 - points) / 2.0, (1.0 + points) / 2.0], axis=1)
    return derivative, weights, interp


DER, WTS, INT = tables()
TWICE = np.array([2.0, 1.0, 1.0, 1.0, 1.0, 1.0, 1.0, 2.0])
HATS = [TWICE * INT[:, 0], TWICE * INT[:, 1]]


def face_moments(face):
    near = 0 if face == 0 else 1
    return [DER[:, face] * (DER @ HATS[i]) for i in (near, 1 - near)]
MASS = [INT[:, 0] * INT[:, 0], INT[:, 0] * INT[:, 1], INT[:, 1] * INT[:, 1]]


def moment_maps(elements, order, slope):
    maps = np.zeros((len(order), elements + 1, 8 * elements))
    for at, offset in enumerate(order):
        for e in range(elements):
            nodes = slice(8 * e, 8 * e + 8)
            if offset == 0:
                maps[at, e, nodes] += 0.25 if slope else MASS[0]
                maps[at, e + 1, nodes] += 0.25 if slope else MASS[2]
            elif offset == 1:
                maps[at, e, nodes] += -0.25 if slope else MASS[1]
            else:
                maps[at, e + 1, nodes] += -0.25 if slope else MASS[1]
    return maps


def unique_interp(elements):
    maps = np.zeros((8 * elements, elements + 1))
    for e in range(elements):
        maps[8 * e : 8 * e + 8, e] = INT[:, 0]
        maps[8 * e : 8 * e + 8, e + 1] = INT[:, 1]
    return maps


def unique_copies(elements):
    maps = np.zeros((2 * elements, elements + 1))
    for e in range(elements):
        maps[2 * e, e] = 1.0
        maps[2 * e + 1, e + 1] = 1.0
    return maps


def split(matrix):
    high = jnp.asarray(matrix, F32).astype(BF16)
    return high, (jnp.asarray(matrix, F32) - high.astype(F32)).astype(BF16)


def right_halves(matrix):
    high, low = split(matrix)
    top = jnp.concatenate([high, low], axis=1)
    return jnp.concatenate([top, jnp.concatenate([high, jnp.zeros_like(low)], axis=1)], axis=0)


def left_halves(matrix):
    high, low = split(matrix)
    return jnp.concatenate([high, low, high], axis=1)


def wide(block):
    return jnp.pad(block, ((0, 0), (0, 256 - block.shape[1])))


def spots_of(parts):
    spots = {}
    at = 0
    for name, block in parts.items():
        spots[name] = (at, block.shape[0])
        at += block.shape[0]
    return spots, jnp.concatenate(list(parts.values()))


def constants(ey, ez):
    square = DER * DER
    eye8 = np.eye(8)
    eye = np.eye(ez)
    early = {
        "square_z": right_halves(np.kron(eye, square)),
        "square_xy": wide(left_halves(np.kron(square.T, eye8) + np.kron(eye8, square.T))),
    }
    low = unique_interp(ey)
    place = np.zeros((4, 8, 8, 16))
    for side in range(2):
        place[..., 8 * side : 8 * side + ey + 1] = (
            INT[:, side][None, :, None, None] * low.reshape(ey, 8, ey + 1)[:, None]
        )
    place = place.reshape(256, 16)
    rest_z = np.zeros((128, 128))
    rest_z[:, : ez + 1] = unique_interp(ez)
    for at in (32, 64, 96):
        rest_z[:, at : at + ez + 1] = unique_interp(ez)
    prol_z = np.zeros((128, 128))
    prol_z[: ez + 1, :] = unique_interp(ez).T
    copy_z = np.zeros((128, 128))
    copy_z[: ez + 1, : 2 * ez] = unique_copies(ez).T
    copy_y = np.zeros((16, 16))
    for side in range(2):
        copy_y[8 * side : 8 * side + 8, 8 * side : 8 * side + ey + 1] = unique_copies(ey)
    own = np.zeros((32, 256))
    for side in range(2):
        own[8 * (side + 1) + 1 : 8 * (side + 1) + 2 + ey] = place.T[8 * side : 8 * side + ey + 1]
    rest_xy = split(own)
    spill = np.zeros((4, 8, 256))
    low_m = low * np.tile(TWICE, ey)[:, None]
    for side in range(2):
        for at, v in ((0, 1 + side), (64, 3 * side)):
            spill[v, 1 : ey + 2, at + 32 * side : at + 32 * side + 32] = low_m.T
        for at, r in ((128, 1 + ey * side), (144, (ey + 2) * side)):
            for vx in range(2):
                spill[1 + vx, r, at + 8 * side : at + 8 * side + 8] = HATS[vx]
    for at, (dx, dy) in enumerate(EDGE):
        near_v, far_v = (1, 0) if dx < 0 else (2, 3)
        near_r, far_r = (1, 0) if dy < 0 else (1 + ey, 2 + ey)
        spill[near_v, near_r, 160 + at] = 1.0
        spill[far_v, near_r, 168 + at] = 1.0
        spill[near_v, far_r, 176 + at] = 1.0
    spill = split(spill.reshape(32, 256))
    rest_z = np.zeros((128, 128))
    rest_z[:, : ez + 1] = unique_interp(ez)
    for at in (32, 64, 96):
        rest_z[:, at : at + ez + 1] = unique_interp(ez)
    prol_z = np.zeros((128, 128))
    prol_z[: ez + 1, :] = unique_interp(ez).T
    copy_z = np.zeros((128, 128))
    copy_z[: ez + 1, : 2 * ez] = unique_copies(ez).T
    copy_y = np.zeros((16, 16))
    for side in range(2):
        copy_y[8 * side : 8 * side + 8, 8 * side : 8 * side + ey + 1] = unique_copies(ey)
    own = np.zeros((32, 256))
    for side in range(2):
        own[8 * (side + 1) + 1 : 8 * (side + 1) + 2 + ey] = place.T[8 * side : 8 * side + ey + 1]
    rest_xy = split(own)
    spill = np.zeros((4, 8, 256))
    low_m = low * np.tile(TWICE, ey)[:, None]
    for side in range(2):
        for at, v in ((0, 1 + side), (64, 3 * side)):
            spill[v, 1 : ey + 2, at + 32 * side : at + 32 * side + 32] = low_m.T
        for at, r in ((128, 1 + ey * side), (144, (ey + 2) * side)):
            for vx in range(2):
                spill[1 + vx, r, at + 8 * side : at + 8 * side + 8] = HATS[vx]
    for at, (dx, dy) in enumerate(EDGE):
        near_v, far_v = (1, 0) if dx < 0 else (2, 3)
        near_r, far_r = (1, 0) if dy < 0 else (1 + ey, 2 + ey)
        spill[near_v, near_r, 160 + at] = 1.0
        spill[far_v, near_r, 168 + at] = 1.0
        spill[near_v, far_r, 176 + at] = 1.0
    spill = split(spill.reshape(32, 256))
    moment_y = np.zeros((2, 2, 8, 8, 8))
    for side in range(2):
        for at, one in enumerate(face_moments(7 * side)):
            moment_y[side, at] = np.eye(8)[:, :, None] * one[None, None, :]
    moment_y = moment_y.reshape(32, 64)
    late = {
        "grad_z": right_halves(np.kron(eye, DER.T)),
        "back_z": right_halves(np.kron(eye, DER)),
        "rest_z": right_halves(rest_z),
        "prol_z": right_halves(prol_z),
        "copy_z": wide(jnp.concatenate([split(copy_z)[0]] * 2)),
        "prol_xy": wide(left_halves(place)),
        "grad_xy": wide(
            jnp.concatenate([left_halves(np.kron(DER, eye8)), left_halves(np.kron(eye8, DER))])
        ),
        "back_y": wide(left_halves(np.kron(eye8, DER.T))),
        "rest_xy": jnp.concatenate([rest_xy[0], rest_xy[1]]),
        "spill": jnp.concatenate([spill[0], spill[1]]),
        "copy_y": wide(left_halves(copy_y)),
    }
    flat = {}
    for name, slope in (("moment_m", False), ("moment_s", True)):
        block = np.zeros((128, 128))
        for at, one in enumerate(moment_maps(ez, (0, 1, -1), slope)):
            block[:, 32 * at : 32 * at + ez + 1] = one.T
        flat[name] = jnp.asarray(block, F32)
    order_y = (-1, 0, 1)
    mass_y = np.zeros((3, 8, 8 * ey))
    mass_y[:, : ey + 1] = moment_maps(ey, order_y, False)
    slope_y = np.zeros((3, 8, 8 * ey))
    slope_y[:, : ey + 1] = moment_maps(ey, order_y, True)
    mass_y = mass_y.reshape(24, 8 * ey)
    slope_y = slope_y.reshape(24, 8 * ey)
    for name, sign in (("mix_plus", 0.25), ("mix_minus", -0.25)):
        block = np.zeros((24, 128))
        block[:, : 24 * ey] = np.concatenate([slope_y, mass_y, sign * mass_y], axis=1)
        flat[name] = jnp.asarray(block, F32)
    return spots_of(early), spots_of(late), spots_of(flat)


def kernel(
    tables_at, n_dom, n_sub, coef_hbm, rhs_hbm, early_hbm, late_hbm, flat_hbm,
    out_ref, coarse_ref,
    coef, rhs, early, late, flat, weighted, field, held, fmask, fmult, inverse, step,
    pmine, ptile, dtile, ctile, stencil, gfield, fside, frow, fedge,
    xs1, vs1, es1, xs2, vs2, es2,
    xr1, vr1, er1, xr2, vr2, er2, px, pt, dr, cr, fx, fy, fe,
    load_sem, s_sem, r_sem, ready,
):
    early_at, late_at, flat_at = tables_at
    dom = lax.axis_index("dom")
    sub = lax.axis_index("sub")

    loads = []
    for at, (source, dest) in enumerate(
        ((coef_hbm, coef), (early_hbm, early), (rhs_hbm, rhs), (flat_hbm, flat), (late_hbm, late))
    ):
        load = pltpu.make_async_copy(source, dest, load_sem.at[at])
        load.start()
        loads.append(load)

    def present(pair):
        dx, dy = pair
        conds = []
        if dx < 0:
            conds.append(dom >= -dx)
        if dx > 0:
            conds.append(dom < n_dom - dx)
        if dy < 0:
            conds.append(sub >= 1)
        if dy > 0:
            conds.append(sub < n_sub - 1)
        return functools.reduce(jnp.logical_and, conds)

    def target(pair):
        return (dom + pair[0], sub + pair[1])

    for buffer in (xr1, vr1, er1, xr2, vr2, er2, px, pt, dr, cr, fx, fy, fe):
        buffer[...] = jnp.zeros_like(buffer)

    barrier = pltpu.get_barrier_semaphore()
    for pair in NEAR:

        @pl.when(present(pair))
        def _(pair=pair):
            pl.semaphore_signal(barrier, inc=1, device_id=target(pair), device_id_type=MESH)

    near_x = jnp.where(dom >= 1, 1, 0) + jnp.where(dom < n_dom - 1, 1, 0)
    near_y = jnp.where(sub >= 1, 1, 0) + jnp.where(sub < n_sub - 1, 1, 0)
    far_x = near_x + jnp.where(dom >= 2, 1, 0) + jnp.where(dom < n_dom - 2, 1, 0)
    n_side = near_x
    n_rims = near_y * (1 + near_x)
    n_wide = (1 + far_x) * (1 + near_y) - 1
    reach_x = far_x + jnp.where(dom >= 3, 1, 0) + jnp.where(dom < n_dom - 3, 1, 0)
    n_reach = (1 + reach_x) * (1 + near_y) - 1

    row = lax.broadcasted_iota(jnp.int32, (256, 128), 0)
    lane = lax.broadcasted_iota(jnp.int32, (256, 128), 1)
    x_at = lax.shift_right_logical(row, 3) & 7
    b_at = row & 7
    c_at = lane & 7
    place_x = dom * 8 + x_at
    place_y = sub * 32 + lax.shift_right_logical(row, 6) * 8 + b_at
    inside = (
        (place_x > 0) & (place_x < 8 * n_dom - 1)
        & (place_y > 0) & (place_y < 32 * n_sub - 1)
        & (lane > 0) & (lane < 127)
    )
    mask = jnp.where(inside, 1.0, 0.0)
    fmask[...] = mask
    twice = jnp.where((x_at == 0) | (x_at == 7), 2.0, 1.0)
    twice = twice * jnp.where((b_at == 0) | (b_at == 7), 2.0, 1.0)
    fmult[...] = mask * twice * jnp.where((c_at == 0) | (c_at == 7), 2.0, 1.0)

    lane8 = lax.broadcasted_iota(jnp.int32, (8, 128), 1)
    sub8 = lax.broadcasted_iota(jnp.int32, (8, 128), 0)
    z_low = ((lane8 & 7) == 0) & (lane8 > 0)
    z_high = ((lane8 & 7) == 7) & (lane8 < 127)

    def weights_along(spot):
        value = jnp.where((spot == 0) | (spot == 7), float(WTS[0]), float(WTS[1]))
        value = jnp.where((spot == 2) | (spot == 5), float(WTS[2]), value)
        return jnp.where((spot == 3) | (spot == 4), float(WTS[3]), value)

    def fold(v):
        v = v.reshape(32, 8, 128)
        v = v + jnp.where(
            z_high[None], pltpu.roll(v, 127, 2),
            jnp.where(z_low[None], pltpu.roll(v, 1, 2), 0.0),
        )
        up = pltpu.roll(v, 1, 1)
        down = pltpu.roll(v, 7, 1)
        none = jnp.zeros((8, 8, 128), F32)
        up = jnp.concatenate([none, up[:24]], axis=0)
        down = jnp.concatenate([down[8:], none], axis=0)
        v = v + jnp.where((sub8 == 0)[None], up, jnp.where((sub8 == 7)[None], down, 0.0))
        return v.reshape(256, 128)

    def halves(v):
        high = v.astype(BF16)
        return high, (v - high.astype(F32)).astype(BF16)

    def dot(left, right):
        return jnp.dot(left, right, preferred_element_type=F32)

    def early_part(name):
        start, count = early_at[name]
        return early[start : start + count, :]

    def late_part(name):
        start, count = late_at[name]
        return late[start : start + count, :]

    def flat_part(name):
        start, count = flat_at[name]
        return flat[start : start + count, :]

    def times_right(pair, matrix):
        both = dot(jnp.concatenate(pair, axis=1), matrix)
        return both[:, :128] + both[:, 128:]

    def stacked(pair):
        high, low = [
            jnp.concatenate([v[at : at + 64] for at in range(0, v.shape[0], 64)], axis=1) for v in pair
        ]
        return jnp.concatenate([high, high, low], axis=0)

    def rows_of(v):
        return jnp.concatenate([v[:, at : at + 128] for at in range(0, v.shape[1], 128)], axis=0)

    def back_x(v):
        v = v.reshape(4, 8, 8, 128)
        matrix = DER.T
        even = [v[:, b] + v[:, 7 - b] for b in range(4)]
        odd = [v[:, b] - v[:, 7 - b] for b in range(4)]
        planes = [None] * 8
        for a in range(4):
            p = sum(float(matrix[a, b] + matrix[a, 7 - b]) / 2 * even[b] for b in range(4))
            q = sum(float(matrix[a, b] - matrix[a, 7 - b]) / 2 * odd[b] for b in range(4))
            planes[a] = p + q
            planes[7 - a] = q - p
        return jnp.stack(planes, axis=1).reshape(256, 128)

    def with_faces(u, faces, w_rows, w_z):
        w = weighted[...]
        pair = halves(jnp.concatenate([u, faces], axis=0))
        both = dot(late_part("grad_xy")[:, 0:192], stacked(pair))
        all_z = times_right(pair, late_part("grad_z"))
        all_y = rows_of(both[64:128])
        flux_z = halves(jnp.concatenate([w * all_z[0:256], w_z * all_z[256:384]], axis=0))
        flux_y = halves(jnp.concatenate([w * all_y[0:256], w_rows * all_y[256:384]], axis=0))
        back = rows_of(dot(late_part("back_y")[:, 0:192], stacked(flux_y)))
        back = back + times_right(flux_z, late_part("back_z"))
        return back[0:256] + back_x(w * rows_of(both[0:64, 0:512])), back[256:384]

    def local_operator(u):
        w = weighted[...]
        pair = halves(u)
        both = dot(late_part("grad_xy")[:, 0:192], stacked(pair))
        flux_z = halves(w * times_right(pair, late_part("grad_z")))
        flux_y = halves(w * rows_of(both[64:128]))
        back = rows_of(dot(late_part("back_y")[:, 0:192], stacked(flux_y)))
        back = back + times_right(flux_z, late_part("back_z"))
        return back + back_x(w * rows_of(both[0:64]))

    def send(table, pair, source, landing, group):
        at = table.index((-pair[0], -pair[1]))

        @pl.when(present(pair))
        def _():
            pltpu.make_async_remote_copy(
                src_ref=source,
                dst_ref=landing.at[at],
                send_sem=s_sem.at[group],
                recv_sem=r_sem.at[group],
                device_id=target(pair),
                device_id_type=MESH,
            ).start()

    counts = {"side": (n_side, (1, 2)), "rows": (near_y, (1, 2)), "edge": (near_x * near_y, (1, 2, 4)), "rims": (n_rims, (1, 2, 3, 4, 6)), "wide": (n_wide, (1, 2, 3, 5, 7, 8, 9, 11, 14)), "reach": (n_reach, (7, 9, 11, 13, 14, 17, 20))}

    def settle(kind, landing, group, sent):
        count, options = counts[kind]
        for one in options:

            @pl.when(count == one)
            def _(one=one):
                copy = pltpu.make_async_remote_copy(
                    src_ref=landing.at[pl.ds(0, one)],
                    dst_ref=landing.at[pl.ds(0, one)],
                    send_sem=s_sem.at[group],
                    recv_sem=r_sem.at[group],
                    device_id=(dom, sub),
                    device_id_type=MESH,
                )
                if sent:
                    copy.wait_send()
                else:
                    copy.wait_recv()

    def pack(refs, fields, xs, vs, es):
        for f in range(fields):
            ref = refs.at[f]
            faces = {-1: ref[pl.ds(0, 8, stride=8), :], 1: ref[pl.ds(199, 8, stride=8), :]}
            for j in range(4):
                xs[0, f, 8 * j : 8 * j + 8] = ref[64 * j : 64 * j + 8, :]
                xs[1, f, 8 * j : 8 * j + 8] = ref[64 * j + 56 : 64 * j + 64, :]
            for at, (_, dy) in enumerate(ROWS):
                vs[at, f] = faces[dy]
            for at, (dx, dy) in enumerate(EDGE):
                line = 0 if dx < 0 else 7
                es[at, f] = faces[dy][line : line + 1]

    def exchange(xs, vs, es, xr, vr, er, group, edge_group):
        for pair in EDGE:
            send(EDGE, pair, es.at[EDGE.index(pair)], er, edge_group)
        for pair in SIDE:
            send(SIDE, pair, xs.at[SIDE.index(pair)], xr, group)
        for pair in ROWS:
            send(ROWS, pair, vs.at[ROWS.index(pair)], vr, group + 1)

    def unpack(refs, fields, xr, vr, er):
        for f in range(fields):
            ref = refs.at[f]
            for j in range(4):
                ref[64 * j : 64 * j + 8, :] += xr[0, f, 8 * j : 8 * j + 8]
                ref[64 * j + 56 : 64 * j + 64, :] += xr[1, f, 8 * j : 8 * j + 8]
            for dy, start in ((-1, 0), (1, 199)):
                extra = vr[ROWS.index((0, dy)), f]
                low = er[EDGE.index((-1, dy)), f]
                high = er[EDGE.index((1, dy)), f]
                extra = extra + jnp.where(sub8 == 0, low, jnp.where(sub8 == 7, high, 0.0))
                ref[pl.ds(start, 8, stride=8), :] += extra

    def in_order(ref):
        v = ref[...].reshape(8, 4, 8, 128)
        return jnp.concatenate([v[:, j] for j in range(4)], axis=0).reshape(256, 128)

    table = weights_along(x_at) * weights_along(b_at) * weights_along(c_at)
    loads[0].wait()
    w = in_order(coef) * table
    weighted[...] = w
    loads[1].wait()
    loads[2].wait()
    field[0] = fold(in_order(rhs))
    w4 = w.reshape(4, 8, 8, 128)
    planes = [w4[:, a].reshape(32, 128) for a in range(8)]
    for side in range(2):
        one, two = face_moments(7 * side)
        rows = [weighted[pl.ds(192 * side + b, 8, stride=8), :] for b in range(8)]
        fside[side, 0:32] = sum(float(one[a]) * planes[a] for a in range(8))
        fside[side, 32:64] = sum(float(two[a]) * planes[a] for a in range(8))
        fside[side, 64:96] = planes[7 * side]
        frow[side, 0] = sum(float(one[b]) * rows[b] for b in range(8))
        frow[side, 1] = sum(float(two[b]) * rows[b] for b in range(8))
        frow[side, 2] = rows[7 * side]
    fedge[...] = jnp.zeros_like(fedge)
    for at, (dx, dy) in enumerate(EDGE):
        x_side, y_side = (dx + 1) // 2, (dy + 1) // 2
        spot, line = 31 * y_side, 7 * x_side
        fedge[at, 0:1] = 2.0 * (fside[x_side, spot : spot + 1] + frow[y_side, 0, line : line + 1])
        fedge[at, 1:2] = 2.0 * fside[x_side, 32 + spot : 33 + spot]
        fedge[at, 2:3] = 2.0 * frow[y_side, 1, line : line + 1]
        fedge[at, 3:4] = 4.0 * frow[y_side, 2, line : line + 1]
    pair = halves(w)
    diagonal = rows_of(dot(early_part("square_xy")[:, 0:192], stacked(pair)))
    field[1] = fold(diagonal + times_right(pair, early_part("square_z")))
    pack(field, 2, xs1, vs1, es1)

    pl.semaphore_wait(barrier, (1 + near_x) * (1 + near_y) - 1)
    exchange(xs1, vs1, es1, xr1, vr1, er1, 0, 11)

    def announce(stage):
        for pair in SIDE:

            @pl.when(present(pair))
            def _(pair=pair):
                pl.semaphore_signal(
                    ready.at[stage], inc=1, device_id=target(pair), device_id_type=MESH
                )

    announce(0)
    for at, pair in enumerate(SIDE):
        send(SIDE, pair, fside.at[at], fx, 2)
    for at, pair in enumerate(ROWS):
        send(ROWS, pair, frow.at[at], fy, 3)
    for at, pair in enumerate(EDGE):
        send(EDGE, pair, fedge.at[at], fe, 4)

    loads[3].wait()
    w4 = weighted[...].reshape(4, 8, 8, 128)
    planes = [w4[:, a].reshape(32, 128) for a in range(8)]
    moments = [sum(float(m[a]) * planes[a] for a in range(8) if m[a] != 0.0) for m in MASS]
    moments.append(moments[0] + 2.0 * moments[1] + moments[2])
    stack = jnp.concatenate(moments, axis=0)
    mass_z = jnp.dot(stack, flat_part("moment_m"), precision=HIGHEST, preferred_element_type=F32)
    slope_z = jnp.dot(stack, flat_part("moment_s"), precision=HIGHEST, preferred_element_type=F32)
    none = jnp.zeros((32, 128), F32)
    mine = []
    for at in range(3):
        part = slice(32 * at, 32 * at + 32)
        parts = jnp.concatenate([mass_z[part], slope_z[part], mass_z[96:128], none], axis=0)
        mix = flat_part("mix_minus" if at == 1 else "mix_plus")
        one = jnp.dot(mix, parts, precision=HIGHEST, preferred_element_type=F32)
        pmine[at] = one
        mine.append(one.reshape(3, 8, 128))
    dtile[...] = jnp.where(lane8 < 32, mine[0][1], pltpu.roll(mine[2][1], 32, 1))
    for side, vertex, first in ((0, 0, 1), (1, 4, 0)):
        total = jnp.zeros((8, 128), F32)
        for c in range(3):
            for d in range(2):
                goal = 2 * c + d
                moved = pltpu.roll(mine[c][first + d], (goal - vertex) % 8, 0)
                total = jnp.where(sub8 == goal, moved, total)
        ptile[side] = total
    send(SIDE, (-1, 0), pmine.at[pl.ds(0, 2)], px, 5)
    send(SIDE, (1, 0), pmine.at[pl.ds(1, 2)], px, 5)
    for pair in RIMS:
        send(RIMS, pair, ptile.at[(pair[1] + 1) // 2], pt, 6)
    pl.semaphore_wait(ready.at[0], near_x)
    announce(1)
    for pair in WIDE:
        send(WIDE, pair, dtile, dr, 7)
    loads[4].wait()

    settle("side", xr1, 0, False)
    settle("rows", vr1, 1, False)
    settle("edge", er1, 11, False)
    unpack(field, 2, xr1, vr1, er1)

    residual = fmask[...] * field[0]
    inv = fmask[...] / field[1]
    inverse[...] = inv
    field[0] = residual
    theta = 1.1
    delta = 0.9
    sigma = theta / delta
    rho0 = 1.0 / sigma
    rho1 = 1.0 / (2.0 * sigma - rho0)
    step_one = inv * residual / theta
    step[...] = step_one
    held[0] = fold(local_operator(step_one))
    pack(held, 1, xs2, vs2, es2)
    exchange(xs2, vs2, es2, xr2, vr2, er2, 8, 12)

    factor = 2.0 * rho1 / delta
    g = factor * inverse[...] * held[0]
    gfield[...] = g
    start = (1.0 + rho1 * rho0) * step_one + factor * inv * residual
    step[...] = start
    settle("side", fx, 2, False)
    settle("rows", fy, 3, False)
    settle("edge", fe, 4, False)
    faces = []
    for first in (0, 56):
        for j in range(4):
            faces.append(g[64 * j + first : 64 * j + first + 8])
    rims = [gfield[pl.ds(0, 8, stride=8), :], gfield[pl.ds(199, 8, stride=8), :]]
    corner = jnp.zeros((8, 128), F32)
    lines = [jnp.zeros((8, 128), F32) for _ in range(4)]
    for at, (dx, dy) in enumerate(EDGE):
        line = 0 if dx < 0 else 7
        moved = pltpu.roll(rims[(dy + 1) // 2], (at - line) % 8, 0)
        corner = jnp.where(sub8 == at, moved, corner)
        given = fe[at]
        for k in range(4):
            lines[k] = jnp.where(sub8 == at, pltpu.roll(given, (at - k) % 8, 0), lines[k])
    none40 = jnp.zeros((40, 128), F32)
    faces = jnp.concatenate(faces + rims + [corner, none40], axis=0)
    two = [2.0 * fx[0, 64:96], 2.0 * fx[1, 64:96], 2.0 * fy[0, 2], 2.0 * fy[1, 2]]
    w_rows = jnp.concatenate(two + [jnp.zeros((48, 128), F32)], axis=0)
    w_z = jnp.concatenate(two + [lines[3], none40], axis=0)
    image, face_image = with_faces(start - g, faces, w_rows, w_z)
    defect = residual - fmult[...] * image
    near_w = [fx[0, 0:32], fx[1, 0:32], fy[0, 0], fy[1, 0], lines[0]]
    far_w = [fx[0, 32:64], fx[1, 32:64], fy[0, 1], fy[1, 1]]
    near = jnp.concatenate(near_w, axis=0) * faces[0:88] + face_image[0:88]
    far = jnp.concatenate(far_w, axis=0) * faces[0:80]
    parts = [
        near[0:64], far[0:64], near[64:80], far[64:80], near[80:88],
        lines[1] * corner, lines[2] * corner, jnp.zeros((72, 128), F32),
    ]
    twice_z = jnp.where(((lane8 & 7) == 0) | ((lane8 & 7) == 7), 2.0, 1.0)
    parts = jnp.concatenate(parts, axis=0).reshape(32, 8, 128) * twice_z[None]
    part = dot(late_part("rest_xy"), jnp.concatenate(halves(defect), axis=1))
    part = part + dot(late_part("spill"), jnp.concatenate(halves(parts.reshape(256, 128)), axis=1))
    part = part[0:32, :128] + part[0:32, 128:] + part[32:64, :128]
    coarse = times_right(halves(part), late_part("rest_z"))
    tile = jnp.where(lane8 < 64, jnp.where(lane8 < 32, coarse[0:8], coarse[8:16]), jnp.where(lane8 < 96, coarse[16:24], coarse[24:32]))
    ctile[...] = tile
    pl.semaphore_wait(ready.at[1], near_x)
    for pair in sorted(REACH, key=lambda p: -abs(p[0]) - abs(p[1])):
        send(REACH, pair, ctile, cr, 10)

    settle("side", px, 5, False)
    settle("rims", pt, 6, False)
    settle("wide", dr, 7, False)
    row_low = sub8 < 2
    row_mid = sub8 == 2

    def extend(own, received):
        moved = []
        for dx in (-2, -1, 0, 1, 2):
            mid = own if dx == 0 else received[WIDE.index((dx, 0))]
            below = received[WIDE.index((dx, -1))]
            above = received[WIDE.index((dx, 1))]
            rim = jnp.where(row_low, above, jnp.where(row_mid, 0.0, below))
            moved.append(pltpu.roll(mid, 1, 0) + pltpu.roll(rim, 5, 0))
        return [moved[v + 1] + pltpu.roll(moved[v], 96, 1) for v in range(4)]

    ext_diag = extend(dtile[...], dr)
    vertex_y = sub * 4 + sub8 - 1
    good_yz = (vertex_y > 0) & (vertex_y < 4 * n_sub) & (sub8 < 7) & (lane8 > 0) & (lane8 < 16)
    scales = []
    for v in range(4):
        vertex_x = dom + v - 1
        good = good_yz & (vertex_x > 0) & (vertex_x < n_dom)
        scales.append(jnp.where(good, (2.0 / 3.0) / jnp.where(good, ext_diag[v], 1.0), 0.0))

    def joined(dx, c):
        if dx == 0:
            base = pmine[c]
        else:
            base = px[SIDE.index((dx, 0)), c if dx > 0 else c - 1]
        base = base.reshape(3, 8, 128)
        below = pt[RIMS.index((dx, -1))]
        above = pt[RIMS.index((dx, 1))]
        out = []
        for d in range(3):
            total = base[d]
            if d < 2:
                moved = pltpu.roll(below, (-2 * c - d) % 8, 0)
                total = total + jnp.where(sub8 == 0, moved, 0.0)
            if d > 0:
                moved = pltpu.roll(above, (4 - 2 * c - (d - 1)) % 8, 0)
                total = total + jnp.where(sub8 == 4, moved, 0.0)
            out.append(total)
        return out

    cross = joined(0, 1)
    own_low = [a + b for a, b in zip(joined(0, 0), joined(-1, 2), strict=True)]
    own_high = [a + b for a, b in zip(joined(0, 2), joined(1, 0), strict=True)]
    for vx, blocks in enumerate(
        ((joined(-1, 1), own_low, cross), (cross, own_high, joined(1, 1)))
    ):
        for at in range(3):
            for d in range(3):
                stencil[vx * 9 + at * 3 + d] = blocks[at][d]
    for v in range(4):
        stencil[18 + v] = scales[v]

    settle("side", xr2, 8, False)
    settle("rows", vr2, 9, False)
    settle("edge", er2, 12, False)
    unpack(held, 1, xr2, vr2, er2)
    step[...] = step[...] - factor * inverse[...] * held[0]

    settle("side", xr1, 0, True)
    settle("rows", vr1, 1, True)
    settle("edge", er1, 11, True)
    settle("side", fx, 2, True)
    settle("rows", fy, 3, True)
    settle("edge", fe, 4, True)
    settle("side", px, 5, True)
    settle("rims", pt, 6, True)
    settle("wide", dr, 7, True)
    settle("side", xr2, 8, True)
    settle("rows", vr2, 9, True)
    settle("edge", er2, 12, True)
    settle("reach", cr, 10, False)

    moved = {}
    mid_rows = (sub8 > 3) & (sub8 < 7)
    for dx in range(-3, 4):
        mid = ctile[...] if dx == 0 else cr[REACH.index((dx, 0))]
        below = cr[REACH.index((dx, -1))]
        above = cr[REACH.index((dx, 1))]
        rim = jnp.where(sub8 < 3, above, jnp.where(mid_rows, below, 0.0))
        moved[dx] = mid + pltpu.roll(rim, 4, 0)
    whole = moved[0] + pltpu.roll(jnp.where(lane8 < 96, moved[1], moved[-3]), 32, 1)
    whole = whole + pltpu.roll(jnp.where(lane8 < 64, moved[2], moved[-2]), 64, 1)
    whole = whole + pltpu.roll(jnp.where(lane8 >= 32, moved[-1], moved[3]), 96, 1)
    ext_rhs = [whole] + [pltpu.roll(whole, 128 - 32 * v, 1) for v in (1, 2, 3)]
    scales = [stencil[18 + v] for v in range(4)]
    ones = [scales[v] * ext_rhs[v] for v in range(4)]
    packed = [c + pltpu.roll(c, 31, 1) + pltpu.roll(c, 65, 1) for c in ones]
    around = [[c, pltpu.roll(c, 7, 0), pltpu.roll(c, 6, 0)] for c in packed]
    results = []
    for vx in range(2):
        total = jnp.zeros((8, 128), F32)
        for at in range(3):
            for d in range(3):
                total = total + stencil[vx * 9 + at * 3 + d] * around[vx + at][d]
        image = total + pltpu.roll(total, 96, 1) + pltpu.roll(total, 64, 1)
        one = pltpu.roll(ones[vx + 1], 7, 0)
        scale = pltpu.roll(scales[vx + 1], 7, 0)
        right = pltpu.roll(ext_rhs[vx + 1], 7, 0)
        results.append(one + scale * (right - image))
    pair = halves(jnp.concatenate(results, axis=0))
    nodes = halves(times_right(pair, late_part("prol_z")))
    nodes = jnp.concatenate([nodes[0], nodes[0], nodes[1]], axis=0)
    fine = step[...] + fmask[...] * dot(late_part("prol_xy")[:, 0:48], nodes)
    fine = fine.reshape(4, 8, 8, 128)
    for j in range(4):
        out_ref[:, 8 * j : 8 * j + 8, :] = fine[j]
    copies = halves(dot(jnp.concatenate(pair, axis=1), late_part("copy_z")[:, 0:128]))
    copies = jnp.concatenate([copies[0], copies[0], copies[1]], axis=0)
    copies = dot(late_part("copy_y")[:, 0:48], copies)
    coarse_ref[...] = copies.reshape(2, 8, 128)[:, :, 0:32]

    settle("reach", cr, 10, True)


def finish(fine, coarse, fine_out, coarse_out, sem):
    one = pltpu.make_async_copy(fine, fine_out, sem.at[0])
    two = pltpu.make_async_copy(coarse, coarse_out, sem.at[1])
    one.start()
    two.start()
    one.wait()
    two.wait()


def solution(mesh):
    n_dom = mesh.shape["dom"]
    n_sub = mesh.shape["sub"]

    def shards(rhs_local, coefficient):
        (early_at, early), (late_at, late), (flat_at, flat) = constants(4, 16)
        any_space = pl.BlockSpec(memory_space=pl.ANY)
        vmem = pl.BlockSpec(memory_space=pltpu.VMEM)
        outs = (
            jax.ShapeDtypeStruct((8, 32, 128), F32),
            jax.ShapeDtypeStruct((2, 8, 32), F32),
        )

        def space(*shape):
            return pltpu.VMEM(shape, F32)

        dma = pltpu.SemaphoreType.DMA
        operands = [
            pltpu.with_memory_space_constraint(v, pltpu.HBM)
            for v in (coefficient, rhs_local, early, late, flat)
        ]
        fine, coarse = pl.pallas_call(
            functools.partial(kernel, (early_at, late_at, flat_at), n_dom, n_sub),
            out_shape=outs,
            in_specs=[any_space] * 5,
            out_specs=(vmem, vmem),
            scratch_shapes=[
                space(8, 32, 128),
                space(8, 32, 128),
                pltpu.VMEM(early.shape, BF16),
                pltpu.VMEM(late.shape, BF16),
                pltpu.VMEM(flat.shape, F32),
                space(256, 128),
                space(2, 256, 128),
                space(1, 256, 128),
                space(256, 128),
                space(256, 128),
                space(256, 128),
                space(256, 128),
                space(3, 24, 128),
                space(2, 8, 128),
                space(8, 128),
                space(8, 128),
                space(22, 8, 128),
                space(256, 128),
                space(2, 96, 128),
                space(2, 3, 8, 128),
                space(4, 8, 128),
                space(2, 2, 32, 128),
                space(2, 2, 8, 128),
                space(4, 2, 1, 128),
                space(2, 1, 32, 128),
                space(2, 1, 8, 128),
                space(4, 1, 1, 128),
                space(2, 2, 32, 128),
                space(2, 2, 8, 128),
                space(4, 2, 1, 128),
                space(2, 1, 32, 128),
                space(2, 1, 8, 128),
                space(4, 1, 1, 128),
                space(2, 2, 24, 128),
                space(6, 8, 128),
                space(14, 8, 128),
                space(20, 8, 128),
                space(2, 96, 128),
                space(2, 3, 8, 128),
                space(4, 8, 128),
                dma((5,)),
                dma((13,)),
                dma((13,)),
                pltpu.SemaphoreType.REGULAR((2,)),
            ],
            compiler_params=pltpu.CompilerParams(
                collective_id=0, has_side_effects=True, vmem_limit_bytes=8 * 2**20
            ),
        )(*operands)
        return pl.pallas_call(
            finish,
            out_shape=outs,
            in_specs=[vmem, vmem],
            out_specs=(any_space, any_space),
            scratch_shapes=[dma((2,))],
            compiler_params=pltpu.CompilerParams(vmem_limit_bytes=2**20),
        )(fine, coarse)

    return jax.shard_map(
        shards,
        mesh=mesh,
        in_specs=(P("dom", "sub", None), P("dom", "sub", None)),
        out_specs=(P("dom", "sub", None), P("dom", "sub", None)),
        check_vma=False,
    )
```

```python
import functools

import jax
import jax.numpy as jnp
import numpy as np
from jax import lax
from jax.experimental import pallas as pl
from jax.experimental.pallas import tpu as pltpu
from jax.sharding import PartitionSpec as P

MESH = pl.DeviceIdType.MESH
HIGHEST = lax.Precision.HIGHEST
F32 = jnp.float32
BF16 = jnp.bfloat16

NEAR = [(dx, dy) for dx in (-1, 0, 1) for dy in (-1, 0, 1) if (dx, dy) != (0, 0)]
WIDE = [(dx, dy) for dx in (-2, -1, 0, 1, 2) for dy in (-1, 0, 1) if (dx, dy) != (0, 0)]
REACH = [(dx, dy) for dx in range(-3, 4) for dy in (-1, 0, 1) if (dx, dy) != (0, 0)]
SIDE = [pair for pair in NEAR if pair[1] == 0]
RIMS = [pair for pair in NEAR if pair[1] != 0]
EDGE = [pair for pair in RIMS if pair[0] != 0]
ROWS = [pair for pair in RIMS if pair[0] == 0]


def opposite(table, pair):
    return table.index((-pair[0], -pair[1]))


def tables():
    degree = 7
    points = np.array(
        [
            -1.0,
            -0.8717401485096066,
            -0.5917001814331423,
            -0.2092992179024789,
            0.2092992179024789,
            0.5917001814331423,
            0.8717401485096066,
            1.0,
        ]
    )
    previous = np.ones(points.shape)
    values = points.copy()
    for level in range(1, degree):
        following = ((2 * level + 1) * points * values - level * previous) / (level + 1)
        previous = values
        values = following
    weights = 2.0 / (degree * (degree + 1) * values**2)
    derivative = np.zeros((8, 8))
    for row_at in range(8):
        for col_at in range(8):
            if row_at != col_at:
                derivative[row_at, col_at] = values[row_at] / (
                    values[col_at] * (points[row_at] - points[col_at])
                )
    derivative[0, 0] = -degree * (degree + 1) / 4.0
    derivative[7, 7] = degree * (degree + 1) / 4.0
    interp = np.stack([(1.0 - points) / 2.0, (1.0 + points) / 2.0], axis=1)
    return derivative, weights, interp


DER, WTS, INT = tables()
TWICE = np.array([2.0, 1.0, 1.0, 1.0, 1.0, 1.0, 1.0, 2.0])
HATS = [TWICE * INT[:, 0], TWICE * INT[:, 1]]


def face_moments(face):
    near = 0 if face == 0 else 1
    return [DER[:, face] * (DER @ HATS[i]) for i in (near, 1 - near)]
MASS = [INT[:, 0] * INT[:, 0], INT[:, 0] * INT[:, 1], INT[:, 1] * INT[:, 1]]


def moment_maps(elements, order, slope):
    maps = np.zeros((len(order), elements + 1, 8 * elements))
    for at, offset in enumerate(order):
        for e in range(elements):
            nodes = slice(8 * e, 8 * e + 8)
            if offset == 0:
                maps[at, e, nodes] += 0.25 if slope else MASS[0]
                maps[at, e + 1, nodes] += 0.25 if slope else MASS[2]
            elif offset == 1:
                maps[at, e, nodes] += -0.25 if slope else MASS[1]
            else:
                maps[at, e + 1, nodes] += -0.25 if slope else MASS[1]
    return maps


def unique_interp(elements):
    maps = np.zeros((8 * elements, elements + 1))
    for e in range(elements):
        maps[8 * e : 8 * e + 8, e] = INT[:, 0]
        maps[8 * e : 8 * e + 8, e + 1] = INT[:, 1]
    return maps


def unique_copies(elements):
    maps = np.zeros((2 * elements, elements + 1))
    for e in range(elements):
        maps[2 * e, e] = 1.0
        maps[2 * e + 1, e + 1] = 1.0
    return maps


def split(matrix):
    high = jnp.asarray(matrix, F32).astype(BF16)
    return high, (jnp.asarray(matrix, F32) - high.astype(F32)).astype(BF16)


def right_halves(matrix):
    high, low = split(matrix)
    top = jnp.concatenate([high, low], axis=1)
    return jnp.concatenate([top, jnp.concatenate([high, jnp.zeros_like(low)], axis=1)], axis=0)


def left_halves(matrix):
    high, low = split(matrix)
    return jnp.concatenate([high, low, high], axis=1)


def wide(block):
    return jnp.pad(block, ((0, 0), (0, 256 - block.shape[1])))


def spots_of(parts):
    spots = {}
    at = 0
    for name, block in parts.items():
        spots[name] = (at, block.shape[0])
        at += block.shape[0]
    return spots, jnp.concatenate(list(parts.values()))


def constants(ey, ez):
    square = DER * DER
    eye8 = np.eye(8)
    eye = np.eye(ez)
    early = {
        "square_z": right_halves(np.kron(eye, square)),
        "square_xy": wide(left_halves(np.kron(square.T, eye8) + np.kron(eye8, square.T))),
    }
    low = unique_interp(ey)
    place = np.zeros((4, 8, 8, 16))
    for side in range(2):
        place[..., 8 * side : 8 * side + ey + 1] = (
            INT[:, side][None, :, None, None] * low.reshape(ey, 8, ey + 1)[:, None]
        )
    place = place.reshape(256, 16)
    rest_z = np.zeros((128, 128))
    rest_z[:, : ez + 1] = unique_interp(ez)
    for at in (32, 64, 96):
        rest_z[:, at : at + ez + 1] = unique_interp(ez)
    prol_z = np.zeros((128, 128))
    prol_z[: ez + 1, :] = unique_interp(ez).T
    copy_z = np.zeros((128, 128))
    copy_z[: ez + 1, : 2 * ez] = unique_copies(ez).T
    copy_y = np.zeros((16, 16))
    for side in range(2):
        copy_y[8 * side : 8 * side + 8, 8 * side : 8 * side + ey + 1] = unique_copies(ey)
    own = np.zeros((32, 256))
    for side in range(2):
        own[8 * (side + 1) + 1 : 8 * (side + 1) + 2 + ey] = place.T[8 * side : 8 * side + ey + 1]
    rest_xy = split(own)
    spill = np.zeros((4, 8, 256))
    low_m = low * np.tile(TWICE, ey)[:, None]
    for side in range(2):
        for at, v in ((0, 1 + side), (64, 3 * side)):
            spill[v, 1 : ey + 2, at + 32 * side : at + 32 * side + 32] = low_m.T
        for at, r in ((128, 1 + ey * side), (144, (ey + 2) * side)):
            for vx in range(2):
                spill[1 + vx, r, at + 8 * side : at + 8 * side + 8] = HATS[vx]
    for at, (dx, dy) in enumerate(EDGE):
        near_v, far_v = (1, 0) if dx < 0 else (2, 3)
        near_r, far_r = (1, 0) if dy < 0 else (1 + ey, 2 + ey)
        spill[near_v, near_r, 160 + at] = 1.0
        spill[far_v, near_r, 168 + at] = 1.0
        spill[near_v, far_r, 176 + at] = 1.0
    spill = split(spill.reshape(32, 256))
    rest_z = np.zeros((128, 128))
    rest_z[:, : ez + 1] = unique_interp(ez)
    for at in (32, 64, 96):
        rest_z[:, at : at + ez + 1] = unique_interp(ez)
    prol_z = np.zeros((128, 128))
    prol_z[: ez + 1, :] = unique_interp(ez).T
    copy_z = np.zeros((128, 128))
    copy_z[: ez + 1, : 2 * ez] = unique_copies(ez).T
    copy_y = np.zeros((16, 16))
    for side in range(2):
        copy_y[8 * side : 8 * side + 8, 8 * side : 8 * side + ey + 1] = unique_copies(ey)
    own = np.zeros((32, 256))
    for side in range(2):
        own[8 * (side + 1) + 1 : 8 * (side + 1) + 2 + ey] = place.T[8 * side : 8 * side + ey + 1]
    rest_xy = split(own)
    spill = np.zeros((4, 8, 256))
    low_m = low * np.tile(TWICE, ey)[:, None]
    for side in range(2):
        for at, v in ((0, 1 + side), (64, 3 * side)):
            spill[v, 1 : ey + 2, at + 32 * side : at + 32 * side + 32] = low_m.T
        for at, r in ((128, 1 + ey * side), (144, (ey + 2) * side)):
            for vx in range(2):
                spill[1 + vx, r, at + 8 * side : at + 8 * side + 8] = HATS[vx]
    for at, (dx, dy) in enumerate(EDGE):
        near_v, far_v = (1, 0) if dx < 0 else (2, 3)
        near_r, far_r = (1, 0) if dy < 0 else (1 + ey, 2 + ey)
        spill[near_v, near_r, 160 + at] = 1.0
        spill[far_v, near_r, 168 + at] = 1.0
        spill[near_v, far_r, 176 + at] = 1.0
    spill = split(spill.reshape(32, 256))
    moment_y = np.zeros((2, 2, 8, 8, 8))
    for side in range(2):
        for at, one in enumerate(face_moments(7 * side)):
            moment_y[side, at] = np.eye(8)[:, :, None] * one[None, None, :]
    moment_y = moment_y.reshape(32, 64)
    late = {
        "grad_z": right_halves(np.kron(eye, DER.T)),
        "back_z": right_halves(np.kron(eye, DER)),
        "rest_z": right_halves(rest_z),
        "prol_z": right_halves(prol_z),
        "copy_z": wide(jnp.concatenate([split(copy_z)[0]] * 2)),
        "prol_xy": wide(left_halves(place)),
        "grad_xy": wide(
            jnp.concatenate([left_halves(np.kron(DER, eye8)), left_halves(np.kron(eye8, DER))])
        ),
        "back_y": wide(left_halves(np.kron(eye8, DER.T))),
        "rest_xy": jnp.concatenate([rest_xy[0], rest_xy[1]]),
        "spill": jnp.concatenate([spill[0], spill[1]]),
        "copy_y": wide(left_halves(copy_y)),
    }
    flat = {}
    for name, slope in (("moment_m", False), ("moment_s", True)):
        block = np.zeros((128, 128))
        for at, one in enumerate(moment_maps(ez, (0, 1, -1), slope)):
            block[:, 32 * at : 32 * at + ez + 1] = one.T
        flat[name] = jnp.asarray(block, F32)
    order_y = (-1, 0, 1)
    mass_y = np.zeros((3, 8, 8 * ey))
    mass_y[:, : ey + 1] = moment_maps(ey, order_y, False)
    slope_y = np.zeros((3, 8, 8 * ey))
    slope_y[:, : ey + 1] = moment_maps(ey, order_y, True)
    mass_y = mass_y.reshape(24, 8 * ey)
    slope_y = slope_y.reshape(24, 8 * ey)
    for name, sign in (("mix_plus", 0.25), ("mix_minus", -0.25)):
        block = np.zeros((24, 128))
        block[:, : 24 * ey] = np.concatenate([slope_y, mass_y, sign * mass_y], axis=1)
        flat[name] = jnp.asarray(block, F32)
    return spots_of(early), spots_of(late), spots_of(flat)


def kernel(
    tables_at, n_dom, n_sub, coef_hbm, rhs_hbm, early_hbm, late_hbm, flat_hbm,
    out_ref, coarse_ref,
    coef, rhs, early, late, flat, weighted, field, held, fmask, fmult, inverse, step,
    pmine, ptile, dtile, ctile, stencil, gfield, fside, frow, fedge,
    xs1, vs1, es1, xs2, vs2, es2,
    xr1, vr1, er1, xr2, vr2, er2, px, pt, dr, cr, fx, fy, fe,
    load_sem, s_sem, r_sem, ready,
):
    early_at, late_at, flat_at = tables_at
    dom = lax.axis_index("dom")
    sub = lax.axis_index("sub")

    loads = []
    for at, (source, dest) in enumerate(
        ((coef_hbm, coef), (early_hbm, early), (rhs_hbm, rhs), (flat_hbm, flat), (late_hbm, late))
    ):
        load = pltpu.make_async_copy(source, dest, load_sem.at[at])
        load.start()
        loads.append(load)

    def present(pair):
        dx, dy = pair
        conds = []
        if dx < 0:
            conds.append(dom >= -dx)
        if dx > 0:
            conds.append(dom < n_dom - dx)
        if dy < 0:
            conds.append(sub >= 1)
        if dy > 0:
            conds.append(sub < n_sub - 1)
        return functools.reduce(jnp.logical_and, conds)

    def target(pair):
        return (dom + pair[0], sub + pair[1])

    for buffer in (xr1, vr1, er1, xr2, vr2, er2, px, pt, dr, cr, fx, fy, fe):
        buffer[...] = jnp.zeros_like(buffer)

    barrier = pltpu.get_barrier_semaphore()
    for pair in NEAR:

        @pl.when(present(pair))
        def _(pair=pair):
            pl.semaphore_signal(barrier, inc=1, device_id=target(pair), device_id_type=MESH)

    near_x = jnp.where(dom >= 1, 1, 0) + jnp.where(dom < n_dom - 1, 1, 0)
    near_y = jnp.where(sub >= 1, 1, 0) + jnp.where(sub < n_sub - 1, 1, 0)
    far_x = near_x + jnp.where(dom >= 2, 1, 0) + jnp.where(dom < n_dom - 2, 1, 0)
    n_side = near_x
    n_rims = near_y * (1 + near_x)
    n_wide = (1 + far_x) * (1 + near_y) - 1
    reach_x = far_x + jnp.where(dom >= 3, 1, 0) + jnp.where(dom < n_dom - 3, 1, 0)
    n_reach = (1 + reach_x) * (1 + near_y) - 1

    row = lax.broadcasted_iota(jnp.int32, (256, 128), 0)
    lane = lax.broadcasted_iota(jnp.int32, (256, 128), 1)
    x_at = lax.shift_right_logical(row, 3) & 7
    b_at = row & 7
    c_at = lane & 7
    place_x = dom * 8 + x_at
    place_y = sub * 32 + lax.shift_right_logical(row, 6) * 8 + b_at
    inside = (
        (place_x > 0) & (place_x < 8 * n_dom - 1)
        & (place_y > 0) & (place_y < 32 * n_sub - 1)
        & (lane > 0) & (lane < 127)
    )
    mask = jnp.where(inside, 1.0, 0.0)
    fmask[...] = mask
    twice = jnp.where((x_at == 0) | (x_at == 7), 2.0, 1.0)
    twice = twice * jnp.where((b_at == 0) | (b_at == 7), 2.0, 1.0)
    fmult[...] = mask * twice * jnp.where((c_at == 0) | (c_at == 7), 2.0, 1.0)

    lane8 = lax.broadcasted_iota(jnp.int32, (8, 128), 1)
    sub8 = lax.broadcasted_iota(jnp.int32, (8, 128), 0)
    z_low = ((lane8 & 7) == 0) & (lane8 > 0)
    z_high = ((lane8 & 7) == 7) & (lane8 < 127)

    def weights_along(spot):
        value = jnp.where((spot == 0) | (spot == 7), float(WTS[0]), float(WTS[1]))
        value = jnp.where((spot == 2) | (spot == 5), float(WTS[2]), value)
        return jnp.where((spot == 3) | (spot == 4), float(WTS[3]), value)

    def fold(v):
        v = v.reshape(32, 8, 128)
        v = v + jnp.where(
            z_high[None], pltpu.roll(v, 127, 2),
            jnp.where(z_low[None], pltpu.roll(v, 1, 2), 0.0),
        )
        up = pltpu.roll(v, 1, 1)
        down = pltpu.roll(v, 7, 1)
        none = jnp.zeros((8, 8, 128), F32)
        up = jnp.concatenate([none, up[:24]], axis=0)
        down = jnp.concatenate([down[8:], none], axis=0)
        v = v + jnp.where((sub8 == 0)[None], up, jnp.where((sub8 == 7)[None], down, 0.0))
        return v.reshape(256, 128)

    def halves(v):
        high = v.astype(BF16)
        return high, (v - high.astype(F32)).astype(BF16)

    def dot(left, right):
        return jnp.dot(left, right, preferred_element_type=F32)

    def early_part(name):
        start, count = early_at[name]
        return early[start : start + count, :]

    def late_part(name):
        start, count = late_at[name]
        return late[start : start + count, :]

    def flat_part(name):
        start, count = flat_at[name]
        return flat[start : start + count, :]

    def times_right(pair, matrix):
        left = jnp.concatenate(pair, axis=1)
        half = left.shape[0] // 2 if left.shape[0] > 32 else left.shape[0]
        sums = []
        for at in range(0, left.shape[0], half):
            both = dot(left[at : at + half], matrix)
            sums.append(both[:, :128] + both[:, 128:])
        return jnp.concatenate(sums, axis=0)

    def stacked(pair):
        high, low = [
            jnp.concatenate([v[at : at + 64] for at in range(0, v.shape[0], 64)], axis=1) for v in pair
        ]
        return jnp.concatenate([high, high, low], axis=0)

    def rows_of(v):
        return jnp.concatenate([v[:, at : at + 128] for at in range(0, v.shape[1], 128)], axis=0)

    def back_x(v):
        v = v.reshape(4, 8, 8, 128)
        matrix = DER.T
        even = [v[:, b] + v[:, 7 - b] for b in range(4)]
        odd = [v[:, b] - v[:, 7 - b] for b in range(4)]
        planes = [None] * 8
        for a in range(4):
            p = sum(float(matrix[a, b] + matrix[a, 7 - b]) / 2 * even[b] for b in range(4))
            q = sum(float(matrix[a, b] - matrix[a, 7 - b]) / 2 * odd[b] for b in range(4))
            planes[a] = p + q
            planes[7 - a] = q - p
        return jnp.stack(planes, axis=1).reshape(256, 128)

    def with_faces(u, faces, face_weights):
        w = weighted[...]
        pair = halves(jnp.concatenate([u, faces], axis=0))
        both = dot(late_part("grad_xy")[:, 0:192], stacked(pair))
        all_z = times_right(pair, late_part("grad_z"))
        all_y = rows_of(both[64:128])
        settle("side", fx, 2, False)
        settle("rows", fy, 3, False)
        settle("edge", fe, 4, False)
        w_rows, w_z = face_weights()
        flux_z = halves(jnp.concatenate([w * all_z[0:256], w_z * all_z[256:384]], axis=0))
        flux_y = halves(jnp.concatenate([w * all_y[0:256], w_rows * all_y[256:384]], axis=0))
        back = rows_of(dot(late_part("back_y")[:, 0:192], stacked(flux_y)))
        back = back + times_right(flux_z, late_part("back_z"))
        return back[0:256] + back_x(w * rows_of(both[0:64, 0:512])), back[256:384]

    def local_operator(u):
        w = weighted[...]
        pair = halves(u)
        both = dot(late_part("grad_xy")[:, 0:192], stacked(pair))
        flux_z = halves(w * times_right(pair, late_part("grad_z")))
        flux_y = halves(w * rows_of(both[64:128]))
        back = rows_of(dot(late_part("back_y")[:, 0:192], stacked(flux_y)))
        back = back + times_right(flux_z, late_part("back_z"))
        return back + back_x(w * rows_of(both[0:64]))

    def send(table, pair, source, landing, group):
        at = table.index((-pair[0], -pair[1]))

        @pl.when(present(pair))
        def _():
            pltpu.make_async_remote_copy(
                src_ref=source,
                dst_ref=landing.at[at],
                send_sem=s_sem.at[group],
                recv_sem=r_sem.at[group],
                device_id=target(pair),
                device_id_type=MESH,
            ).start()

    counts = {"side": (n_side, (1, 2)), "rows": (near_y, (1, 2)), "edge": (near_x * near_y, (1, 2, 4)), "rims": (n_rims, (1, 2, 3, 4, 6)), "wide": (n_wide, (1, 2, 3, 5, 7, 8, 9, 11, 14)), "reach": (n_reach, (7, 9, 11, 13, 14, 17, 20))}

    def settle(kind, landing, group, sent):
        count, options = counts[kind]
        for one in options:

            @pl.when(count == one)
            def _(one=one):
                copy = pltpu.make_async_remote_copy(
                    src_ref=landing.at[pl.ds(0, one)],
                    dst_ref=landing.at[pl.ds(0, one)],
                    send_sem=s_sem.at[group],
                    recv_sem=r_sem.at[group],
                    device_id=(dom, sub),
                    device_id_type=MESH,
                )
                if sent:
                    copy.wait_send()
                else:
                    copy.wait_recv()

    def pack(refs, fields, xs, vs, es):
        for f in range(fields):
            ref = refs.at[f]
            faces = {-1: ref[pl.ds(0, 8, stride=8), :], 1: ref[pl.ds(199, 8, stride=8), :]}
            for j in range(4):
                xs[0, f, 8 * j : 8 * j + 8] = ref[64 * j : 64 * j + 8, :]
                xs[1, f, 8 * j : 8 * j + 8] = ref[64 * j + 56 : 64 * j + 64, :]
            for at, (_, dy) in enumerate(ROWS):
                vs[at, f] = faces[dy]
            for at, (dx, dy) in enumerate(EDGE):
                line = 0 if dx < 0 else 7
                es[at, f] = faces[dy][line : line + 1]

    def exchange(xs, vs, es, xr, vr, er, group, edge_group):
        for pair in EDGE:
            send(EDGE, pair, es.at[EDGE.index(pair)], er, edge_group)
        for pair in SIDE:
            send(SIDE, pair, xs.at[SIDE.index(pair)], xr, group)
        for pair in ROWS:
            send(ROWS, pair, vs.at[ROWS.index(pair)], vr, group + 1)

    def unpack(refs, fields, xr, vr, er):
        for f in range(fields):
            ref = refs.at[f]
            for j in range(4):
                ref[64 * j : 64 * j + 8, :] += xr[0, f, 8 * j : 8 * j + 8]
                ref[64 * j + 56 : 64 * j + 64, :] += xr[1, f, 8 * j : 8 * j + 8]
            for dy, start in ((-1, 0), (1, 199)):
                extra = vr[ROWS.index((0, dy)), f]
                low = er[EDGE.index((-1, dy)), f]
                high = er[EDGE.index((1, dy)), f]
                extra = extra + jnp.where(sub8 == 0, low, jnp.where(sub8 == 7, high, 0.0))
                ref[pl.ds(start, 8, stride=8), :] += extra

    def in_order(ref):
        v = ref[...].reshape(8, 4, 8, 128)
        return jnp.concatenate([v[:, j] for j in range(4)], axis=0).reshape(256, 128)

    table = weights_along(x_at) * weights_along(b_at) * weights_along(c_at)
    loads[0].wait()
    w = in_order(coef) * table
    weighted[...] = w
    loads[1].wait()
    loads[2].wait()
    field[0] = fold(in_order(rhs))
    w4 = w.reshape(4, 8, 8, 128)
    planes = [w4[:, a].reshape(32, 128) for a in range(8)]
    for side in range(2):
        one, two = face_moments(7 * side)
        rows = [weighted[pl.ds(192 * side + b, 8, stride=8), :] for b in range(8)]
        fside[side, 0:32] = sum(float(one[a]) * planes[a] for a in range(8))
        fside[side, 32:64] = sum(float(two[a]) * planes[a] for a in range(8))
        fside[side, 64:96] = planes[7 * side]
        frow[side, 0] = sum(float(one[b]) * rows[b] for b in range(8))
        frow[side, 1] = sum(float(two[b]) * rows[b] for b in range(8))
        frow[side, 2] = rows[7 * side]
    fedge[...] = jnp.zeros_like(fedge)
    for at, (dx, dy) in enumerate(EDGE):
        x_side, y_side = (dx + 1) // 2, (dy + 1) // 2
        spot, line = 31 * y_side, 7 * x_side
        fedge[at, 0:1] = 2.0 * (fside[x_side, spot : spot + 1] + frow[y_side, 0, line : line + 1])
        fedge[at, 1:2] = 2.0 * fside[x_side, 32 + spot : 33 + spot]
        fedge[at, 2:3] = 2.0 * frow[y_side, 1, line : line + 1]
        fedge[at, 3:4] = 4.0 * frow[y_side, 2, line : line + 1]
    pair = halves(w)
    diagonal = rows_of(dot(early_part("square_xy")[:, 0:192], stacked(pair)))
    field[1] = fold(diagonal + times_right(pair, early_part("square_z")))
    pack(field, 2, xs1, vs1, es1)

    pl.semaphore_wait(barrier, (1 + near_x) * (1 + near_y) - 1)
    exchange(xs1, vs1, es1, xr1, vr1, er1, 0, 11)

    def announce(stage):
        for pair in SIDE:

            @pl.when(present(pair))
            def _(pair=pair):
                pl.semaphore_signal(
                    ready.at[stage], inc=1, device_id=target(pair), device_id_type=MESH
                )

    announce(0)
    for at, pair in enumerate(SIDE):
        send(SIDE, pair, fside.at[at], fx, 2)
    for at, pair in enumerate(ROWS):
        send(ROWS, pair, frow.at[at], fy, 3)
    for at, pair in enumerate(EDGE):
        send(EDGE, pair, fedge.at[at], fe, 4)

    loads[3].wait()
    w4 = weighted[...].reshape(4, 8, 8, 128)
    planes = [w4[:, a].reshape(32, 128) for a in range(8)]
    moments = [sum(float(m[a]) * planes[a] for a in range(8) if m[a] != 0.0) for m in MASS]
    moments.append(moments[0] + 2.0 * moments[1] + moments[2])
    stack = jnp.concatenate(moments, axis=0)
    mass_z = jnp.dot(stack, flat_part("moment_m"), precision=HIGHEST, preferred_element_type=F32)
    slope_z = jnp.dot(stack, flat_part("moment_s"), precision=HIGHEST, preferred_element_type=F32)
    none = jnp.zeros((32, 128), F32)
    mine = []
    for at in range(3):
        part = slice(32 * at, 32 * at + 32)
        parts = jnp.concatenate([mass_z[part], slope_z[part], mass_z[96:128], none], axis=0)
        mix = flat_part("mix_minus" if at == 1 else "mix_plus")
        one = jnp.dot(mix, parts, precision=HIGHEST, preferred_element_type=F32)
        pmine[at] = one
        mine.append(one.reshape(3, 8, 128))
    dtile[...] = jnp.where(lane8 < 32, mine[0][1], pltpu.roll(mine[2][1], 32, 1))
    for side, vertex, first in ((0, 0, 1), (1, 4, 0)):
        total = jnp.zeros((8, 128), F32)
        for c in range(3):
            for d in range(2):
                goal = 2 * c + d
                moved = pltpu.roll(mine[c][first + d], (goal - vertex) % 8, 0)
                total = jnp.where(sub8 == goal, moved, total)
        ptile[side] = total
    send(SIDE, (-1, 0), pmine.at[pl.ds(0, 2)], px, 5)
    send(SIDE, (1, 0), pmine.at[pl.ds(1, 2)], px, 5)
    for pair in RIMS:
        send(RIMS, pair, ptile.at[(pair[1] + 1) // 2], pt, 6)
    pl.semaphore_wait(ready.at[0], near_x)
    announce(1)
    for pair in WIDE:
        send(WIDE, pair, dtile, dr, 7)
    loads[4].wait()

    settle("side", xr1, 0, False)
    settle("rows", vr1, 1, False)
    settle("edge", er1, 11, False)
    unpack(field, 2, xr1, vr1, er1)

    residual = fmask[...] * field[0]
    inv = fmask[...] / field[1]
    inverse[...] = inv
    field[0] = residual
    theta = 1.1
    delta = 0.9
    sigma = theta / delta
    rho0 = 1.0 / sigma
    rho1 = 1.0 / (2.0 * sigma - rho0)
    step_one = inv * residual / theta
    step[...] = step_one
    held[0] = fold(local_operator(step_one))
    pack(held, 1, xs2, vs2, es2)
    exchange(xs2, vs2, es2, xr2, vr2, er2, 8, 12)

    factor = 2.0 * rho1 / delta
    g = factor * inverse[...] * held[0]
    gfield[...] = g
    start = (1.0 + rho1 * rho0) * step_one + factor * inv * residual
    step[...] = start
    faces = []
    for first in (0, 56):
        for j in range(4):
            faces.append(g[64 * j + first : 64 * j + first + 8])
    rims = [gfield[pl.ds(0, 8, stride=8), :], gfield[pl.ds(199, 8, stride=8), :]]
    corner = jnp.zeros((8, 128), F32)
    for at, (dx, dy) in enumerate(EDGE):
        line = 0 if dx < 0 else 7
        moved = pltpu.roll(rims[(dy + 1) // 2], (at - line) % 8, 0)
        corner = jnp.where(sub8 == at, moved, corner)
    none40 = jnp.zeros((40, 128), F32)
    faces = jnp.concatenate(faces + rims + [corner, none40], axis=0)
    lines = []

    def face_weights():
        for k in range(4):
            one = jnp.zeros((8, 128), F32)
            for at in range(4):
                one = jnp.where(sub8 == at, pltpu.roll(fe[at], (at - k) % 8, 0), one)
            lines.append(one)
        two = [2.0 * fx[0, 64:96], 2.0 * fx[1, 64:96], 2.0 * fy[0, 2], 2.0 * fy[1, 2]]
        w_rows = jnp.concatenate(two + [jnp.zeros((48, 128), F32)], axis=0)
        return w_rows, jnp.concatenate(two + [lines[3], none40], axis=0)

    image, face_image = with_faces(start - g, faces, face_weights)
    defect = residual - fmult[...] * image
    near_w = [fx[0, 0:32], fx[1, 0:32], fy[0, 0], fy[1, 0], lines[0]]
    far_w = [fx[0, 32:64], fx[1, 32:64], fy[0, 1], fy[1, 1]]
    near = jnp.concatenate(near_w, axis=0) * faces[0:88] + face_image[0:88]
    far = jnp.concatenate(far_w, axis=0) * faces[0:80]
    parts = [
        near[0:64], far[0:64], near[64:80], far[64:80], near[80:88],
        lines[1] * corner, lines[2] * corner, jnp.zeros((72, 128), F32),
    ]
    twice_z = jnp.where(((lane8 & 7) == 0) | ((lane8 & 7) == 7), 2.0, 1.0)
    parts = jnp.concatenate(parts, axis=0).reshape(32, 8, 128) * twice_z[None]
    part = dot(late_part("rest_xy"), jnp.concatenate(halves(defect), axis=1))
    part = part + dot(late_part("spill"), jnp.concatenate(halves(parts.reshape(256, 128)), axis=1))
    part = part[0:32, :128] + part[0:32, 128:] + part[32:64, :128]
    coarse = times_right(halves(part), late_part("rest_z"))
    tile = jnp.where(lane8 < 64, jnp.where(lane8 < 32, coarse[0:8], coarse[8:16]), jnp.where(lane8 < 96, coarse[16:24], coarse[24:32]))
    ctile[...] = tile
    pl.semaphore_wait(ready.at[1], near_x)
    for pair in sorted(REACH, key=lambda p: -abs(p[0]) - abs(p[1])):
        send(REACH, pair, ctile, cr, 10)

    settle("side", px, 5, False)
    settle("rims", pt, 6, False)
    settle("wide", dr, 7, False)
    row_low = sub8 < 2
    row_mid = sub8 == 2

    def extend(own, received):
        moved = []
        for dx in (-2, -1, 0, 1, 2):
            mid = own if dx == 0 else received[WIDE.index((dx, 0))]
            below = received[WIDE.index((dx, -1))]
            above = received[WIDE.index((dx, 1))]
            rim = jnp.where(row_low, above, jnp.where(row_mid, 0.0, below))
            moved.append(pltpu.roll(mid, 1, 0) + pltpu.roll(rim, 5, 0))
        return [moved[v + 1] + pltpu.roll(moved[v], 96, 1) for v in range(4)]

    ext_diag = extend(dtile[...], dr)
    vertex_y = sub * 4 + sub8 - 1
    good_yz = (vertex_y > 0) & (vertex_y < 4 * n_sub) & (sub8 < 7) & (lane8 > 0) & (lane8 < 16)
    scales = []
    for v in range(4):
        vertex_x = dom + v - 1
        good = good_yz & (vertex_x > 0) & (vertex_x < n_dom)
        scales.append(jnp.where(good, (2.0 / 3.0) / jnp.where(good, ext_diag[v], 1.0), 0.0))

    def joined(dx, c):
        if dx == 0:
            base = pmine[c]
        else:
            base = px[SIDE.index((dx, 0)), c if dx > 0 else c - 1]
        base = base.reshape(3, 8, 128)
        below = pt[RIMS.index((dx, -1))]
        above = pt[RIMS.index((dx, 1))]
        out = []
        for d in range(3):
            total = base[d]
            if d < 2:
                moved = pltpu.roll(below, (-2 * c - d) % 8, 0)
                total = total + jnp.where(sub8 == 0, moved, 0.0)
            if d > 0:
                moved = pltpu.roll(above, (4 - 2 * c - (d - 1)) % 8, 0)
                total = total + jnp.where(sub8 == 4, moved, 0.0)
            out.append(total)
        return out

    cross = joined(0, 1)
    own_low = [a + b for a, b in zip(joined(0, 0), joined(-1, 2), strict=True)]
    own_high = [a + b for a, b in zip(joined(0, 2), joined(1, 0), strict=True)]
    for vx, blocks in enumerate(
        ((joined(-1, 1), own_low, cross), (cross, own_high, joined(1, 1)))
    ):
        for at in range(3):
            for d in range(3):
                stencil[vx * 9 + at * 3 + d] = blocks[at][d]
    for v in range(4):
        stencil[18 + v] = scales[v]

    settle("side", xr2, 8, False)
    settle("rows", vr2, 9, False)
    settle("edge", er2, 12, False)
    unpack(held, 1, xr2, vr2, er2)
    step[...] = step[...] - factor * inverse[...] * held[0]

    settle("side", xr1, 0, True)
    settle("rows", vr1, 1, True)
    settle("edge", er1, 11, True)
    settle("side", fx, 2, True)
    settle("rows", fy, 3, True)
    settle("edge", fe, 4, True)
    settle("side", px, 5, True)
    settle("rims", pt, 6, True)
    settle("wide", dr, 7, True)
    settle("side", xr2, 8, True)
    settle("rows", vr2, 9, True)
    settle("edge", er2, 12, True)
    settle("reach", cr, 10, False)

    moved = {}
    mid_rows = (sub8 > 3) & (sub8 < 7)
    for dx in range(-3, 4):
        mid = ctile[...] if dx == 0 else cr[REACH.index((dx, 0))]
        below = cr[REACH.index((dx, -1))]
        above = cr[REACH.index((dx, 1))]
        rim = jnp.where(sub8 < 3, above, jnp.where(mid_rows, below, 0.0))
        moved[dx] = mid + pltpu.roll(rim, 4, 0)
    whole = moved[0] + pltpu.roll(jnp.where(lane8 < 96, moved[1], moved[-3]), 32, 1)
    whole = whole + pltpu.roll(jnp.where(lane8 < 64, moved[2], moved[-2]), 64, 1)
    whole = whole + pltpu.roll(jnp.where(lane8 >= 32, moved[-1], moved[3]), 96, 1)
    ext_rhs = [whole] + [pltpu.roll(whole, 128 - 32 * v, 1) for v in (1, 2, 3)]
    scales = [stencil[18 + v] for v in range(4)]
    ones = [scales[v] * ext_rhs[v] for v in range(4)]
    packed = [c + pltpu.roll(c, 31, 1) + pltpu.roll(c, 65, 1) for c in ones]
    around = [[c, pltpu.roll(c, 7, 0), pltpu.roll(c, 6, 0)] for c in packed]
    results = []
    for vx in range(2):
        total = jnp.zeros((8, 128), F32)
        for at in range(3):
            for d in range(3):
                total = total + stencil[vx * 9 + at * 3 + d] * around[vx + at][d]
        image = total + pltpu.roll(total, 96, 1) + pltpu.roll(total, 64, 1)
        one = pltpu.roll(ones[vx + 1], 7, 0)
        scale = pltpu.roll(scales[vx + 1], 7, 0)
        right = pltpu.roll(ext_rhs[vx + 1], 7, 0)
        results.append(one + scale * (right - image))
    pair = halves(jnp.concatenate(results, axis=0))
    nodes = halves(times_right(pair, late_part("prol_z")))
    nodes = jnp.concatenate([nodes[0], nodes[0], nodes[1]], axis=0)
    fine = step[...] + fmask[...] * dot(late_part("prol_xy")[:, 0:48], nodes)
    fine = fine.reshape(4, 8, 8, 128)
    for j in range(4):
        out_ref[:, 8 * j : 8 * j + 8, :] = fine[j]
    copies = halves(dot(jnp.concatenate(pair, axis=1), late_part("copy_z")[:, 0:128]))
    copies = jnp.concatenate([copies[0], copies[0], copies[1]], axis=0)
    copies = dot(late_part("copy_y")[:, 0:48], copies)
    coarse_ref[...] = copies.reshape(2, 8, 128)[:, :, 0:32]

    settle("reach", cr, 10, True)


def finish(fine, coarse, fine_out, coarse_out, sem):
    one = pltpu.make_async_copy(fine, fine_out, sem.at[0])
    two = pltpu.make_async_copy(coarse, coarse_out, sem.at[1])
    one.start()
    two.start()
    one.wait()
    two.wait()


def solution(mesh):
    n_dom = mesh.shape["dom"]
    n_sub = mesh.shape["sub"]

    def shards(rhs_local, coefficient):
        (early_at, early), (late_at, late), (flat_at, flat) = constants(4, 16)
        any_space = pl.BlockSpec(memory_space=pl.ANY)
        vmem = pl.BlockSpec(memory_space=pltpu.VMEM)
        outs = (
            jax.ShapeDtypeStruct((8, 32, 128), F32),
            jax.ShapeDtypeStruct((2, 8, 32), F32),
        )

        def space(*shape):
            return pltpu.VMEM(shape, F32)

        dma = pltpu.SemaphoreType.DMA
        operands = [
            pltpu.with_memory_space_constraint(v, pltpu.HBM)
            for v in (coefficient, rhs_local, early, late, flat)
        ]
        fine, coarse = pl.pallas_call(
            functools.partial(kernel, (early_at, late_at, flat_at), n_dom, n_sub),
            out_shape=outs,
            in_specs=[any_space] * 5,
            out_specs=(vmem, vmem),
            scratch_shapes=[
                space(8, 32, 128),
                space(8, 32, 128),
                pltpu.VMEM(early.shape, BF16),
                pltpu.VMEM(late.shape, BF16),
                pltpu.VMEM(flat.shape, F32),
                space(256, 128),
                space(2, 256, 128),
                space(1, 256, 128),
                space(256, 128),
                space(256, 128),
                space(256, 128),
                space(256, 128),
                space(3, 24, 128),
                space(2, 8, 128),
                space(8, 128),
                space(8, 128),
                space(22, 8, 128),
                space(256, 128),
                space(2, 96, 128),
                space(2, 3, 8, 128),
                space(4, 8, 128),
                space(2, 2, 32, 128),
                space(2, 2, 8, 128),
                space(4, 2, 1, 128),
                space(2, 1, 32, 128),
                space(2, 1, 8, 128),
                space(4, 1, 1, 128),
                space(2, 2, 32, 128),
                space(2, 2, 8, 128),
                space(4, 2, 1, 128),
                space(2, 1, 32, 128),
                space(2, 1, 8, 128),
                space(4, 1, 1, 128),
                space(2, 2, 24, 128),
                space(6, 8, 128),
                space(14, 8, 128),
                space(20, 8, 128),
                space(2, 96, 128),
                space(2, 3, 8, 128),
                space(4, 8, 128),
                dma((5,)),
                dma((13,)),
                dma((13,)),
                pltpu.SemaphoreType.REGULAR((2,)),
            ],
            compiler_params=pltpu.CompilerParams(
                collective_id=0, has_side_effects=True, vmem_limit_bytes=8 * 2**20
            ),
        )(*operands)
        return pl.pallas_call(
            finish,
            out_shape=outs,
            in_specs=[vmem, vmem],
            out_specs=(any_space, any_space),
            scratch_shapes=[dma((2,))],
            compiler_params=pltpu.CompilerParams(vmem_limit_bytes=2**20),
        )(fine, coarse)

    return jax.shard_map(
        shards,
        mesh=mesh,
        in_specs=(P("dom", "sub", None), P("dom", "sub", None)),
        out_specs=(P("dom", "sub", None), P("dom", "sub", None)),
        check_vma=False,
    )
```

```python
import functools

import jax
import jax.numpy as jnp
import numpy as np
from jax import lax
from jax.experimental import pallas as pl
from jax.experimental.pallas import tpu as pltpu
from jax.sharding import PartitionSpec as P

MESH = pl.DeviceIdType.MESH
HIGHEST = lax.Precision.HIGHEST
F32 = jnp.float32
BF16 = jnp.bfloat16

NEAR = [(dx, dy) for dx in (-1, 0, 1) for dy in (-1, 0, 1) if (dx, dy) != (0, 0)]
WIDE = [(dx, dy) for dx in (-2, -1, 0, 1, 2) for dy in (-1, 0, 1) if (dx, dy) != (0, 0)]
REACH = [(dx, dy) for dx in range(-3, 4) for dy in (-1, 0, 1) if (dx, dy) != (0, 0)]
SIDE = [pair for pair in NEAR if pair[1] == 0]
RIMS = [pair for pair in NEAR if pair[1] != 0]
EDGE = [pair for pair in RIMS if pair[0] != 0]
ROWS = [pair for pair in RIMS if pair[0] == 0]


def opposite(table, pair):
    return table.index((-pair[0], -pair[1]))


def tables():
    degree = 7
    points = np.array(
        [
            -1.0,
            -0.8717401485096066,
            -0.5917001814331423,
            -0.2092992179024789,
            0.2092992179024789,
            0.5917001814331423,
            0.8717401485096066,
            1.0,
        ]
    )
    previous = np.ones(points.shape)
    values = points.copy()
    for level in range(1, degree):
        following = ((2 * level + 1) * points * values - level * previous) / (level + 1)
        previous = values
        values = following
    weights = 2.0 / (degree * (degree + 1) * values**2)
    derivative = np.zeros((8, 8))
    for row_at in range(8):
        for col_at in range(8):
            if row_at != col_at:
                derivative[row_at, col_at] = values[row_at] / (
                    values[col_at] * (points[row_at] - points[col_at])
                )
    derivative[0, 0] = -degree * (degree + 1) / 4.0
    derivative[7, 7] = degree * (degree + 1) / 4.0
    interp = np.stack([(1.0 - points) / 2.0, (1.0 + points) / 2.0], axis=1)
    return derivative, weights, interp


DER, WTS, INT = tables()
TWICE = np.array([2.0, 1.0, 1.0, 1.0, 1.0, 1.0, 1.0, 2.0])
HATS = [TWICE * INT[:, 0], TWICE * INT[:, 1]]


def face_moments(face):
    near = 0 if face == 0 else 1
    return [DER[:, face] * (DER @ HATS[i]) for i in (near, 1 - near)]
MASS = [INT[:, 0] * INT[:, 0], INT[:, 0] * INT[:, 1], INT[:, 1] * INT[:, 1]]


def moment_maps(elements, order, slope):
    maps = np.zeros((len(order), elements + 1, 8 * elements))
    for at, offset in enumerate(order):
        for e in range(elements):
            nodes = slice(8 * e, 8 * e + 8)
            if offset == 0:
                maps[at, e, nodes] += 0.25 if slope else MASS[0]
                maps[at, e + 1, nodes] += 0.25 if slope else MASS[2]
            elif offset == 1:
                maps[at, e, nodes] += -0.25 if slope else MASS[1]
            else:
                maps[at, e + 1, nodes] += -0.25 if slope else MASS[1]
    return maps


def unique_interp(elements):
    maps = np.zeros((8 * elements, elements + 1))
    for e in range(elements):
        maps[8 * e : 8 * e + 8, e] = INT[:, 0]
        maps[8 * e : 8 * e + 8, e + 1] = INT[:, 1]
    return maps


def unique_copies(elements):
    maps = np.zeros((2 * elements, elements + 1))
    for e in range(elements):
        maps[2 * e, e] = 1.0
        maps[2 * e + 1, e + 1] = 1.0
    return maps


def split(matrix):
    high = jnp.asarray(matrix, F32).astype(BF16)
    return high, (jnp.asarray(matrix, F32) - high.astype(F32)).astype(BF16)


def right_halves(matrix):
    high, low = split(matrix)
    top = jnp.concatenate([high, low], axis=1)
    return jnp.concatenate([top, jnp.concatenate([high, jnp.zeros_like(low)], axis=1)], axis=0)


def left_halves(matrix):
    high, low = split(matrix)
    return jnp.concatenate([high, low, high], axis=1)


def wide(block):
    return jnp.pad(block, ((0, 0), (0, 256 - block.shape[1])))


def spots_of(parts):
    spots = {}
    at = 0
    for name, block in parts.items():
        spots[name] = (at, block.shape[0])
        at += block.shape[0]
    return spots, jnp.concatenate(list(parts.values()))


def constants(ey, ez):
    square = DER * DER
    eye8 = np.eye(8)
    eye = np.eye(ez)
    early = {
        "square_z": right_halves(np.kron(eye, square)),
        "square_xy": wide(left_halves(np.kron(square.T, eye8) + np.kron(eye8, square.T))),
    }
    low = unique_interp(ey)
    place = np.zeros((4, 8, 8, 16))
    for side in range(2):
        place[..., 8 * side : 8 * side + ey + 1] = (
            INT[:, side][None, :, None, None] * low.reshape(ey, 8, ey + 1)[:, None]
        )
    place = place.reshape(256, 16)
    rest_z = np.zeros((128, 128))
    rest_z[:, : ez + 1] = unique_interp(ez)
    for at in (32, 64, 96):
        rest_z[:, at : at + ez + 1] = unique_interp(ez)
    prol_z = np.zeros((128, 128))
    prol_z[: ez + 1, :] = unique_interp(ez).T
    copy_z = np.zeros((128, 128))
    copy_z[: ez + 1, : 2 * ez] = unique_copies(ez).T
    copy_y = np.zeros((16, 16))
    for side in range(2):
        copy_y[8 * side : 8 * side + 8, 8 * side : 8 * side + ey + 1] = unique_copies(ey)
    own = np.zeros((32, 256))
    for side in range(2):
        own[8 * (side + 1) + 1 : 8 * (side + 1) + 2 + ey] = place.T[8 * side : 8 * side + ey + 1]
    rest_xy = split(own)
    spill = np.zeros((4, 8, 256))
    low_m = low * np.tile(TWICE, ey)[:, None]
    for side in range(2):
        for at, v in ((0, 1 + side), (64, 3 * side)):
            spill[v, 1 : ey + 2, at + 32 * side : at + 32 * side + 32] = low_m.T
        for at, r in ((128, 1 + ey * side), (144, (ey + 2) * side)):
            for vx in range(2):
                spill[1 + vx, r, at + 8 * side : at + 8 * side + 8] = HATS[vx]
    for at, (dx, dy) in enumerate(EDGE):
        near_v, far_v = (1, 0) if dx < 0 else (2, 3)
        near_r, far_r = (1, 0) if dy < 0 else (1 + ey, 2 + ey)
        spill[near_v, near_r, 160 + at] = 1.0
        spill[far_v, near_r, 168 + at] = 1.0
        spill[near_v, far_r, 176 + at] = 1.0
    spill = split(spill.reshape(32, 256))
    rest_z = np.zeros((128, 128))
    rest_z[:, : ez + 1] = unique_interp(ez)
    for at in (32, 64, 96):
        rest_z[:, at : at + ez + 1] = unique_interp(ez)
    prol_z = np.zeros((128, 128))
    prol_z[: ez + 1, :] = unique_interp(ez).T
    copy_z = np.zeros((128, 128))
    copy_z[: ez + 1, : 2 * ez] = unique_copies(ez).T
    copy_y = np.zeros((16, 16))
    for side in range(2):
        copy_y[8 * side : 8 * side + 8, 8 * side : 8 * side + ey + 1] = unique_copies(ey)
    own = np.zeros((32, 256))
    for side in range(2):
        own[8 * (side + 1) + 1 : 8 * (side + 1) + 2 + ey] = place.T[8 * side : 8 * side + ey + 1]
    rest_xy = split(own)
    spill = np.zeros((4, 8, 256))
    low_m = low * np.tile(TWICE, ey)[:, None]
    for side in range(2):
        for at, v in ((0, 1 + side), (64, 3 * side)):
            spill[v, 1 : ey + 2, at + 32 * side : at + 32 * side + 32] = low_m.T
        for at, r in ((128, 1 + ey * side), (144, (ey + 2) * side)):
            for vx in range(2):
                spill[1 + vx, r, at + 8 * side : at + 8 * side + 8] = HATS[vx]
    for at, (dx, dy) in enumerate(EDGE):
        near_v, far_v = (1, 0) if dx < 0 else (2, 3)
        near_r, far_r = (1, 0) if dy < 0 else (1 + ey, 2 + ey)
        spill[near_v, near_r, 160 + at] = 1.0
        spill[far_v, near_r, 168 + at] = 1.0
        spill[near_v, far_r, 176 + at] = 1.0
    spill = split(spill.reshape(32, 256))
    moment_y = np.zeros((2, 2, 8, 8, 8))
    for side in range(2):
        for at, one in enumerate(face_moments(7 * side)):
            moment_y[side, at] = np.eye(8)[:, :, None] * one[None, None, :]
    moment_y = moment_y.reshape(32, 64)
    late = {
        "grad_z": right_halves(np.kron(eye, DER.T)),
        "back_z": right_halves(np.kron(eye, DER)),
        "rest_z": right_halves(rest_z),
        "prol_z": right_halves(prol_z),
        "copy_z": wide(jnp.concatenate([split(copy_z)[0]] * 2)),
        "prol_xy": wide(left_halves(place)),
        "grad_xy": wide(
            jnp.concatenate([left_halves(np.kron(DER, eye8)), left_halves(np.kron(eye8, DER))])
        ),
        "back_y": wide(left_halves(np.kron(eye8, DER.T))),
        "rest_xy": jnp.concatenate([rest_xy[0], rest_xy[1]]),
        "spill": jnp.concatenate([spill[0], spill[1]]),
        "copy_y": wide(left_halves(copy_y)),
    }
    flat = {}
    for name, slope in (("moment_m", False), ("moment_s", True)):
        block = np.zeros((128, 128))
        for at, one in enumerate(moment_maps(ez, (0, 1, -1), slope)):
            block[:, 32 * at : 32 * at + ez + 1] = one.T
        flat[name] = jnp.asarray(block, F32)
    order_y = (-1, 0, 1)
    mass_y = np.zeros((3, 8, 8 * ey))
    mass_y[:, : ey + 1] = moment_maps(ey, order_y, False)
    slope_y = np.zeros((3, 8, 8 * ey))
    slope_y[:, : ey + 1] = moment_maps(ey, order_y, True)
    mass_y = mass_y.reshape(24, 8 * ey)
    slope_y = slope_y.reshape(24, 8 * ey)
    for name, sign in (("mix_plus", 0.25), ("mix_minus", -0.25)):
        block = np.zeros((24, 128))
        block[:, : 24 * ey] = np.concatenate([slope_y, mass_y, sign * mass_y], axis=1)
        flat[name] = jnp.asarray(block, F32)
    return spots_of(early), spots_of(late), spots_of(flat)


def kernel(
    tables_at, n_dom, n_sub, coef_hbm, rhs_hbm, early_hbm, late_hbm, flat_hbm,
    out_ref, coarse_ref,
    coef, rhs, early, late, flat, weighted, field, held, fmask, fmult, inverse, step,
    pmine, ptile, dtile, ctile, stencil, gfield, fside, frow, fedge,
    xs1, vs1, es1, xs2, vs2, es2,
    xr1, vr1, er1, xr2, vr2, er2, px, pt, dr, cr, fx, fy, fe,
    load_sem, s_sem, r_sem, ready,
):
    early_at, late_at, flat_at = tables_at
    dom = lax.axis_index("dom")
    sub = lax.axis_index("sub")

    loads = []
    for at, (source, dest) in enumerate(
        ((coef_hbm, coef), (early_hbm, early), (rhs_hbm, rhs), (flat_hbm, flat), (late_hbm, late))
    ):
        load = pltpu.make_async_copy(source, dest, load_sem.at[at])
        load.start()
        loads.append(load)

    def present(pair):
        dx, dy = pair
        conds = []
        if dx < 0:
            conds.append(dom >= -dx)
        if dx > 0:
            conds.append(dom < n_dom - dx)
        if dy < 0:
            conds.append(sub >= 1)
        if dy > 0:
            conds.append(sub < n_sub - 1)
        return functools.reduce(jnp.logical_and, conds)

    def target(pair):
        return (dom + pair[0], sub + pair[1])

    for buffer in (xr1, vr1, er1, xr2, vr2, er2, px, pt, dr, cr, fx, fy, fe):
        buffer[...] = jnp.zeros_like(buffer)

    barrier = pltpu.get_barrier_semaphore()
    for pair in sorted(NEAR, key=lambda p: -abs(p[0]) - abs(p[1])):

        @pl.when(present(pair))
        def _(pair=pair):
            pl.semaphore_signal(barrier, inc=1, device_id=target(pair), device_id_type=MESH)

    near_x = jnp.where(dom >= 1, 1, 0) + jnp.where(dom < n_dom - 1, 1, 0)
    near_y = jnp.where(sub >= 1, 1, 0) + jnp.where(sub < n_sub - 1, 1, 0)
    far_x = near_x + jnp.where(dom >= 2, 1, 0) + jnp.where(dom < n_dom - 2, 1, 0)
    n_side = near_x
    n_rims = near_y * (1 + near_x)
    n_wide = (1 + far_x) * (1 + near_y) - 1
    reach_x = far_x + jnp.where(dom >= 3, 1, 0) + jnp.where(dom < n_dom - 3, 1, 0)
    n_reach = (1 + reach_x) * (1 + near_y) - 1

    row = lax.broadcasted_iota(jnp.int32, (256, 128), 0)
    lane = lax.broadcasted_iota(jnp.int32, (256, 128), 1)
    x_at = lax.shift_right_logical(row, 3) & 7
    b_at = row & 7
    c_at = lane & 7
    place_x = dom * 8 + x_at
    place_y = sub * 32 + lax.shift_right_logical(row, 6) * 8 + b_at
    inside = (
        (place_x > 0) & (place_x < 8 * n_dom - 1)
        & (place_y > 0) & (place_y < 32 * n_sub - 1)
        & (lane > 0) & (lane < 127)
    )
    mask = jnp.where(inside, 1.0, 0.0)
    fmask[...] = mask
    twice = jnp.where((x_at == 0) | (x_at == 7), 2.0, 1.0)
    twice = twice * jnp.where((b_at == 0) | (b_at == 7), 2.0, 1.0)
    fmult[...] = mask * twice * jnp.where((c_at == 0) | (c_at == 7), 2.0, 1.0)

    lane8 = lax.broadcasted_iota(jnp.int32, (8, 128), 1)
    sub8 = lax.broadcasted_iota(jnp.int32, (8, 128), 0)
    z_low = ((lane8 & 7) == 0) & (lane8 > 0)
    z_high = ((lane8 & 7) == 7) & (lane8 < 127)

    def weights_along(spot):
        value = jnp.where((spot == 0) | (spot == 7), float(WTS[0]), float(WTS[1]))
        value = jnp.where((spot == 2) | (spot == 5), float(WTS[2]), value)
        return jnp.where((spot == 3) | (spot == 4), float(WTS[3]), value)

    def fold(v):
        v = v.reshape(32, 8, 128)
        v = v + jnp.where(
            z_high[None], pltpu.roll(v, 127, 2),
            jnp.where(z_low[None], pltpu.roll(v, 1, 2), 0.0),
        )
        up = pltpu.roll(v, 1, 1)
        down = pltpu.roll(v, 7, 1)
        none = jnp.zeros((8, 8, 128), F32)
        up = jnp.concatenate([none, up[:24]], axis=0)
        down = jnp.concatenate([down[8:], none], axis=0)
        v = v + jnp.where((sub8 == 0)[None], up, jnp.where((sub8 == 7)[None], down, 0.0))
        return v.reshape(256, 128)

    def halves(v):
        high = v.astype(BF16)
        return high, (v - high.astype(F32)).astype(BF16)

    def dot(left, right):
        return jnp.dot(left, right, preferred_element_type=F32)

    def early_part(name):
        start, count = early_at[name]
        return early[start : start + count, :]

    def late_part(name):
        start, count = late_at[name]
        return late[start : start + count, :]

    def flat_part(name):
        start, count = flat_at[name]
        return flat[start : start + count, :]

    def times_right(pair, matrix):
        both = dot(jnp.concatenate(pair, axis=1), matrix)
        return both[:, :128] + both[:, 128:]

    def stacked(pair):
        high, low = [
            jnp.concatenate([v[at : at + 64] for at in range(0, v.shape[0], 64)], axis=1) for v in pair
        ]
        return jnp.concatenate([high, high, low], axis=0)

    def rows_of(v):
        return jnp.concatenate([v[:, at : at + 128] for at in range(0, v.shape[1], 128)], axis=0)

    def back_x(v):
        v = v.reshape(4, 8, 8, 128)
        matrix = DER.T
        even = [v[:, b] + v[:, 7 - b] for b in range(4)]
        odd = [v[:, b] - v[:, 7 - b] for b in range(4)]
        planes = [None] * 8
        for a in range(4):
            p = sum(float(matrix[a, b] + matrix[a, 7 - b]) / 2 * even[b] for b in range(4))
            q = sum(float(matrix[a, b] - matrix[a, 7 - b]) / 2 * odd[b] for b in range(4))
            planes[a] = p + q
            planes[7 - a] = q - p
        return jnp.stack(planes, axis=1).reshape(256, 128)

    def with_faces(u, faces, w_rows, w_z):
        w = weighted[...]
        pair = halves(jnp.concatenate([u, faces], axis=0))
        both = dot(late_part("grad_xy")[:, 0:192], stacked(pair))
        all_z = times_right(pair, late_part("grad_z"))
        all_y = rows_of(both[64:128])
        flux_z = halves(jnp.concatenate([w * all_z[0:256], w_z * all_z[256:384]], axis=0))
        flux_y = halves(jnp.concatenate([w * all_y[0:256], w_rows * all_y[256:384]], axis=0))
        back = rows_of(dot(late_part("back_y")[:, 0:192], stacked(flux_y)))
        back = back + times_right(flux_z, late_part("back_z"))
        return back[0:256] + back_x(w * rows_of(both[0:64, 0:512])), back[256:384]

    def local_operator(u):
        w = weighted[...]
        pair = halves(u)
        both = dot(late_part("grad_xy")[:, 0:192], stacked(pair))
        flux_z = halves(w * times_right(pair, late_part("grad_z")))
        flux_y = halves(w * rows_of(both[64:128]))
        back = rows_of(dot(late_part("back_y")[:, 0:192], stacked(flux_y)))
        back = back + times_right(flux_z, late_part("back_z"))
        return back + back_x(w * rows_of(both[0:64]))

    def send(table, pair, source, landing, group):
        at = table.index((-pair[0], -pair[1]))

        @pl.when(present(pair))
        def _():
            pltpu.make_async_remote_copy(
                src_ref=source,
                dst_ref=landing.at[at],
                send_sem=s_sem.at[group],
                recv_sem=r_sem.at[group],
                device_id=target(pair),
                device_id_type=MESH,
            ).start()

    counts = {"side": (n_side, (1, 2)), "rows": (near_y, (1, 2)), "edge": (near_x * near_y, (1, 2, 4)), "rims": (n_rims, (1, 2, 3, 4, 6)), "wide": (n_wide, (1, 2, 3, 5, 7, 8, 9, 11, 14)), "reach": (n_reach, (7, 9, 11, 13, 14, 17, 20))}

    def settle(kind, landing, group, sent):
        count, options = counts[kind]
        for one in options:

            @pl.when(count == one)
            def _(one=one):
                copy = pltpu.make_async_remote_copy(
                    src_ref=landing.at[pl.ds(0, one)],
                    dst_ref=landing.at[pl.ds(0, one)],
                    send_sem=s_sem.at[group],
                    recv_sem=r_sem.at[group],
                    device_id=(dom, sub),
                    device_id_type=MESH,
                )
                if sent:
                    copy.wait_send()
                else:
                    copy.wait_recv()

    def pack(refs, fields, xs, vs, es):
        for f in range(fields):
            ref = refs.at[f]
            faces = {-1: ref[pl.ds(0, 8, stride=8), :], 1: ref[pl.ds(199, 8, stride=8), :]}
            for j in range(4):
                xs[0, f, 8 * j : 8 * j + 8] = ref[64 * j : 64 * j + 8, :]
                xs[1, f, 8 * j : 8 * j + 8] = ref[64 * j + 56 : 64 * j + 64, :]
            for at, (_, dy) in enumerate(ROWS):
                vs[at, f] = faces[dy]
            for at, (dx, dy) in enumerate(EDGE):
                line = 0 if dx < 0 else 7
                es[at, f] = faces[dy][line : line + 1]

    def exchange(xs, vs, es, xr, vr, er, group, edge_group):
        for pair in EDGE:
            send(EDGE, pair, es.at[EDGE.index(pair)], er, edge_group)
        for pair in SIDE:
            send(SIDE, pair, xs.at[SIDE.index(pair)], xr, group)
        for pair in ROWS:
            send(ROWS, pair, vs.at[ROWS.index(pair)], vr, group + 1)

    def unpack(refs, fields, xr, vr, er):
        for f in range(fields):
            ref = refs.at[f]
            for j in range(4):
                ref[64 * j : 64 * j + 8, :] += xr[0, f, 8 * j : 8 * j + 8]
                ref[64 * j + 56 : 64 * j + 64, :] += xr[1, f, 8 * j : 8 * j + 8]
            for dy, start in ((-1, 0), (1, 199)):
                extra = vr[ROWS.index((0, dy)), f]
                low = er[EDGE.index((-1, dy)), f]
                high = er[EDGE.index((1, dy)), f]
                extra = extra + jnp.where(sub8 == 0, low, jnp.where(sub8 == 7, high, 0.0))
                ref[pl.ds(start, 8, stride=8), :] += extra

    def in_order(ref):
        v = ref[...].reshape(8, 4, 8, 128)
        return jnp.concatenate([v[:, j] for j in range(4)], axis=0).reshape(256, 128)

    table = weights_along(x_at) * weights_along(b_at) * weights_along(c_at)
    loads[0].wait()
    w = in_order(coef) * table
    weighted[...] = w
    loads[1].wait()
    loads[2].wait()
    field[0] = fold(in_order(rhs))
    w4 = w.reshape(4, 8, 8, 128)
    planes = [w4[:, a].reshape(32, 128) for a in range(8)]
    for side in range(2):
        one, two = face_moments(7 * side)
        rows = [weighted[pl.ds(192 * side + b, 8, stride=8), :] for b in range(8)]
        fside[side, 0:32] = sum(float(one[a]) * planes[a] for a in range(8))
        fside[side, 32:64] = sum(float(two[a]) * planes[a] for a in range(8))
        fside[side, 64:96] = planes[7 * side]
        frow[side, 0] = sum(float(one[b]) * rows[b] for b in range(8))
        frow[side, 1] = sum(float(two[b]) * rows[b] for b in range(8))
        frow[side, 2] = rows[7 * side]
    fedge[...] = jnp.zeros_like(fedge)
    for at, (dx, dy) in enumerate(EDGE):
        x_side, y_side = (dx + 1) // 2, (dy + 1) // 2
        spot, line = 31 * y_side, 7 * x_side
        fedge[at, 0:1] = 2.0 * (fside[x_side, spot : spot + 1] + frow[y_side, 0, line : line + 1])
        fedge[at, 1:2] = 2.0 * fside[x_side, 32 + spot : 33 + spot]
        fedge[at, 2:3] = 2.0 * frow[y_side, 1, line : line + 1]
        fedge[at, 3:4] = 4.0 * frow[y_side, 2, line : line + 1]
    pair = halves(w)
    diagonal = rows_of(dot(early_part("square_xy")[:, 0:192], stacked(pair)))
    field[1] = fold(diagonal + times_right(pair, early_part("square_z")))
    pack(field, 2, xs1, vs1, es1)

    pl.semaphore_wait(barrier, (1 + near_x) * (1 + near_y) - 1)
    exchange(xs1, vs1, es1, xr1, vr1, er1, 0, 11)

    def announce(stage):
        for pair in SIDE:

            @pl.when(present(pair))
            def _(pair=pair):
                pl.semaphore_signal(
                    ready.at[stage], inc=1, device_id=target(pair), device_id_type=MESH
                )

    for at, pair in enumerate(SIDE):
        send(SIDE, pair, fside.at[at], fx, 2)
    for at, pair in enumerate(ROWS):
        send(ROWS, pair, frow.at[at], fy, 3)
    for at, pair in enumerate(EDGE):
        send(EDGE, pair, fedge.at[at], fe, 4)
    announce(0)

    loads[3].wait()
    w4 = weighted[...].reshape(4, 8, 8, 128)
    planes = [w4[:, a].reshape(32, 128) for a in range(8)]
    moments = [sum(float(m[a]) * planes[a] for a in range(8) if m[a] != 0.0) for m in MASS]
    moments.append(moments[0] + 2.0 * moments[1] + moments[2])
    stack = jnp.concatenate(moments, axis=0)
    mass_z = jnp.dot(stack, flat_part("moment_m"), precision=HIGHEST, preferred_element_type=F32)
    slope_z = jnp.dot(stack, flat_part("moment_s"), precision=HIGHEST, preferred_element_type=F32)
    none = jnp.zeros((32, 128), F32)
    mine = []
    for at in range(3):
        part = slice(32 * at, 32 * at + 32)
        parts = jnp.concatenate([mass_z[part], slope_z[part], mass_z[96:128], none], axis=0)
        mix = flat_part("mix_minus" if at == 1 else "mix_plus")
        one = jnp.dot(mix, parts, precision=HIGHEST, preferred_element_type=F32)
        pmine[at] = one
        mine.append(one.reshape(3, 8, 128))
    dtile[...] = jnp.where(lane8 < 32, mine[0][1], pltpu.roll(mine[2][1], 32, 1))
    for side, vertex, first in ((0, 0, 1), (1, 4, 0)):
        total = jnp.zeros((8, 128), F32)
        for c in range(3):
            for d in range(2):
                goal = 2 * c + d
                moved = pltpu.roll(mine[c][first + d], (goal - vertex) % 8, 0)
                total = jnp.where(sub8 == goal, moved, total)
        ptile[side] = total
    send(SIDE, (-1, 0), pmine.at[pl.ds(0, 2)], px, 5)
    send(SIDE, (1, 0), pmine.at[pl.ds(1, 2)], px, 5)
    for pair in RIMS:
        send(RIMS, pair, ptile.at[(pair[1] + 1) // 2], pt, 6)
    pl.semaphore_wait(ready.at[0], near_x)
    announce(1)
    for pair in WIDE:
        send(WIDE, pair, dtile, dr, 7)
    loads[4].wait()

    settle("side", xr1, 0, False)
    settle("rows", vr1, 1, False)
    settle("edge", er1, 11, False)
    unpack(field, 2, xr1, vr1, er1)

    residual = fmask[...] * field[0]
    inv = fmask[...] / field[1]
    inverse[...] = inv
    field[0] = residual
    theta = 1.1
    delta = 0.9
    sigma = theta / delta
    rho0 = 1.0 / sigma
    rho1 = 1.0 / (2.0 * sigma - rho0)
    step_one = inv * residual / theta
    step[...] = step_one
    held[0] = fold(local_operator(step_one))
    pack(held, 1, xs2, vs2, es2)
    exchange(xs2, vs2, es2, xr2, vr2, er2, 8, 12)

    factor = 2.0 * rho1 / delta
    g = factor * inverse[...] * held[0]
    gfield[...] = g
    start = (1.0 + rho1 * rho0) * step_one + factor * inv * residual
    step[...] = start
    settle("side", fx, 2, False)
    settle("rows", fy, 3, False)
    settle("edge", fe, 4, False)
    faces = []
    for first in (0, 56):
        for j in range(4):
            faces.append(g[64 * j + first : 64 * j + first + 8])
    rims = [gfield[pl.ds(0, 8, stride=8), :], gfield[pl.ds(199, 8, stride=8), :]]
    corner = jnp.zeros((8, 128), F32)
    lines = [jnp.zeros((8, 128), F32) for _ in range(4)]
    for at, (dx, dy) in enumerate(EDGE):
        line = 0 if dx < 0 else 7
        moved = pltpu.roll(rims[(dy + 1) // 2], (at - line) % 8, 0)
        corner = jnp.where(sub8 == at, moved, corner)
        given = fe[at]
        for k in range(4):
            lines[k] = jnp.where(sub8 == at, pltpu.roll(given, (at - k) % 8, 0), lines[k])
    none40 = jnp.zeros((40, 128), F32)
    faces = jnp.concatenate(faces + rims + [corner, none40], axis=0)
    two = [2.0 * fx[0, 64:96], 2.0 * fx[1, 64:96], 2.0 * fy[0, 2], 2.0 * fy[1, 2]]
    w_rows = jnp.concatenate(two + [jnp.zeros((48, 128), F32)], axis=0)
    w_z = jnp.concatenate(two + [lines[3], none40], axis=0)
    image, face_image = with_faces(start - g, faces, w_rows, w_z)
    defect = residual - fmult[...] * image
    near_w = [fx[0, 0:32], fx[1, 0:32], fy[0, 0], fy[1, 0], lines[0]]
    far_w = [fx[0, 32:64], fx[1, 32:64], fy[0, 1], fy[1, 1]]
    near = jnp.concatenate(near_w, axis=0) * faces[0:88] + face_image[0:88]
    far = jnp.concatenate(far_w, axis=0) * faces[0:80]
    parts = [
        near[0:64], far[0:64], near[64:80], far[64:80], near[80:88],
        lines[1] * corner, lines[2] * corner, jnp.zeros((72, 128), F32),
    ]
    twice_z = jnp.where(((lane8 & 7) == 0) | ((lane8 & 7) == 7), 2.0, 1.0)
    parts = jnp.concatenate(parts, axis=0).reshape(32, 8, 128) * twice_z[None]
    part = dot(late_part("rest_xy"), jnp.concatenate(halves(defect), axis=1))
    part = part + dot(late_part("spill"), jnp.concatenate(halves(parts.reshape(256, 128)), axis=1))
    part = part[0:32, :128] + part[0:32, 128:] + part[32:64, :128]
    coarse = times_right(halves(part), late_part("rest_z"))
    tile = jnp.where(lane8 < 64, jnp.where(lane8 < 32, coarse[0:8], coarse[8:16]), jnp.where(lane8 < 96, coarse[16:24], coarse[24:32]))
    ctile[...] = tile
    pl.semaphore_wait(ready.at[1], near_x)
    for pair in sorted(REACH, key=lambda p: -abs(p[0]) - abs(p[1])):
        send(REACH, pair, ctile, cr, 10)

    settle("side", px, 5, False)
    settle("rims", pt, 6, False)
    settle("wide", dr, 7, False)
    row_low = sub8 < 2
    row_mid = sub8 == 2

    def extend(own, received):
        moved = []
        for dx in (-2, -1, 0, 1, 2):
            mid = own if dx == 0 else received[WIDE.index((dx, 0))]
            below = received[WIDE.index((dx, -1))]
            above = received[WIDE.index((dx, 1))]
            rim = jnp.where(row_low, above, jnp.where(row_mid, 0.0, below))
            moved.append(pltpu.roll(mid, 1, 0) + pltpu.roll(rim, 5, 0))
        return [moved[v + 1] + pltpu.roll(moved[v], 96, 1) for v in range(4)]

    ext_diag = extend(dtile[...], dr)
    vertex_y = sub * 4 + sub8 - 1
    good_yz = (vertex_y > 0) & (vertex_y < 4 * n_sub) & (sub8 < 7) & (lane8 > 0) & (lane8 < 16)
    scales = []
    for v in range(4):
        vertex_x = dom + v - 1
        good = good_yz & (vertex_x > 0) & (vertex_x < n_dom)
        scales.append(jnp.where(good, (2.0 / 3.0) / jnp.where(good, ext_diag[v], 1.0), 0.0))

    def joined(dx, c):
        if dx == 0:
            base = pmine[c]
        else:
            base = px[SIDE.index((dx, 0)), c if dx > 0 else c - 1]
        base = base.reshape(3, 8, 128)
        below = pt[RIMS.index((dx, -1))]
        above = pt[RIMS.index((dx, 1))]
        out = []
        for d in range(3):
            total = base[d]
            if d < 2:
                moved = pltpu.roll(below, (-2 * c - d) % 8, 0)
                total = total + jnp.where(sub8 == 0, moved, 0.0)
            if d > 0:
                moved = pltpu.roll(above, (4 - 2 * c - (d - 1)) % 8, 0)
                total = total + jnp.where(sub8 == 4, moved, 0.0)
            out.append(total)
        return out

    cross = joined(0, 1)
    own_low = [a + b for a, b in zip(joined(0, 0), joined(-1, 2), strict=True)]
    own_high = [a + b for a, b in zip(joined(0, 2), joined(1, 0), strict=True)]
    for vx, blocks in enumerate(
        ((joined(-1, 1), own_low, cross), (cross, own_high, joined(1, 1)))
    ):
        for at in range(3):
            for d in range(3):
                stencil[vx * 9 + at * 3 + d] = blocks[at][d]
    for v in range(4):
        stencil[18 + v] = scales[v]

    settle("side", xr2, 8, False)
    settle("rows", vr2, 9, False)
    settle("edge", er2, 12, False)
    unpack(held, 1, xr2, vr2, er2)
    step[...] = step[...] - factor * inverse[...] * held[0]

    settle("side", xr1, 0, True)
    settle("rows", vr1, 1, True)
    settle("edge", er1, 11, True)
    settle("side", fx, 2, True)
    settle("rows", fy, 3, True)
    settle("edge", fe, 4, True)
    settle("side", px, 5, True)
    settle("rims", pt, 6, True)
    settle("wide", dr, 7, True)
    settle("side", xr2, 8, True)
    settle("rows", vr2, 9, True)
    settle("edge", er2, 12, True)
    settle("reach", cr, 10, False)

    moved = {}
    mid_rows = (sub8 > 3) & (sub8 < 7)
    for dx in range(-3, 4):
        mid = ctile[...] if dx == 0 else cr[REACH.index((dx, 0))]
        below = cr[REACH.index((dx, -1))]
        above = cr[REACH.index((dx, 1))]
        rim = jnp.where(sub8 < 3, above, jnp.where(mid_rows, below, 0.0))
        moved[dx] = mid + pltpu.roll(rim, 4, 0)
    whole = moved[0] + pltpu.roll(jnp.where(lane8 < 96, moved[1], moved[-3]), 32, 1)
    whole = whole + pltpu.roll(jnp.where(lane8 < 64, moved[2], moved[-2]), 64, 1)
    whole = whole + pltpu.roll(jnp.where(lane8 >= 32, moved[-1], moved[3]), 96, 1)
    ext_rhs = [whole] + [pltpu.roll(whole, 128 - 32 * v, 1) for v in (1, 2, 3)]
    scales = [stencil[18 + v] for v in range(4)]
    ones = [scales[v] * ext_rhs[v] for v in range(4)]
    packed = [c + pltpu.roll(c, 31, 1) + pltpu.roll(c, 65, 1) for c in ones]
    around = [[c, pltpu.roll(c, 7, 0), pltpu.roll(c, 6, 0)] for c in packed]
    results = []
    for vx in range(2):
        total = jnp.zeros((8, 128), F32)
        for at in range(3):
            for d in range(3):
                total = total + stencil[vx * 9 + at * 3 + d] * around[vx + at][d]
        image = total + pltpu.roll(total, 96, 1) + pltpu.roll(total, 64, 1)
        one = pltpu.roll(ones[vx + 1], 7, 0)
        scale = pltpu.roll(scales[vx + 1], 7, 0)
        right = pltpu.roll(ext_rhs[vx + 1], 7, 0)
        results.append(one + scale * (right - image))
    pair = halves(jnp.concatenate(results, axis=0))
    nodes = halves(times_right(pair, late_part("prol_z")))
    nodes = jnp.concatenate([nodes[0], nodes[0], nodes[1]], axis=0)
    fine = step[...] + fmask[...] * dot(late_part("prol_xy")[:, 0:48], nodes)
    fine = fine.reshape(4, 8, 8, 128)
    for j in range(4):
        out_ref[:, 8 * j : 8 * j + 8, :] = fine[j]
    copies = halves(dot(jnp.concatenate(pair, axis=1), late_part("copy_z")[:, 0:128]))
    copies = jnp.concatenate([copies[0], copies[0], copies[1]], axis=0)
    copies = dot(late_part("copy_y")[:, 0:48], copies)
    coarse_ref[...] = copies.reshape(2, 8, 128)[:, :, 0:32]

    settle("reach", cr, 10, True)


def finish(fine, coarse, fine_out, coarse_out, sem):
    one = pltpu.make_async_copy(fine, fine_out, sem.at[0])
    two = pltpu.make_async_copy(coarse, coarse_out, sem.at[1])
    one.start()
    two.start()
    one.wait()
    two.wait()


def solution(mesh):
    n_dom = mesh.shape["dom"]
    n_sub = mesh.shape["sub"]

    def shards(rhs_local, coefficient):
        (early_at, early), (late_at, late), (flat_at, flat) = constants(4, 16)
        any_space = pl.BlockSpec(memory_space=pl.ANY)
        vmem = pl.BlockSpec(memory_space=pltpu.VMEM)
        outs = (
            jax.ShapeDtypeStruct((8, 32, 128), F32),
            jax.ShapeDtypeStruct((2, 8, 32), F32),
        )

        def space(*shape):
            return pltpu.VMEM(shape, F32)

        dma = pltpu.SemaphoreType.DMA
        operands = [
            pltpu.with_memory_space_constraint(v, pltpu.HBM)
            for v in (coefficient, rhs_local, early, late, flat)
        ]
        fine, coarse = pl.pallas_call(
            functools.partial(kernel, (early_at, late_at, flat_at), n_dom, n_sub),
            out_shape=outs,
            in_specs=[any_space] * 5,
            out_specs=(vmem, vmem),
            scratch_shapes=[
                space(8, 32, 128),
                space(8, 32, 128),
                pltpu.VMEM(early.shape, BF16),
                pltpu.VMEM(late.shape, BF16),
                pltpu.VMEM(flat.shape, F32),
                space(256, 128),
                space(2, 256, 128),
                space(1, 256, 128),
                space(256, 128),
                space(256, 128),
                space(256, 128),
                space(256, 128),
                space(3, 24, 128),
                space(2, 8, 128),
                space(8, 128),
                space(8, 128),
                space(22, 8, 128),
                space(256, 128),
                space(2, 96, 128),
                space(2, 3, 8, 128),
                space(4, 8, 128),
                space(2, 2, 32, 128),
                space(2, 2, 8, 128),
                space(4, 2, 1, 128),
                space(2, 1, 32, 128),
                space(2, 1, 8, 128),
                space(4, 1, 1, 128),
                space(2, 2, 32, 128),
                space(2, 2, 8, 128),
                space(4, 2, 1, 128),
                space(2, 1, 32, 128),
                space(2, 1, 8, 128),
                space(4, 1, 1, 128),
                space(2, 2, 24, 128),
                space(6, 8, 128),
                space(14, 8, 128),
                space(20, 8, 128),
                space(2, 96, 128),
                space(2, 3, 8, 128),
                space(4, 8, 128),
                dma((5,)),
                dma((13,)),
                dma((13,)),
                pltpu.SemaphoreType.REGULAR((2,)),
            ],
            compiler_params=pltpu.CompilerParams(
                collective_id=0, has_side_effects=True, vmem_limit_bytes=8 * 2**20
            ),
        )(*operands)
        return pl.pallas_call(
            finish,
            out_shape=outs,
            in_specs=[vmem, vmem],
            out_specs=(any_space, any_space),
            scratch_shapes=[dma((2,))],
            compiler_params=pltpu.CompilerParams(vmem_limit_bytes=2**20),
        )(fine, coarse)

    return jax.shard_map(
        shards,
        mesh=mesh,
        in_specs=(P("dom", "sub", None), P("dom", "sub", None)),
        out_specs=(P("dom", "sub", None), P("dom", "sub", None)),
        check_vma=False,
    )
```
